32 devices in a mesh: dp: 32 (over z, y, x, core).
Axes of the slice: x: 2, y: 2, z: 4, core: 2. Of those that a mesh axis runs over, the one named last changes fastest.
Arguments:
- hidden: float32 [16384, 1536], P('dp'), may hold values from -6 to 6
- cotangent: float32 [16384, 1536], P('dp'), may hold values from -6 to 6
- block_ids: int32 [64, 256], P('dp'), may hold values from 0 to 3, never falling along the last dimension, each value on 1 to 128 neighbouring positions
- routes: int32 [16384, 8], P('dp'), may hold values from 0 to 31, all different within a row
- pair_rank: int32 [64, 2048], P('dp'), may hold values from 0 to 2047, each once within a row
- norm1_gain: bfloat16 [1536], P('dp'), may hold values from 0.5 to 1.5
- norm2_gain: bfloat16 [1536], P('dp'), may hold values from 0.5 to 1.5
- w_query: bfloat16 [1536, 1536], P('dp'), may hold values from -0.625 to 0.625
- w_key: bfloat16 [1536, 512], P('dp'), may hold values from -0.625 to 0.625
- w_value: bfloat16 [1536, 512], P('dp'), may hold values from -0.625 to 0.625
- w_out: bfloat16 [1536, 1536], P('dp'), may hold values from -0.875 to 0.875
- w_router: bfloat16 [1536, 32], P('dp'), may hold values from -0.078125 to 0.078125
- w_gate: bfloat16 [32, 1536, 512], P('dp'), may hold values from -0.15625 to 0.15625
- w_up: bfloat16 [32, 1536, 512], P('dp'), may hold values from -0.625 to 0.625
- w_down: bfloat16 [32, 512, 1536], P('dp'), may hold values from -1.5 to 1.5
Outputs:
- output: float32 [16384, 1536], P('dp')
- grad_hidden: float32 [16384, 1536], P('dp')
- grad_norm1: float32 [1536], P('dp')
- grad_norm2: float32 [1536], P('dp')
- grad_query: float32 [1536, 1536], P('dp')
- grad_key: float32 [1536, 512], P('dp')
- grad_value: float32 [1536, 512], P('dp')
- grad_out: float32 [1536, 1536], P('dp')
- grad_router: float32 [1536, 32], P('dp')
- grad_gate: float32 [32, 1536, 512], P('dp')
- grad_up: float32 [32, 1536, 512], P('dp')
- grad_down: float32 [32, 512, 1536], P('dp')
The draws below stay inside these ranges and needn't reach their ends.
Inputs may be any that keep to these rules, and one draw needn't show every extreme that they name: `block_ids`: within a sequence block numbers never fall; each block holds 1 to 128 tokens, one exactly 128. `routes`: each token names 8 different experts. `pair_rank`: each row is a permutation; pair t * 8 + k is the k-th route of the row's t-th token.
All inputs are finite; a program needn't handle non-finite values.
Results may differ from the reference program's by a relative error of at most 0.017.
The reference program's roundings to bfloat16 on the way count: a program that leaves them out, or rounds other values in their place, can miss the bound.
Values may be sent and summed in bfloat16 or wider, within the bound.
No kernel may reach another device: no remote copies, remote signals or barrier semaphores. Data moves between devices by JAX's collectives and lax.ppermute only.
A program may use at most 320 MiB of HBM per device.

```python
import math
import jax
import jax.numpy as jnp
import numpy as np
from jax import lax

D = 1536
H = 24
KVH = 8
HD = 64
FF = 512
TOP = 8
SEQ = 256
BLOCKS = 4
BLOCK = 128
MICRO = 2
EXPERTS = 32
CAP = 72
SEQS = 64
TOKENS = 16384
N_DP = 32


def steps_of(key, extent, pieces, low, top_value):
    gain, own = 1.0, jax.random.fold_in(key, 6)
    for axis_at, shards_of in pieces:
        draws = jnp.exp(jax.random.uniform(jax.random.fold_in(own, axis_at), (shards_of,), jnp.float32, low / len(pieces), top_value / len(pieces)))
        gain = gain * jnp.repeat(draws, extent[axis_at] // shards_of).reshape([-1 if axis == axis_at else 1 for axis in range(len(extent))])
    return gain


def picks_of(rng, rows, count, top, lift):
    ranking = jax.random.permutation(jax.random.fold_in(rng, 1), count)
    boost = ranking
    for power in range(3):
        boost = boost * boost // count
    boost = boost * lift // count
    lots = jax.random.randint(jax.random.fold_in(rng, 2), (rows, count), 0, 4096) + boost
    holders = jax.random.permutation(jax.random.fold_in(rng, 3), rows)[jnp.arange(count) % rows]
    lots = jnp.where(jnp.arange(rows)[:, None] == holders[None, :], 1 << 14, lots)
    score = lots * count + jnp.arange(count)
    return lax.top_k(score.astype(jnp.int32), top)[1].astype(jnp.int32)


def length_profile(number_of, total, bound, slope):
    loads = [(1 << 20) // math.isqrt(rank ** slope) + 1 for rank in range(2, number_of + 1)]
    rest, holding = total - bound - (number_of - 1), [1] * (number_of - 1)
    while rest > 0:
        candidates = [i for i in range(number_of - 1) if holding[i] < bound]
        mass, remaining = sum([loads[i] for i in candidates]), rest
        for i in candidates:
            extra = min(bound - holding[i], max(1, remaining * loads[i] // mass), rest)
            holding[i] = holding[i] + extra
            rest = rest - extra
    return np.array([bound] + holding)


def uneven_parts(rng, number_of, total, limit, slope):
    if number_of == 2:
        one = jax.random.randint(rng, (), max(1, total - limit), min(limit, total - 1) + 1)
        return jnp.stack([one, total - one])
    sizes = jnp.asarray(length_profile(number_of, total, limit, slope), jnp.int32)
    pairs = (number_of - 1) // 2
    source_of, receiver = sizes[1:1 + 2 * pairs:2], sizes[2:2 + 2 * pairs:2]
    slack = jnp.minimum(source_of - 1, limit - receiver)
    passed = jax.random.randint(jax.random.fold_in(rng, 1), (pairs,), 0, 1 << 20) % (slack + 1)
    sizes = sizes.at[1:1 + 2 * pairs:2].set(source_of - passed).at[2:2 + 2 * pairs:2].set(receiver + passed)
    return sizes[jax.random.permutation(jax.random.fold_in(rng, 2), number_of)]


def noise(key, dims, scale, bound, split=(), held_as=jnp.bfloat16):
    drawn = jax.random.normal(key, dims, jnp.float32) * scale
    if len(split) > 0:
        drawn = steps_of(key, dims, split, -0.22, 0.18) * drawn
    return jnp.clip(drawn, min=-bound, max=bound).astype(held_as)


def setup_inputs(seed: int = 0) -> dict:
    keys = jax.random.split(jax.random.key(seed), 16)
    return {
        "hidden": noise(keys[0], (TOKENS, D), 1.0, 6.0, ((0, 32),), jnp.float32),
        "cotangent": noise(keys[1], (TOKENS, D), 1.0, 6.0, ((0, 32),), jnp.float32),
        "block_ids": jax.vmap(lambda own: jnp.searchsorted(jnp.cumsum(uneven_parts(own, BLOCKS, SEQ, BLOCK, 0)), jnp.arange(SEQ), side="right"))(jax.random.split(keys[2], SEQS)).reshape((SEQS, SEQ)).astype(jnp.int32),
        "routes": picks_of(keys[3], TOKENS, EXPERTS, TOP, 2048),
        "pair_rank": jax.vmap(lambda own: jax.random.permutation(own, SEQ * TOP))(jax.random.split(keys[4], SEQS)).reshape((SEQS, SEQ * TOP)).astype(jnp.int32),
        "norm1_gain": jnp.clip(1.0 + 0.1 * jax.random.normal(keys[5], (D,), jnp.float32), 0.5, 1.5).astype(jnp.bfloat16),
        "norm2_gain": jnp.clip(1.0 + 0.1 * jax.random.normal(keys[6], (D,), jnp.float32), 0.5, 1.5).astype(jnp.bfloat16),
        "w_query": noise(keys[7], (D, H * HD), (D // 16) ** -0.5, 0.625, ((0, 32),)),
        "w_key": noise(keys[8], (D, KVH * HD), (D // 16) ** -0.5, 0.625, ((0, 32),)),
        "w_value": noise(keys[9], (D, KVH * HD), (D // 16) ** -0.5, 0.625, ((0, 32),)),
        "w_out": noise(keys[10], (H * HD, D), (H * HD // 32) ** -0.5, 0.875, ((0, 32),)),
        "w_router": noise(keys[11], (D, EXPERTS), (4 * D) ** -0.5, 0.078125, ((0, 32),)),
        "w_gate": noise(keys[12], (EXPERTS, D, FF), D ** -0.5, 0.15625, ((0, 32),)),
        "w_up": noise(keys[13], (EXPERTS, D, FF), (D // 16) ** -0.5, 0.625, ((0, 32),)),
        "w_down": noise(keys[14], (EXPERTS, FF, D), (FF // 32) ** -0.5, 1.5, ((0, 32),)),
    }


res_scale = 0.22
attn_scale = 0.015625
norm_eps = 1e-06
rope_base = 10000.0
highest = lax.Precision.HIGHEST

@jax.custom_vjp
def low(v):
    return lax.optimization_barrier(v.astype(jnp.bfloat16)).astype(jnp.float32)

@jax.custom_vjp
def low_back(v):
    return v

def low_keep(v):
    return (low(v), None)

def low_pass(kept, grad):
    return (grad,)

def back_keep(v):
    return (v, None)

def back_low(kept, grad):
    return (low(grad),)
low.defvjp(low_keep, low_pass)
low_back.defvjp(back_keep, back_low)

def rotary_tables(length, head_size):
    half_size = head_size // 2
    frequency = rope_base ** (-(jnp.arange(half_size, dtype=jnp.float32) * 2.0) / head_size)
    angles = jnp.arange(length, dtype=jnp.float32)[:, None] * frequency[None, :]
    return (jnp.cos(angles)[:, None, :], jnp.sin(angles)[:, None, :])

def rotate(operand, cos_table, sin_table):
    half_size = operand.shape[-1] // 2
    lower_half = operand[..., :half_size]
    upper_half = operand[..., half_size:]
    return jnp.concatenate([lower_half * cos_table - upper_half * sin_table, upper_half * cos_table + lower_half * sin_table], axis=-1)

def slot_table(route_rows, rank_row, experts, capacity):
    flat_routes = route_rows.reshape(-1).astype(jnp.int32)
    pair_count = flat_routes.shape[0]
    served_order = jnp.argsort(rank_row).astype(jnp.int32)
    ranked = flat_routes[served_order]
    labels = jnp.arange(experts, dtype=jnp.int32)
    onehot = (ranked[:, None] == labels[None, :]).astype(jnp.int32)
    before = (jnp.cumsum(onehot, axis=0) - onehot).astype(jnp.int32)
    ranked_slot = lax.optimization_barrier(jnp.sum(before * onehot, axis=1)).astype(jnp.int32)
    pair_slot = ranked_slot[rank_row.astype(jnp.int32)]
    is_kept = pair_slot < capacity
    slot_dest = jnp.where(is_kept, flat_routes * capacity + pair_slot, experts * capacity).astype(jnp.int32)
    slot_pair = jnp.full((experts * capacity + 1,), pair_count, jnp.int32)
    slot_pair = slot_pair.at[slot_dest].set(jnp.arange(pair_count, dtype=jnp.int32))
    return (slot_dest, slot_pair[:experts * capacity])

def matmul_hi(left_op, right_op):
    return jnp.dot(left_op, right_op, precision=highest, preferred_element_type=jnp.float32)

def sequence_forward(params, tokens_in, blocks, route_rows, rank_row):
    gain_first, gain_second, proj_query, proj_key, proj_value, proj_out, proj_router, expert_gate, expert_up, expert_down = params
    seq_len = tokens_in.shape[0]
    groups = H // KVH
    cos_table, sin_table = rotary_tables(seq_len, HD)
    recip_first = lax.rsqrt(lax.optimization_barrier(jnp.mean(tokens_in * tokens_in, axis=1, keepdims=True)) + norm_eps)
    normed_in = low(tokens_in * recip_first * gain_first)
    queries = low_back(matmul_hi(normed_in, proj_query)).reshape(seq_len, H, HD)
    keys_raw = low_back(matmul_hi(normed_in, proj_key)).reshape(seq_len, KVH, HD)
    values = low(low_back(matmul_hi(normed_in, proj_value))).reshape(seq_len, KVH, HD)
    query_rot = low(rotate(queries, cos_table, sin_table)).reshape(seq_len, KVH, groups, HD)
    key_rot = low(rotate(keys_raw, cos_table, sin_table))
    scores = low_back(attn_scale * jnp.einsum('qhgd,khd->hgqk', query_rot, key_rot, precision=highest))
    visible = blocks[None, :] <= blocks[:, None]
    scores = jnp.where(visible, scores, -1e+30)
    row_peak = lax.optimization_barrier(jnp.max(scores, axis=3, keepdims=True))
    shifted_exp = jnp.exp(scores - row_peak)
    attn_probs = shifted_exp / lax.optimization_barrier(jnp.sum(shifted_exp, axis=3, keepdims=True))
    mixture = jnp.einsum('hgqk,khd->qhgd', low(attn_probs), values, precision=highest).reshape(seq_len, H * HD)
    mixture = low(low_back(mixture))
    attn_out = low_back(matmul_hi(mixture, proj_out))
    residual = tokens_in + res_scale * attn_out
    recip_second = lax.rsqrt(lax.optimization_barrier(jnp.mean(residual * residual, axis=1, keepdims=True)) + norm_eps)
    normed_mid = low(residual * recip_second * gain_second)
    logits = low_back(matmul_hi(normed_mid, proj_router))
    chosen = jnp.take_along_axis(logits, route_rows.astype(jnp.int32), axis=1)
    gate_probs = jax.nn.softmax(chosen, axis=1)
    experts = proj_router.shape[1]
    top_count = route_rows.shape[1]
    slot_dest, slot_pair = slot_table(route_rows, rank_row, experts, CAP)
    padded_rows = jnp.concatenate([normed_mid, jnp.zeros((1, normed_mid.shape[1]), jnp.float32)], axis=0)
    dispatched = low_back(padded_rows[slot_pair // top_count]).reshape(experts, CAP, -1)
    gate_pre = low_back(jnp.einsum('ecd,edf->ecf', dispatched, expert_gate, precision=highest))
    up_pre = low_back(jnp.einsum('ecd,edf->ecf', dispatched, expert_up, precision=highest))
    hidden_act = low(jax.nn.silu(gate_pre) * up_pre)
    produced = low(low_back(jnp.einsum('ecf,efd->ecd', hidden_act, expert_down, precision=highest)))
    padded_out = jnp.concatenate([produced.reshape(experts * CAP, -1), jnp.zeros((1, produced.shape[2]), jnp.float32)], axis=0)
    pair_values = padded_out[slot_dest].reshape(seq_len, top_count, -1)
    blended = jnp.einsum('tk,tkd->td', gate_probs, pair_values, precision=highest)
    return residual + res_scale * blended

def group_forward(weights, token_group, block_group, route_group, rank_group):
    return jax.vmap(sequence_forward, in_axes=(None, 0, 0, 0, 0))(weights, token_group, block_group, route_group, rank_group)

def reference(hidden, cotangent, block_ids, routes, pair_rank, norm1_gain, norm2_gain, w_query, w_key, w_value, w_out, w_router, w_gate, w_up, w_down):
    params = tuple((weight.astype(jnp.float32) for weight in (norm1_gain, norm2_gain, w_query, w_key, w_value, w_out, w_router, w_gate, w_up, w_down)))
    block_groups = block_ids.reshape(N_DP, MICRO, SEQ)
    route_groups = routes.reshape(N_DP, MICRO, SEQ, TOP)
    rank_groups = pair_rank.reshape(N_DP, MICRO, SEQ * TOP)
    checked = jax.checkpoint(group_forward)

    def forward(weights, tokens_all):

        def scan_step(carry, item):
            return (carry, checked(weights, item[0], item[1], item[2], item[3]))
        scan_items = (tokens_all.reshape(N_DP, MICRO, SEQ, D), block_groups, route_groups, rank_groups)
        unused, outputs = lax.scan(scan_step, jnp.zeros((), jnp.float32), scan_items)
        return outputs.reshape(TOKENS, D)
    outputs, pullback = jax.vjp(forward, params, hidden.astype(jnp.float32))
    grads, grad_hidden = pullback(cotangent.astype(jnp.float32))
    return (outputs, grad_hidden, grads[0], grads[1], grads[2], grads[3], grads[4], grads[5], grads[6], grads[7], grads[8], grads[9])
```

```python
import jax
import jax.numpy as jnp
from jax import lax
from jax.sharding import PartitionSpec as P

H = 24
KVH = 8
HD = 64


res_scale = 0.22
attn_scale = 0.015625
norm_eps = 1e-06
rope_base = 10000.0


def rotary_tables(length, head_size):
    half_size = head_size // 2
    frequency = rope_base ** (-(jnp.arange(half_size, dtype=jnp.float32) * 2.0) / head_size)
    angles = jnp.arange(length, dtype=jnp.float32)[:, None] * frequency[None, :]
    return (jnp.cos(angles)[:, None, :], jnp.sin(angles)[:, None, :])


def rotate(operand, cos_table, sin_table):
    half_size = operand.shape[-1] // 2
    lower_half = operand[..., :half_size]
    upper_half = operand[..., half_size:]
    return jnp.concatenate(
        [
            lower_half * cos_table - upper_half * sin_table,
            upper_half * cos_table + lower_half * sin_table,
        ],
        axis=-1,
    )


def unrotate(operand, cos_table, sin_table):
    half_size = operand.shape[-1] // 2
    lower_half = operand[..., :half_size]
    upper_half = operand[..., half_size:]
    return jnp.concatenate(
        [
            lower_half * cos_table + upper_half * sin_table,
            upper_half * cos_table - lower_half * sin_table,
        ],
        axis=-1,
    )


LINES = 4


def norm_backward(grad_normed, source, recip, gain):
    scaled_grad = grad_normed * gain
    grad_source = recip * scaled_grad - source * (recip * recip * recip) * jnp.mean(
        scaled_grad * source, axis=1, keepdims=True
    )
    return (grad_source, jnp.sum(grad_normed * source * recip, axis=0))


def masked_gates(logits, routed):
    peak = jnp.max(jnp.where(routed, logits, -jnp.inf), axis=-2, keepdims=True)
    shifted = jnp.where(routed, jnp.exp(jnp.minimum(logits - peak, 0.0)), 0.0)
    return shifted / jnp.sum(shifted, axis=-2, keepdims=True)


def on_device(
    hidden,
    cotangent,
    block_ids,
    routes,
    pair_rank,
    norm1_gain,
    norm2_gain,
    w_query,
    w_key,
    w_value,
    w_out,
    w_router,
    w_gate,
    w_up,
    w_down,
):
    micro_count, seq_len = block_ids.shape
    model_width = hidden.shape[1]
    top_count = routes.shape[1]
    devices = lax.axis_size("dp")
    experts = w_router.shape[1]
    plane = devices // LINES
    capacity = (9 * seq_len * top_count + 8 * experts - 1) // (8 * experts)
    groups = H // KVH
    query_width = w_query.shape[1]
    kv_width = w_key.shape[1]
    qkv_width = query_width + 2 * kv_width
    cos_table, sin_table = rotary_tables(seq_len, HD)
    gate_local = w_gate[0]
    up_local = w_up[0]
    down_local = w_down[0]
    bf16 = jnp.bfloat16
    f32 = jnp.float32
    here = lax.axis_index("dp") // plane
    plane_groups = [[line * plane + i for i in range(plane)] for line in range(LINES)]

    def line_shift(step):
        return [
            (i, ((i // plane + step) % LINES) * plane + i % plane) for i in range(devices)
        ]

    def spread(block):
        return [block] + [
            lax.ppermute(block, "dp", line_shift(step)) for step in range(1, LINES)
        ]

    def give_back(blocks):
        return [blocks[0]] + [
            lax.ppermute(blocks[step], "dp", line_shift(-step)) for step in range(1, LINES)
        ]

    def exchange(block):
        return lax.all_to_all(
            block, "dp", split_axis=0, concat_axis=0, tiled=True, axis_index_groups=plane_groups
        )

    small = jnp.concatenate([norm1_gain[:, None], norm2_gain[:, None], w_router], axis=1)
    pad = -small.shape[1] % 128
    first = lax.all_gather(
        jnp.concatenate(
            [w_query, w_key, w_value, jnp.pad(small, ((0, 0), (0, pad)))], axis=1
        ),
        "dp",
        axis=0,
        tiled=True,
    )
    out_proj = lax.all_gather(w_out, "dp", axis=0, tiled=True)
    qkv_proj = first[:, :qkv_width]
    gain_first = first[:, qkv_width].astype(f32)
    gain_second = first[:, qkv_width + 1].astype(f32)
    router = first[:, qkv_width + 2 : qkv_width + 2 + experts]

    labels = jnp.arange(experts, dtype=jnp.int32)
    route_seq = routes.reshape(micro_count, seq_len, top_count)
    rank_seq = pair_rank.reshape(micro_count, seq_len, top_count)
    named = route_seq[:, None, :, :] == labels[None, :, None, None]
    routed = jnp.any(named, axis=3)
    rank_of = jnp.where(
        routed, jnp.sum(jnp.where(named, rank_seq[:, None], 0), axis=3), seq_len * top_count
    )
    ahead = jnp.sum((rank_of[:, :, :, None] < rank_of[:, :, None, :]).astype(jnp.int32), axis=2)
    slot_of = jnp.where(routed, ahead, -1)
    slot_blocks = jnp.stack(spread(slot_of))
    slots_here = lax.dynamic_slice_in_dim(slot_blocks, here * plane, plane, axis=2)
    places = jnp.arange(capacity, dtype=jnp.int32)
    picks = [
        (slots_here[:, micro, :, None, :] == places[None, None, :, None]).astype(bf16)
        for micro in range(micro_count)
    ]

    cotan_seq = cotangent.reshape(micro_count, seq_len, model_width)
    hidden_seq = hidden.reshape(micro_count, seq_len, model_width)

    def dispatch(micro, blocks):
        rows = jnp.einsum(
            "ject,jtd->ejcd", picks[micro], jnp.stack(blocks), preferred_element_type=f32
        ).astype(bf16)
        return exchange(rows.reshape(plane, LINES * capacity, model_width)).reshape(
            -1, model_width
        )

    def combine(micro, rows):
        arrived = exchange(rows.reshape(plane, LINES * capacity, model_width)).reshape(
            plane, LINES, capacity, model_width
        )
        sums = jnp.einsum(
            "ject,ejcd->jtd", picks[micro], arrived, preferred_element_type=f32
        ).astype(bf16)
        back = give_back([sums[step] for step in range(LINES)])
        total = back[0].astype(f32)
        for part in back[1:]:
            total = total + part.astype(f32)
        return total

    grad_arrived = [
        dispatch(micro, spread((res_scale * cotan_seq[micro]).astype(bf16)))
        for micro in range(micro_count)
    ]

    kept = []
    for micro in range(micro_count):
        tokens_in = hidden_seq[micro]
        blocks = block_ids[micro]
        recip_first = lax.rsqrt(jnp.mean(tokens_in * tokens_in, axis=1, keepdims=True) + norm_eps)
        normed_in = (tokens_in * recip_first * gain_first).astype(bf16)
        projected = jnp.dot(normed_in, qkv_proj, preferred_element_type=f32)
        queries = projected[:, :query_width].reshape(seq_len, H, HD)
        keys_raw = projected[:, query_width : query_width + kv_width].reshape(seq_len, KVH, HD)
        values = projected[:, query_width + kv_width :].astype(bf16).reshape(seq_len, KVH, HD)
        query_rot = (
            rotate(queries, cos_table, sin_table).astype(bf16).reshape(seq_len, KVH, groups, HD)
        )
        key_rot = rotate(keys_raw, cos_table, sin_table).astype(bf16)
        visible = blocks[None, :] <= blocks[:, None]
        scores = attn_scale * jnp.einsum(
            "qhgd,khd->hgqk", query_rot, key_rot, preferred_element_type=f32
        )
        scores = jnp.where(visible, scores, -1e30)
        row_peak = jnp.max(scores, axis=3, keepdims=True)
        shifted_exp = jnp.exp(scores - row_peak)
        row_total = jnp.sum(shifted_exp, axis=3, keepdims=True)
        attn_probs = shifted_exp / row_total
        log_total = row_peak + jnp.log(row_total)
        mixture = (
            jnp.einsum(
                "hgqk,khd->qhgd", attn_probs.astype(bf16), values, preferred_element_type=f32
            )
            .reshape(seq_len, H * HD)
            .astype(bf16)
        )
        attn_out = jnp.dot(mixture, out_proj, preferred_element_type=f32)
        residual = tokens_in + res_scale * attn_out
        recip_second = lax.rsqrt(jnp.mean(residual * residual, axis=1, keepdims=True) + norm_eps)
        normed_mid = (residual * recip_second * gain_second).astype(bf16)
        kept.append(
            (
                recip_first,
                normed_in,
                values,
                query_rot,
                key_rot,
                visible,
                log_total,
                mixture,
                residual,
                recip_second,
                normed_mid,
            )
        )

    returned = []
    grad_down_w = grad_gate_w = grad_up_w = 0.0
    for micro in range(micro_count):
        normed_mid = kept[micro][-1]
        blocks = spread(normed_mid)
        logits = jnp.einsum(
            "de,jtd->jet", router, jnp.stack(blocks), preferred_element_type=f32
        )
        gates = masked_gates(logits, slot_blocks[:, micro] >= 0)
        gates_here = lax.dynamic_slice_in_dim(gates, here * plane, plane, axis=1)
        slot_gates = jnp.sum(
            jnp.where(picks[micro] > 0, gates_here[:, :, None, :], 0.0), axis=3
        ).transpose(1, 0, 2)
        gate_rows = exchange(slot_gates.reshape(plane, LINES * capacity)).reshape(-1, 1)
        arrived = dispatch(micro, blocks)
        blend_rows = grad_arrived[micro]
        gate_pre = jnp.dot(arrived, gate_local, preferred_element_type=f32)
        up_pre = jnp.dot(arrived, up_local, preferred_element_type=f32)
        logistic = jax.nn.sigmoid(gate_pre)
        silu = gate_pre * logistic
        hidden_act = (silu * up_pre).astype(bf16)
        produced = jnp.dot(hidden_act, down_local, preferred_element_type=f32)
        pair_grads = jnp.sum(produced * blend_rows.astype(f32), axis=1)
        scaled = (gate_rows * produced).astype(bf16)
        grad_produced = (gate_rows * blend_rows.astype(f32)).astype(bf16)
        grad_inner = jnp.einsum(
            "rd,fd->rf", grad_produced, down_local, preferred_element_type=f32
        )
        grad_gate_pre = (
            grad_inner * up_pre * (logistic * (1.0 + gate_pre * (1.0 - logistic)))
        ).astype(bf16)
        grad_up_pre = (grad_inner * silu).astype(bf16)
        grad_rows = jnp.einsum(
            "rf,df->rd", grad_gate_pre, gate_local, preferred_element_type=f32
        )
        grad_rows = grad_rows + jnp.einsum(
            "rf,df->rd", grad_up_pre, up_local, preferred_element_type=f32
        )
        pair_back = exchange(pair_grads.reshape(plane, LINES * capacity)).reshape(
            plane, LINES, capacity
        )
        token_grads = jnp.sum(
            jnp.where(picks[micro] > 0, pair_back.transpose(1, 0, 2)[:, :, :, None], 0.0), axis=2
        )
        pair_blocks = give_back([token_grads[step] for step in range(LINES)])
        grad_mid_sum = combine(micro, grad_rows.astype(bf16))
        blended = combine(micro, scaled)
        returned.append((grad_mid_sum, blended, pair_blocks, gates[0]))
        grad_down_w = grad_down_w + jnp.einsum(
            "rf,rd->fd", hidden_act, grad_produced, preferred_element_type=f32
        )
        grad_gate_w = grad_gate_w + jnp.einsum(
            "rd,rf->df", arrived, grad_gate_pre, preferred_element_type=f32
        )
        grad_up_w = grad_up_w + jnp.einsum(
            "rd,rf->df", arrived, grad_up_pre, preferred_element_type=f32
        )

    outputs = []
    token_grads_out = []
    gain_first_w = gain_second_w = qkv_w = out_w = router_w = 0.0
    for micro in range(micro_count):
        (
            recip_first,
            normed_in,
            values,
            query_rot,
            key_rot,
            visible,
            log_total,
            mixture,
            residual,
            recip_second,
            normed_mid,
        ) = kept[micro]
        grad_mid_sum, blended, pair_blocks, gates = returned[micro]
        tokens_in = hidden_seq[micro]
        cotan_in = cotan_seq[micro]
        outputs.append(residual + blended * res_scale)
        pair_grads = jnp.zeros((experts, seq_len), f32)
        for step in range(LINES):
            pair_grads = lax.dynamic_update_slice_in_dim(
                pair_grads, pair_blocks[step], ((here + step) % LINES) * plane, axis=0
            )
        grad_logits = (
            gates * (pair_grads - jnp.sum(gates * pair_grads, axis=0, keepdims=True))
        ).astype(bf16)
        router_w = router_w + jnp.einsum(
            "td,et->de", normed_mid, grad_logits, preferred_element_type=f32
        )
        grad_mid = grad_mid_sum + jnp.einsum(
            "et,de->td", grad_logits, router, preferred_element_type=f32
        )
        grad_residual, grad_gain = norm_backward(grad_mid, residual, recip_second, gain_second)
        gain_second_w = gain_second_w + grad_gain
        grad_residual = cotan_in + grad_residual
        grad_attn = (res_scale * grad_residual).astype(bf16)
        out_w = out_w + jnp.einsum("tc,td->cd", mixture, grad_attn, preferred_element_type=f32)
        grad_mixture = (
            jnp.einsum("td,cd->tc", grad_attn, out_proj, preferred_element_type=f32)
            .astype(bf16)
            .reshape(seq_len, KVH, groups, HD)
        )
        scores_again = attn_scale * jnp.einsum(
            "qhgd,khd->hgqk", query_rot, key_rot, preferred_element_type=f32
        )
        scores_again = jnp.where(visible, scores_again, -1e30)
        probs_again = jnp.exp(scores_again - log_total)
        grad_probs = jnp.einsum("qhgd,khd->hgqk", grad_mixture, values, preferred_element_type=f32)
        grad_values = (
            jnp.einsum(
                "hgqk,qhgd->khd", probs_again.astype(bf16), grad_mixture, preferred_element_type=f32
            )
            .astype(bf16)
            .reshape(seq_len, KVH * HD)
        )
        grad_scores = (
            probs_again * (grad_probs - jnp.sum(probs_again * grad_probs, axis=3, keepdims=True))
        ).astype(bf16)
        grad_query_rot = attn_scale * jnp.einsum(
            "hgqk,khd->qhgd", grad_scores, key_rot, preferred_element_type=f32
        )
        grad_key_rot = attn_scale * jnp.einsum(
            "hgqk,qhgd->khd", grad_scores, query_rot, preferred_element_type=f32
        )
        grad_queries = (
            unrotate(grad_query_rot.reshape(seq_len, H, HD), cos_table, sin_table)
            .astype(bf16)
            .reshape(seq_len, H * HD)
        )
        grad_keys = (
            unrotate(grad_key_rot, cos_table, sin_table).astype(bf16).reshape(seq_len, KVH * HD)
        )
        grad_qkv = jnp.concatenate([grad_queries, grad_keys, grad_values], axis=1)
        qkv_w = qkv_w + jnp.einsum("td,tc->dc", normed_in, grad_qkv, preferred_element_type=f32)
        grad_normed = jnp.einsum("tc,dc->td", grad_qkv, qkv_proj, preferred_element_type=f32)
        grad_source, grad_gain = norm_backward(grad_normed, tokens_in, recip_first, gain_first)
        gain_first_w = gain_first_w + grad_gain
        token_grads_out.append(grad_residual + grad_source)

    small_w = jnp.concatenate([gain_second_w[:, None], router_w], axis=1)
    small_w = jnp.pad(small_w, ((0, 0), (0, -small_w.shape[1] % 128)))
    out_sum = lax.psum_scatter(
        jnp.concatenate([out_w, small_w], axis=1).astype(bf16),
        "dp",
        scatter_dimension=0,
        tiled=True,
    ).astype(f32)
    qkv_sum = lax.psum_scatter(
        jnp.concatenate([qkv_w, jnp.pad(gain_first_w[:, None], ((0, 0), (0, 127)))], axis=1).astype(
            bf16
        ),
        "dp",
        scatter_dimension=0,
        tiled=True,
    ).astype(f32)
    return (
        jnp.concatenate(outputs, axis=0),
        jnp.concatenate(token_grads_out, axis=0),
        qkv_sum[:, qkv_width],
        out_sum[:, model_width],
        qkv_sum[:, :query_width],
        qkv_sum[:, query_width : query_width + kv_width],
        qkv_sum[:, query_width + kv_width : qkv_width],
        out_sum[:, :model_width],
        out_sum[:, model_width + 1 : model_width + 1 + experts],
        grad_gate_w[None],
        grad_up_w[None],
        grad_down_w[None],
    )


def solution(mesh):
    return jax.shard_map(
        on_device,
        mesh=mesh,
        in_specs=(
            P("dp", None),
            P("dp", None),
            P("dp", None),
            P("dp", None),
            P("dp", None),
            P("dp"),
            P("dp"),
            P("dp", None),
            P("dp", None),
            P("dp", None),
            P("dp", None),
            P("dp", None),
            P("dp", None, None),
            P("dp", None, None),
            P("dp", None, None),
        ),
        out_specs=(
            P("dp", None),
            P("dp", None),
            P("dp"),
            P("dp"),
            P("dp", None),
            P("dp", None),
            P("dp", None),
            P("dp", None),
            P("dp", None),
            P("dp", None, None),
            P("dp", None, None),
            P("dp", None, None),
        ),
        check_vma=False,
    )
```

```python
import jax
import jax.numpy as jnp
from jax import lax
from jax.experimental import pallas as pl
from jax.sharding import PartitionSpec as P

H = 24
KVH = 8
HD = 64


res_scale = 0.22
attn_scale = 0.015625
norm_eps = 1e-06
rope_base = 10000.0


def rotary_tables(length, head_size):
    half_size = head_size // 2
    frequency = rope_base ** (-(jnp.arange(half_size, dtype=jnp.float32) * 2.0) / head_size)
    angles = jnp.arange(length, dtype=jnp.float32)[:, None] * frequency[None, :]
    return (jnp.cos(angles)[:, None, :], jnp.sin(angles)[:, None, :])


def rotate(operand, cos_table, sin_table):
    half_size = operand.shape[-1] // 2
    lower_half = operand[..., :half_size]
    upper_half = operand[..., half_size:]
    return jnp.concatenate(
        [
            lower_half * cos_table - upper_half * sin_table,
            upper_half * cos_table + lower_half * sin_table,
        ],
        axis=-1,
    )


def unrotate(operand, cos_table, sin_table):
    half_size = operand.shape[-1] // 2
    lower_half = operand[..., :half_size]
    upper_half = operand[..., half_size:]
    return jnp.concatenate(
        [
            lower_half * cos_table + upper_half * sin_table,
            upper_half * cos_table - lower_half * sin_table,
        ],
        axis=-1,
    )


LINES = 4


def norm_backward(grad_normed, source, recip, gain):
    scaled_grad = grad_normed * gain
    grad_source = recip * scaled_grad - source * (recip * recip * recip) * jnp.mean(
        scaled_grad * source, axis=1, keepdims=True
    )
    return (grad_source, jnp.sum(grad_normed * source * recip, axis=0))


def masked_gates(logits, routed):
    peak = jnp.max(jnp.where(routed, logits, -jnp.inf), axis=-2, keepdims=True)
    shifted = jnp.where(routed, jnp.exp(jnp.minimum(logits - peak, 0.0)), 0.0)
    return shifted / jnp.sum(shifted, axis=-2, keepdims=True)


def expert_kernel(
    rows_ref,
    blend_ref,
    gates_ref,
    gate_ref,
    up_ref,
    down_ref,
    grads_ref,
    scaled_ref,
    pairs_ref,
    gate_sum_ref,
    up_sum_ref,
    down_sum_ref,
):
    f32 = jnp.float32
    bf16 = jnp.bfloat16

    def product(left, right, left_axis, right_axis):
        return lax.dot_general(
            left, right, (((left_axis,), (right_axis,)), ((), ())), preferred_element_type=f32
        )

    @pl.when(pl.program_id(0) == 0)
    def _():
        gate_sum_ref[...] = jnp.zeros_like(gate_sum_ref)
        up_sum_ref[...] = jnp.zeros_like(up_sum_ref)
        down_sum_ref[...] = jnp.zeros_like(down_sum_ref)

    rows = rows_ref[...]
    gates = gates_ref[...]
    blend = blend_ref[...].astype(f32)
    gate_pre = product(rows, gate_ref[...], 1, 0)
    up_pre = product(rows, up_ref[...], 1, 0)
    logistic = 1.0 / (1.0 + jnp.exp(-gate_pre))
    silu = gate_pre * logistic
    hidden_act = (silu * up_pre).astype(bf16)
    produced = product(hidden_act, down_ref[...], 1, 0)
    pairs_ref[...] = jnp.sum(produced * blend, axis=1, keepdims=True)
    scaled_ref[...] = (gates * produced).astype(bf16)
    grad_produced = (gates * blend).astype(bf16)
    grad_inner = product(grad_produced, down_ref[...], 1, 1)
    grad_gate_pre = (
        grad_inner * up_pre * (logistic * (1.0 + gate_pre * (1.0 - logistic)))
    ).astype(bf16)
    grad_up_pre = (grad_inner * silu).astype(bf16)
    grads_ref[...] = (
        product(grad_gate_pre, gate_ref[...], 1, 1) + product(grad_up_pre, up_ref[...], 1, 1)
    ).astype(bf16)
    down_sum_ref[...] += product(hidden_act, grad_produced, 0, 0)
    gate_sum_ref[...] += product(rows, grad_gate_pre, 0, 0)
    up_sum_ref[...] += product(rows, grad_up_pre, 0, 0)


def run_experts(rows, blend, gates, gate_local, up_local, down_local):
    count, width = rows.shape
    ff_width = gate_local.shape[1]
    block = next(b for b in (384, 256, 128, count) if count % b == 0)
    f32 = jnp.float32
    wide = pl.BlockSpec((block, width), lambda i: (i, 0))
    thin = pl.BlockSpec((block, 1), lambda i: (i, 0))
    inner = pl.BlockSpec((width, ff_width), lambda i: (0, 0))
    outer = pl.BlockSpec((ff_width, width), lambda i: (0, 0))
    return pl.pallas_call(
        expert_kernel,
        grid=(count // block,),
        in_specs=[wide, wide, thin, inner, inner, outer],
        out_specs=[wide, wide, thin, inner, inner, outer],
        out_shape=[
            jax.ShapeDtypeStruct((count, width), rows.dtype),
            jax.ShapeDtypeStruct((count, width), rows.dtype),
            jax.ShapeDtypeStruct((count, 1), f32),
            jax.ShapeDtypeStruct((width, ff_width), f32),
            jax.ShapeDtypeStruct((width, ff_width), f32),
            jax.ShapeDtypeStruct((ff_width, width), f32),
        ],
        cost_estimate=pl.CostEstimate(flops=1000, bytes_accessed=1000, transcendentals=0),
        name="experts",
    )(rows, blend, gates, gate_local, up_local, down_local)


def build_kernel(slots_ref, *refs):
    out_ref = refs[-1]
    plane, lines, capacity, width = out_ref.shape
    for line in range(lines):
        slots = slots_ref[line]
        places = lax.broadcasted_iota(jnp.int32, (plane, capacity, slots.shape[1]), 1)
        picks = jnp.where(slots[:, None, :] == places, 1.0, 0.0)
        rows = jnp.dot(
            picks.reshape(plane * capacity, slots.shape[1]).astype(jnp.bfloat16),
            refs[line][...],
            preferred_element_type=jnp.float32,
        )
        out_ref[:, line] = rows.reshape(plane, capacity, width).astype(jnp.bfloat16)


def build_rows(slots, blocks, capacity):
    lines, plane, unused = slots.shape
    width = blocks[0].shape[1]
    return pl.pallas_call(
        build_kernel,
        out_shape=jax.ShapeDtypeStruct((plane, lines, capacity, width), blocks[0].dtype),
        cost_estimate=pl.CostEstimate(flops=1000, bytes_accessed=1000, transcendentals=0),
        name="build_rows",
    )(slots, *blocks)


def on_device(
    hidden,
    cotangent,
    block_ids,
    routes,
    pair_rank,
    norm1_gain,
    norm2_gain,
    w_query,
    w_key,
    w_value,
    w_out,
    w_router,
    w_gate,
    w_up,
    w_down,
):
    micro_count, seq_len = block_ids.shape
    model_width = hidden.shape[1]
    top_count = routes.shape[1]
    devices = lax.axis_size("dp")
    experts = w_router.shape[1]
    plane = devices // LINES
    capacity = (9 * seq_len * top_count + 8 * experts - 1) // (8 * experts)
    groups = H // KVH
    query_width = w_query.shape[1]
    kv_width = w_key.shape[1]
    qkv_width = query_width + 2 * kv_width
    cos_table, sin_table = rotary_tables(seq_len, HD)
    gate_local = w_gate[0]
    up_local = w_up[0]
    down_local = w_down[0]
    bf16 = jnp.bfloat16
    f32 = jnp.float32
    here = lax.axis_index("dp") // plane
    plane_groups = [[line * plane + i for i in range(plane)] for line in range(LINES)]

    def line_shift(step):
        return [
            (i, ((i // plane + step) % LINES) * plane + i % plane) for i in range(devices)
        ]

    def spread(block):
        return [block] + [
            lax.ppermute(block, "dp", line_shift(step)) for step in range(1, LINES)
        ]

    def give_back(blocks):
        return [blocks[0]] + [
            lax.ppermute(blocks[step], "dp", line_shift(-step)) for step in range(1, LINES)
        ]

    def exchange(block):
        return lax.all_to_all(
            block, "dp", split_axis=0, concat_axis=0, tiled=True, axis_index_groups=plane_groups
        )

    small = jnp.concatenate([norm1_gain[:, None], norm2_gain[:, None], w_router], axis=1)
    pad = -small.shape[1] % 128
    first = lax.all_gather(
        jnp.concatenate(
            [w_query, w_key, w_value, jnp.pad(small, ((0, 0), (0, pad)))], axis=1
        ),
        "dp",
        axis=0,
        tiled=True,
    )
    out_proj = lax.all_gather(w_out, "dp", axis=0, tiled=True)
    qkv_proj = first[:, :qkv_width]
    gain_first = first[:, qkv_width].astype(f32)
    gain_second = first[:, qkv_width + 1].astype(f32)
    router = first[:, qkv_width + 2 : qkv_width + 2 + experts]

    labels = jnp.arange(experts, dtype=jnp.int32)
    route_seq = routes.reshape(micro_count, seq_len, top_count)
    rank_seq = pair_rank.reshape(micro_count, seq_len, top_count)
    named = route_seq[:, None, :, :] == labels[None, :, None, None]
    routed = jnp.any(named, axis=3)
    rank_of = jnp.where(
        routed, jnp.sum(jnp.where(named, rank_seq[:, None], 0), axis=3), seq_len * top_count
    )
    ahead = jnp.sum((rank_of[:, :, :, None] < rank_of[:, :, None, :]).astype(jnp.int32), axis=2)
    slot_of = jnp.where(routed, ahead, -1)
    slot_blocks = jnp.stack(spread(slot_of))
    slots_here = lax.dynamic_slice_in_dim(slot_blocks, here * plane, plane, axis=2)
    places = jnp.arange(capacity, dtype=jnp.int32)
    picks = [
        (slots_here[:, micro, :, None, :] == places[None, None, :, None]).astype(bf16)
        for micro in range(micro_count)
    ]

    cotan_seq = cotangent.reshape(micro_count, seq_len, model_width)
    hidden_seq = hidden.reshape(micro_count, seq_len, model_width)

    def hold(value, *after):
        return lax.optimization_barrier((value, after))[0]

    def build(micro, blocks):
        if capacity % 8 == 0:
            rows = build_rows(slots_here[:, micro], blocks, capacity)
        else:
            rows = jnp.einsum(
                "ject,jtd->ejcd", picks[micro], jnp.stack(blocks), preferred_element_type=f32
            ).astype(bf16)
        return rows.reshape(plane, LINES * capacity, model_width)

    def sums_of(micro, arrived):
        sums = jnp.einsum(
            "ject,ejcd->jtd",
            picks[micro],
            arrived.reshape(plane, LINES, capacity, model_width),
            preferred_element_type=f32,
        ).astype(bf16)
        return give_back([sums[step] for step in range(LINES)])

    def total_of(parts):
        total = parts[0].astype(f32)
        for part in parts[1:]:
            total = total + part.astype(f32)
        return total

    def attend(unused, inputs):
        tokens_in, blocks = inputs
        recip_first = lax.rsqrt(jnp.mean(tokens_in * tokens_in, axis=1, keepdims=True) + norm_eps)
        normed_in = (tokens_in * recip_first * gain_first).astype(bf16)
        projected = jnp.dot(normed_in, qkv_proj, preferred_element_type=f32)
        queries = projected[:, :query_width].reshape(seq_len, H, HD)
        keys_raw = projected[:, query_width : query_width + kv_width].reshape(seq_len, KVH, HD)
        values = projected[:, query_width + kv_width :].astype(bf16).reshape(seq_len, KVH, HD)
        query_rot = (
            rotate(queries, cos_table, sin_table).astype(bf16).reshape(seq_len, KVH, groups, HD)
        )
        key_rot = rotate(keys_raw, cos_table, sin_table).astype(bf16)
        visible = blocks[None, :] <= blocks[:, None]
        scores = attn_scale * jnp.einsum(
            "qhgd,khd->hgqk", query_rot, key_rot, preferred_element_type=f32
        )
        scores = jnp.where(visible, scores, -1e30)
        row_peak = jnp.max(scores, axis=3, keepdims=True)
        shifted_exp = jnp.exp(scores - row_peak)
        row_total = jnp.sum(shifted_exp, axis=3, keepdims=True)
        attn_probs = shifted_exp / row_total
        log_total = row_peak + jnp.log(row_total)
        mixture = (
            jnp.einsum(
                "hgqk,khd->qhgd", attn_probs.astype(bf16), values, preferred_element_type=f32
            )
            .reshape(seq_len, H * HD)
            .astype(bf16)
        )
        return (
            unused,
            dict(
                recip_first=recip_first,
                normed_in=normed_in,
                values=values,
                query_rot=query_rot,
                key_rot=key_rot,
                log_total=log_total,
                mixture=mixture,
            ),
        )

    def after_attention(kept, tokens_in):
        attn_out = jnp.dot(kept["mixture"], out_proj, preferred_element_type=f32)
        residual = tokens_in + res_scale * attn_out
        recip_second = lax.rsqrt(jnp.mean(residual * residual, axis=1, keepdims=True) + norm_eps)
        normed_mid = (residual * recip_second * gain_second).astype(bf16)
        return dict(kept, residual=residual, recip_second=recip_second, normed_mid=normed_mid)

    def gates_of(micro, blocks):
        logits = jnp.einsum("de,jtd->jet", router, jnp.stack(blocks), preferred_element_type=f32)
        gates = masked_gates(logits, slot_blocks[:, micro] >= 0)
        gates_here = lax.dynamic_slice_in_dim(gates, here * plane, plane, axis=1)
        slot_gates = jnp.sum(
            jnp.where(picks[micro] > 0, gates_here[:, :, None, :], 0.0), axis=3
        ).transpose(1, 0, 2)
        return gates[0], slot_gates.reshape(plane, LINES * capacity)

    def run_expert(mid, blend, gate_rows):
        grads, scaled, pair_grads, *weights = run_experts(
            mid.reshape(-1, model_width),
            blend.reshape(-1, model_width),
            gate_rows.reshape(-1, 1),
            gate_local,
            up_local,
            down_local,
        )
        return (
            grads.reshape(mid.shape),
            scaled.reshape(mid.shape),
            pair_grads.reshape(mid.shape[:2]),
            weights,
        )

    def pairs_home(pair_back):
        token_grads = [
            jnp.sum(
                jnp.where(
                    picks[m] > 0,
                    pair_back[:, m]
                    .reshape(plane, LINES, capacity)
                    .transpose(1, 0, 2)[:, :, :, None],
                    0.0,
                ),
                axis=2,
            )
            for m in range(micro_count)
        ]
        both = jnp.stack(token_grads, axis=1)
        return give_back([both[step] for step in range(LINES)])

    def attend_back(micro, grad_mid_sum, pair_blocks, gates, kept):
        tokens_in = hidden_seq[micro]
        cotan_in = cotan_seq[micro]
        recip_first, normed_in, values = kept["recip_first"], kept["normed_in"], kept["values"]
        query_rot, key_rot = kept["query_rot"], kept["key_rot"]
        visible = block_ids[micro][None, :] <= block_ids[micro][:, None]
        log_total, mixture, residual = kept["log_total"], kept["mixture"], kept["residual"]
        recip_second, normed_mid = kept["recip_second"], kept["normed_mid"]
        pair_grads = jnp.zeros((experts, seq_len), f32)
        for step in range(LINES):
            pair_grads = lax.dynamic_update_slice_in_dim(
                pair_grads, pair_blocks[step], ((here + step) % LINES) * plane, axis=0
            )
        grad_logits = (
            gates * (pair_grads - jnp.sum(gates * pair_grads, axis=0, keepdims=True))
        ).astype(bf16)
        router_w = jnp.einsum(
            "td,et->de", normed_mid, grad_logits, preferred_element_type=f32
        )
        grad_mid = grad_mid_sum + jnp.einsum(
            "et,de->td", grad_logits, router, preferred_element_type=f32
        )
        grad_residual, grad_gain = norm_backward(grad_mid, residual, recip_second, gain_second)
        gain_second_w = grad_gain
        grad_residual = cotan_in + grad_residual
        grad_attn = (res_scale * grad_residual).astype(bf16)
        out_w = jnp.einsum("tc,td->cd", mixture, grad_attn, preferred_element_type=f32)
        grad_mixture = (
            jnp.einsum("td,cd->tc", grad_attn, out_proj, preferred_element_type=f32)
            .astype(bf16)
            .reshape(seq_len, KVH, groups, HD)
        )
        scores_again = attn_scale * jnp.einsum(
            "qhgd,khd->hgqk", query_rot, key_rot, preferred_element_type=f32
        )
        scores_again = jnp.where(visible, scores_again, -1e30)
        probs_again = jnp.exp(scores_again - log_total)
        grad_probs = jnp.einsum("qhgd,khd->hgqk", grad_mixture, values, preferred_element_type=f32)
        grad_values = (
            jnp.einsum(
                "hgqk,qhgd->khd", probs_again.astype(bf16), grad_mixture, preferred_element_type=f32
            )
            .astype(bf16)
            .reshape(seq_len, KVH * HD)
        )
        grad_scores = (
            probs_again * (grad_probs - jnp.sum(probs_again * grad_probs, axis=3, keepdims=True))
        ).astype(bf16)
        grad_query_rot = attn_scale * jnp.einsum(
            "hgqk,khd->qhgd", grad_scores, key_rot, preferred_element_type=f32
        )
        grad_key_rot = attn_scale * jnp.einsum(
            "hgqk,qhgd->khd", grad_scores, query_rot, preferred_element_type=f32
        )
        grad_queries = (
            unrotate(grad_query_rot.reshape(seq_len, H, HD), cos_table, sin_table)
            .astype(bf16)
            .reshape(seq_len, H * HD)
        )
        grad_keys = (
            unrotate(grad_key_rot, cos_table, sin_table).astype(bf16).reshape(seq_len, KVH * HD)
        )
        grad_qkv = jnp.concatenate([grad_queries, grad_keys, grad_values], axis=1)
        qkv_w = jnp.einsum("td,tc->dc", normed_in, grad_qkv, preferred_element_type=f32)
        grad_normed = jnp.einsum("tc,dc->td", grad_qkv, qkv_proj, preferred_element_type=f32)
        grad_source, grad_gain = norm_backward(grad_normed, tokens_in, recip_first, gain_first)
        return (
            grad_residual + grad_source,
            out_w,
            qkv_w,
            grad_gain,
            gain_second_w,
            router_w,
        )

    blend_blocks = [spread((res_scale * cotan_seq[m]).astype(bf16)) for m in range(2)]
    blend0 = build(0, blend_blocks[0])
    moved_blend0 = exchange(blend0)
    unused, kept_both = lax.scan(
        attend, jnp.zeros((), f32), (hold(hidden_seq, blend0), block_ids)
    )
    blend1 = build(1, hold(blend_blocks[1], kept_both["mixture"]))
    moved_blend1 = exchange(hold(blend1, moved_blend0))
    kept0, kept1 = (
        after_attention({name: part[m] for name, part in kept_both.items()}, hidden_seq[m])
        for m in range(2)
    )
    blocks0 = spread(kept0["normed_mid"])
    blocks1 = spread(kept1["normed_mid"])
    moved_mid0 = exchange(hold(build(0, blocks0), moved_blend1))
    gates0, slot_gates0 = gates_of(0, blocks0)
    gates1, slot_gates1 = gates_of(1, blocks1)
    gate_rows = exchange(
        hold(jnp.stack([slot_gates0, slot_gates1], axis=1), moved_mid0)
    )
    mid1 = build(1, blocks1)
    moved_mid1 = exchange(hold(mid1, gate_rows))
    grads0, scaled0, pairs0, weights0 = run_expert(
        hold(moved_mid0, mid1), moved_blend0, gate_rows[:, 0]
    )
    moved_grads0 = exchange(hold(grads0, moved_mid1))
    grads1, scaled1, pairs1, weights1 = run_expert(moved_mid1, moved_blend1, gate_rows[:, 1])
    pair_back = exchange(hold(jnp.stack([pairs0, pairs1], axis=1), moved_grads0))
    moved_grads1 = exchange(hold(grads1, pair_back))
    pair_blocks = pairs_home(pair_back)
    back0 = sums_of(0, moved_grads0)
    moved_scaled0 = exchange(hold(scaled0, moved_grads1, back0))
    back1 = sums_of(1, moved_grads1)
    result0 = attend_back(
        0, total_of(back0), [block[0] for block in pair_blocks], gates0, kept0
    )
    moved_scaled1 = exchange(hold(scaled1, moved_scaled0, back1, result0))
    blend_back0 = sums_of(0, moved_scaled0)
    result1 = attend_back(
        1, hold(total_of(back1), result0), [block[1] for block in pair_blocks], gates1, kept1
    )
    blend_back1 = sums_of(1, moved_scaled1)
    outputs = [
        kept0["residual"] + res_scale * total_of(blend_back0),
        kept1["residual"] + res_scale * total_of(blend_back1),
    ]
    token_grads_out = [result0[0], result1[0]]
    out_w, qkv_w, gain_first_w, gain_second_w, router_w = (
        a + b for a, b in zip(result0[1:], result1[1:], strict=True)
    )
    grad_gate_w, grad_up_w, grad_down_w = (
        a + b for a, b in zip(weights0, weights1, strict=True)
    )

    small_w = jnp.concatenate([gain_second_w[:, None], router_w], axis=1)
    small_w = jnp.pad(small_w, ((0, 0), (0, -small_w.shape[1] % 128)))
    out_sum = lax.psum_scatter(
        jnp.concatenate([out_w, small_w], axis=1).astype(bf16),
        "dp",
        scatter_dimension=0,
        tiled=True,
    ).astype(f32)
    qkv_sum = lax.psum_scatter(
        jnp.concatenate([qkv_w, jnp.pad(gain_first_w[:, None], ((0, 0), (0, 127)))], axis=1).astype(
            bf16
        ),
        "dp",
        scatter_dimension=0,
        tiled=True,
    ).astype(f32)
    return (
        jnp.concatenate(outputs, axis=0),
        jnp.concatenate(token_grads_out, axis=0),
        qkv_sum[:, qkv_width],
        out_sum[:, model_width],
        qkv_sum[:, :query_width],
        qkv_sum[:, query_width : query_width + kv_width],
        qkv_sum[:, query_width + kv_width : qkv_width],
        out_sum[:, :model_width],
        out_sum[:, model_width + 1 : model_width + 1 + experts],
        grad_gate_w[None],
        grad_up_w[None],
        grad_down_w[None],
    )


def solution(mesh):
    return jax.shard_map(
        on_device,
        mesh=mesh,
        in_specs=(
            P("dp", None),
            P("dp", None),
            P("dp", None),
            P("dp", None),
            P("dp", None),
            P("dp"),
            P("dp"),
            P("dp", None),
            P("dp", None),
            P("dp", None),
            P("dp", None),
            P("dp", None),
            P("dp", None, None),
            P("dp", None, None),
            P("dp", None, None),
        ),
        out_specs=(
            P("dp", None),
            P("dp", None),
            P("dp"),
            P("dp"),
            P("dp", None),
            P("dp", None),
            P("dp", None),
            P("dp", None),
            P("dp", None),
            P("dp", None, None),
            P("dp", None, None),
            P("dp", None, None),
        ),
        check_vma=False,
    )
```

```python
import jax
import jax.numpy as jnp
from jax import lax
from jax.experimental import pallas as pl
from jax.experimental.pallas import tpu as pltpu
from jax.sharding import PartitionSpec as P

H = 24
KVH = 8
HD = 64


res_scale = 0.22
attn_scale = 0.015625
norm_eps = 1e-06
rope_base = 10000.0


def rotary_tables(length, head_size):
    half_size = head_size // 2
    frequency = rope_base ** (-(jnp.arange(half_size, dtype=jnp.float32) * 2.0) / head_size)
    angles = jnp.arange(length, dtype=jnp.float32)[:, None] * frequency[None, :]
    return (jnp.cos(angles)[:, None, :], jnp.sin(angles)[:, None, :])


LINES = 4


def norm_backward(grad_normed, source, recip, gain):
    scaled_grad = grad_normed * gain
    grad_source = recip * scaled_grad - source * (recip * recip * recip) * jnp.mean(
        scaled_grad * source, axis=1, keepdims=True
    )
    return (grad_source, jnp.sum(grad_normed * source * recip, axis=0))


def masked_gates(logits, routed):
    peak = jnp.max(jnp.where(routed, logits, -jnp.inf), axis=-2, keepdims=True)
    shifted = jnp.where(routed, jnp.exp(jnp.minimum(logits - peak, 0.0)), 0.0)
    return shifted / jnp.sum(shifted, axis=-2, keepdims=True)


def expert_kernel(
    rows_ref,
    blend_ref,
    gates_ref,
    gate_ref,
    up_ref,
    down_ref,
    grads_ref,
    scaled_ref,
    pairs_ref,
    gate_sum_ref,
    up_sum_ref,
    down_sum_ref,
):
    f32 = jnp.float32
    bf16 = jnp.bfloat16

    def product(left, right, left_axis, right_axis):
        return lax.dot_general(
            left, right, (((left_axis,), (right_axis,)), ((), ())), preferred_element_type=f32
        )

    @pl.when(pl.program_id(0) == 0)
    def _():
        gate_sum_ref[...] = jnp.zeros_like(gate_sum_ref)
        up_sum_ref[...] = jnp.zeros_like(up_sum_ref)
        down_sum_ref[...] = jnp.zeros_like(down_sum_ref)

    rows = rows_ref[...]
    gates = gates_ref[...]
    blend = blend_ref[...].astype(f32)
    gate_pre = product(rows, gate_ref[...], 1, 0)
    up_pre = product(rows, up_ref[...], 1, 0)
    logistic = 1.0 / (1.0 + jnp.exp(-gate_pre))
    silu = gate_pre * logistic
    hidden_act = (silu * up_pre).astype(bf16)
    produced = product(hidden_act, down_ref[...], 1, 0)
    pairs_ref[...] = jnp.sum(produced * blend, axis=1, keepdims=True)
    scaled_ref[...] = (gates * produced).astype(bf16)
    grad_produced = (gates * blend).astype(bf16)
    grad_inner = product(grad_produced, down_ref[...], 1, 1)
    grad_gate_pre = (
        grad_inner * up_pre * (logistic * (1.0 + gate_pre * (1.0 - logistic)))
    ).astype(bf16)
    grad_up_pre = (grad_inner * silu).astype(bf16)
    grads_ref[...] = (
        product(grad_gate_pre, gate_ref[...], 1, 1) + product(grad_up_pre, up_ref[...], 1, 1)
    ).astype(bf16)
    down_sum_ref[...] += product(hidden_act, grad_produced, 0, 0)
    gate_sum_ref[...] += product(rows, grad_gate_pre, 0, 0)
    up_sum_ref[...] += product(rows, grad_up_pre, 0, 0)


def run_experts(rows, blend, gates, gate_local, up_local, down_local):
    count, width = rows.shape
    ff_width = gate_local.shape[1]
    block = next(b for b in (384, 256, 128, count) if count % b == 0)
    f32 = jnp.float32
    wide = pl.BlockSpec((block, width), lambda i: (i, 0))
    thin = pl.BlockSpec((block, 1), lambda i: (i, 0))
    inner = pl.BlockSpec((width, ff_width), lambda i: (0, 0))
    outer = pl.BlockSpec((ff_width, width), lambda i: (0, 0))
    return pl.pallas_call(
        expert_kernel,
        grid=(count // block,),
        in_specs=[wide, wide, thin, inner, inner, outer],
        out_specs=[wide, wide, thin, inner, inner, outer],
        out_shape=[
            jax.ShapeDtypeStruct((count, width), rows.dtype),
            jax.ShapeDtypeStruct((count, width), rows.dtype),
            jax.ShapeDtypeStruct((count, 1), f32),
            jax.ShapeDtypeStruct((width, ff_width), f32),
            jax.ShapeDtypeStruct((width, ff_width), f32),
            jax.ShapeDtypeStruct((ff_width, width), f32),
        ],
        cost_estimate=pl.CostEstimate(flops=1000, bytes_accessed=1000, transcendentals=0),
        name="experts",
    )(rows, blend, gates, gate_local, up_local, down_local)


def build_kernel(slots_ref, *refs):
    out_ref = refs[-1]
    plane, lines, capacity, width = out_ref.shape
    for line in range(lines):
        slots = slots_ref[line]
        places = lax.broadcasted_iota(jnp.int32, (plane, capacity, slots.shape[1]), 1)
        picks = jnp.where(slots[:, None, :] == places, 1.0, 0.0)
        rows = jnp.dot(
            picks.reshape(plane * capacity, slots.shape[1]).astype(jnp.bfloat16),
            refs[line][...],
            preferred_element_type=jnp.float32,
        )
        out_ref[:, line] = rows.reshape(plane, capacity, width).astype(jnp.bfloat16)


def build_rows(slots, blocks, capacity):
    lines, plane, unused = slots.shape
    width = blocks[0].shape[1]
    return pl.pallas_call(
        build_kernel,
        out_shape=jax.ShapeDtypeStruct((plane, lines, capacity, width), blocks[0].dtype),
        cost_estimate=pl.CostEstimate(flops=1000, bytes_accessed=1000, transcendentals=0),
        name="build_rows",
    )(slots, *blocks)


def swap_halves(value):
    width = value.shape[1]
    half = HD // 2
    lanes = lax.broadcasted_iota(jnp.int32, value.shape, 1)
    return jnp.where(
        lanes % HD < half, pltpu.roll(value, width - half, 1), pltpu.roll(value, half, 1)
    )


def head_of(value, head):
    return value[:, head * HD : (head + 1) * HD]


def head_product(left, right, left_axis, right_axis):
    return lax.dot_general(
        left,
        right,
        (((left_axis,), (right_axis,)), ((), ())),
        preferred_element_type=jnp.float32,
    )


def probabilities(query, key, visible):
    scores = jnp.where(visible, attn_scale * head_product(query, key, 1, 1), -1e30)
    shifted = jnp.exp(scores - jnp.max(scores, axis=1, keepdims=True))
    return shifted / jnp.sum(shifted, axis=1, keepdims=True)


def attend_kernel(
    query_ref,
    key_ref,
    value_ref,
    cos_ref,
    sin_ref,
    own_ref,
    other_ref,
    query_out,
    key_out,
    value_out,
    mixture_out,
):
    bf16 = jnp.bfloat16
    key_width = key_ref.shape[1]
    queries = query_ref[...]
    keys = key_ref[...]
    cos_table = cos_ref[...]
    sin_table = sin_ref[...]
    queries = (queries * cos_table + swap_halves(queries) * sin_table).astype(bf16)
    keys = (
        keys * cos_table[:, :key_width] + swap_halves(keys) * sin_table[:, :key_width]
    ).astype(bf16)
    values = value_ref[...].astype(bf16)
    query_out[...] = queries
    key_out[...] = keys
    value_out[...] = values
    visible = other_ref[0] <= own_ref[...]
    mixed = []
    for head in range(queries.shape[1] // HD):
        shared = head // (H // KVH)
        probs = probabilities(head_of(queries, head), head_of(keys, shared), visible)
        mixed.append(head_product(probs.astype(bf16), head_of(values, shared), 1, 0))
    mixture_out[...] = jnp.concatenate(mixed, axis=1).astype(bf16)


def attend_back_kernel(
    query_ref,
    key_ref,
    value_ref,
    mixture_ref,
    cos_ref,
    sin_ref,
    own_ref,
    other_ref,
    query_out,
    key_out,
    value_out,
):
    bf16 = jnp.bfloat16
    key_width = key_ref.shape[1]
    queries = query_ref[...]
    keys = key_ref[...]
    values = value_ref[...]
    grad_mixture = mixture_ref[...]
    cos_table = cos_ref[...]
    sin_table = sin_ref[...]
    visible = other_ref[0] <= own_ref[...]
    grad_queries = []
    grad_keys = [0.0] * (key_width // HD)
    grad_values = [0.0] * (key_width // HD)
    for head in range(queries.shape[1] // HD):
        shared = head // (H // KVH)
        query, key = head_of(queries, head), head_of(keys, shared)
        grad_mix = head_of(grad_mixture, head)
        probs = probabilities(query, key, visible)
        grad_probs = head_product(grad_mix, head_of(values, shared), 1, 1)
        inner = jnp.sum(probs * grad_probs, axis=1, keepdims=True)
        grad_scores = (probs * (grad_probs - inner)).astype(bf16)
        grad_values[shared] += head_product(probs.astype(bf16), grad_mix, 0, 0)
        grad_keys[shared] += head_product(grad_scores, query, 0, 0)
        grad_queries.append(head_product(grad_scores, key, 1, 0))
    grad_query = attn_scale * jnp.concatenate(grad_queries, axis=1)
    grad_key = attn_scale * jnp.concatenate(grad_keys, axis=1)
    query_out[...] = (grad_query * cos_table - swap_halves(grad_query) * sin_table).astype(bf16)
    key_out[...] = (
        grad_key * cos_table[:, :key_width] - swap_halves(grad_key) * sin_table[:, :key_width]
    ).astype(bf16)
    value_out[...] = jnp.concatenate(grad_values, axis=1).astype(bf16)


def attention_specs(seq_len):
    query_block = 2 * (H // KVH) * HD
    key_block = 2 * HD
    wide = pl.BlockSpec((seq_len, query_block), lambda m, i: (m, i))
    thin = pl.BlockSpec((seq_len, key_block), lambda m, i: (m, i))
    table = pl.BlockSpec((seq_len, query_block), lambda m, i: (0, 0))
    own = pl.BlockSpec((seq_len, 1), lambda m, i: (m, 0))
    other = pl.BlockSpec((1, 1, seq_len), lambda m, i: (m, 0, 0))
    return wide, thin, table, own, other


def wide_tables(seq_len):
    cos_table, sin_table = rotary_tables(seq_len, HD)
    cos_table, sin_table = cos_table[:, 0], sin_table[:, 0]
    count = 2 * (H // KVH)
    return (
        jnp.tile(jnp.concatenate([cos_table, cos_table], axis=1), (1, count)),
        jnp.tile(jnp.concatenate([-sin_table, sin_table], axis=1), (1, count)),
    )


def run_attention(projected, tables, block_ids):
    micro_count, seq_len = block_ids.shape
    wide, thin, table, own, other = attention_specs(seq_len)
    rows = projected.shape[0]
    bf16 = jnp.bfloat16
    first_key = H * HD // (2 * HD)
    first_value = first_key + KVH // 2
    return pl.pallas_call(
        attend_kernel,
        grid=(micro_count, KVH // 2),
        in_specs=[
            wide,
            pl.BlockSpec((seq_len, 2 * HD), lambda m, i: (m, first_key + i)),
            pl.BlockSpec((seq_len, 2 * HD), lambda m, i: (m, first_value + i)),
            table,
            table,
            own,
            other,
        ],
        out_specs=[wide, thin, thin, wide],
        out_shape=[
            jax.ShapeDtypeStruct((rows, H * HD), bf16),
            jax.ShapeDtypeStruct((rows, KVH * HD), bf16),
            jax.ShapeDtypeStruct((rows, KVH * HD), bf16),
            jax.ShapeDtypeStruct((rows, H * HD), bf16),
        ],
        cost_estimate=pl.CostEstimate(flops=1000, bytes_accessed=1000, transcendentals=0),
        name="attention",
    )(
        projected,
        projected,
        projected,
        *tables,
        block_ids.reshape(-1, 1),
        block_ids.reshape(micro_count, 1, seq_len),
    )


def run_attention_back(queries, keys, values, grad_mixture, tables, block_ids, micro):
    micro_count, seq_len = block_ids.shape
    wide, thin, table, own, other = attention_specs(seq_len)
    bf16 = jnp.bfloat16

    def at(spec, index):
        return pl.BlockSpec(spec.block_shape, index)

    return pl.pallas_call(
        attend_back_kernel,
        grid=(1, KVH // 2),
        in_specs=[
            at(wide, lambda m, i: (micro, i)),
            at(thin, lambda m, i: (micro, i)),
            at(thin, lambda m, i: (micro, i)),
            wide,
            table,
            table,
            at(own, lambda m, i: (micro, 0)),
            at(other, lambda m, i: (micro, 0, 0)),
        ],
        out_specs=[wide, thin, thin],
        out_shape=[
            jax.ShapeDtypeStruct((seq_len, H * HD), bf16),
            jax.ShapeDtypeStruct((seq_len, KVH * HD), bf16),
            jax.ShapeDtypeStruct((seq_len, KVH * HD), bf16),
        ],
        cost_estimate=pl.CostEstimate(flops=1000, bytes_accessed=1000, transcendentals=0),
        name="attention_back",
    )(
        queries,
        keys,
        values,
        grad_mixture,
        *tables,
        block_ids.reshape(-1, 1),
        block_ids.reshape(micro_count, 1, seq_len),
    )


def on_device(
    hidden,
    cotangent,
    block_ids,
    routes,
    pair_rank,
    norm1_gain,
    norm2_gain,
    w_query,
    w_key,
    w_value,
    w_out,
    w_router,
    w_gate,
    w_up,
    w_down,
):
    micro_count, seq_len = block_ids.shape
    model_width = hidden.shape[1]
    top_count = routes.shape[1]
    devices = lax.axis_size("dp")
    experts = w_router.shape[1]
    plane = devices // LINES
    capacity = (9 * seq_len * top_count + 8 * experts - 1) // (8 * experts)
    query_width = w_query.shape[1]
    kv_width = w_key.shape[1]
    qkv_width = query_width + 2 * kv_width
    tables = wide_tables(seq_len)
    gate_local = w_gate[0]
    up_local = w_up[0]
    down_local = w_down[0]
    bf16 = jnp.bfloat16
    f32 = jnp.float32
    here = lax.axis_index("dp") // plane
    plane_groups = [[line * plane + i for i in range(plane)] for line in range(LINES)]

    def line_shift(step):
        return [
            (i, ((i // plane + step) % LINES) * plane + i % plane) for i in range(devices)
        ]

    def spread(block):
        return [block] + [
            lax.ppermute(block, "dp", line_shift(step)) for step in range(1, LINES)
        ]

    def give_back(blocks):
        return [blocks[0]] + [
            lax.ppermute(blocks[step], "dp", line_shift(-step)) for step in range(1, LINES)
        ]

    def exchange(block):
        return lax.all_to_all(
            block, "dp", split_axis=0, concat_axis=0, tiled=True, axis_index_groups=plane_groups
        )

    small = jnp.concatenate([norm1_gain[:, None], norm2_gain[:, None], w_router], axis=1)
    pad = -small.shape[1] % 128
    first = lax.all_gather(
        jnp.concatenate(
            [w_query, w_key, w_value, jnp.pad(small, ((0, 0), (0, pad)))], axis=1
        ),
        "dp",
        axis=0,
        tiled=True,
    )
    out_proj = lax.all_gather(w_out, "dp", axis=0, tiled=True)
    qkv_proj = first[:, :qkv_width]
    gain_first = first[:, qkv_width].astype(f32)
    gain_second = first[:, qkv_width + 1].astype(f32)
    router = first[:, qkv_width + 2 : qkv_width + 2 + experts]

    labels = jnp.arange(experts, dtype=jnp.int32)
    route_seq = routes.reshape(micro_count, seq_len, top_count)
    rank_seq = pair_rank.reshape(micro_count, seq_len, top_count)
    named = route_seq[:, None, :, :] == labels[None, :, None, None]
    routed = jnp.any(named, axis=3)
    rank_of = jnp.where(
        routed, jnp.sum(jnp.where(named, rank_seq[:, None], 0), axis=3), seq_len * top_count
    )
    ahead = jnp.sum((rank_of[:, :, :, None] < rank_of[:, :, None, :]).astype(jnp.int32), axis=2)
    slot_of = jnp.where(routed, ahead, -1)
    slot_blocks = jnp.stack(spread(slot_of))
    slots_here = lax.dynamic_slice_in_dim(slot_blocks, here * plane, plane, axis=2)
    places = jnp.arange(capacity, dtype=jnp.int32)
    picks = [
        (slots_here[:, micro, :, None, :] == places[None, None, :, None]).astype(bf16)
        for micro in range(micro_count)
    ]

    cotan_seq = cotangent.reshape(micro_count, seq_len, model_width)
    hidden_seq = hidden.reshape(micro_count, seq_len, model_width)

    def hold(value, *after):
        return lax.optimization_barrier((value, after))[0]

    def build(micro, blocks):
        if capacity % 8 == 0:
            rows = build_rows(slots_here[:, micro], blocks, capacity)
        else:
            rows = jnp.einsum(
                "ject,jtd->ejcd", picks[micro], jnp.stack(blocks), preferred_element_type=f32
            ).astype(bf16)
        return rows.reshape(plane, LINES * capacity, model_width)

    def sums_of(micro, arrived):
        sums = jnp.einsum(
            "ject,ejcd->jtd",
            picks[micro],
            arrived.reshape(plane, LINES, capacity, model_width),
            preferred_element_type=f32,
        ).astype(bf16)
        return give_back([sums[step] for step in range(LINES)])

    def total_of(parts):
        total = parts[0].astype(f32)
        for part in parts[1:]:
            total = total + part.astype(f32)
        return total

    def attend(tokens_in):
        recip_first = lax.rsqrt(jnp.mean(tokens_in * tokens_in, axis=1, keepdims=True) + norm_eps)
        normed_in = (tokens_in * recip_first * gain_first).astype(bf16)
        projected = jnp.dot(normed_in, qkv_proj, preferred_element_type=f32)
        queries, keys, values, mixture = run_attention(projected, tables, block_ids)
        return recip_first, normed_in, queries, keys, values, mixture

    def after_attention(mixture, tokens_in):
        attn_out = jnp.dot(mixture, out_proj, preferred_element_type=f32)
        residual = tokens_in + res_scale * attn_out
        recip_second = lax.rsqrt(jnp.mean(residual * residual, axis=1, keepdims=True) + norm_eps)
        normed_mid = (residual * recip_second * gain_second).astype(bf16)
        return residual, recip_second, normed_mid

    def gates_of(micro, blocks):
        logits = jnp.einsum("de,jtd->jet", router, jnp.stack(blocks), preferred_element_type=f32)
        gates = masked_gates(logits, slot_blocks[:, micro] >= 0)
        gates_here = lax.dynamic_slice_in_dim(gates, here * plane, plane, axis=1)
        slot_gates = jnp.sum(
            jnp.where(picks[micro] > 0, gates_here[:, :, None, :], 0.0), axis=3
        ).transpose(1, 0, 2)
        return gates[0], slot_gates.reshape(plane, LINES * capacity)

    def run_expert(mid, blend, gate_rows):
        grads, scaled, pair_grads, *weights = run_experts(
            mid.reshape(-1, model_width),
            blend.reshape(-1, model_width),
            gate_rows.reshape(-1, 1),
            gate_local,
            up_local,
            down_local,
        )
        return (
            grads.reshape(mid.shape),
            scaled.reshape(mid.shape),
            pair_grads.reshape(mid.shape[:2]),
            weights,
        )

    def pairs_home(pair_back):
        token_grads = [
            jnp.sum(
                jnp.where(
                    picks[m] > 0,
                    pair_back[:, m]
                    .reshape(plane, LINES, capacity)
                    .transpose(1, 0, 2)[:, :, :, None],
                    0.0,
                ),
                axis=2,
            )
            for m in range(micro_count)
        ]
        both = jnp.stack(token_grads, axis=1)
        return give_back([both[step] for step in range(LINES)])

    def attend_back(micro, grad_mid_sum, pair_blocks, gates):
        tokens_in = hidden_seq[micro]
        cotan_in = cotan_seq[micro]
        residual, recip_second, normed_mid = after[micro]
        first_recip, first_normed, mixed = (
            rows_of(part, micro) for part in (recip_first, normed_in, mixture)
        )
        pair_grads = jnp.zeros((experts, seq_len), f32)
        for step in range(LINES):
            pair_grads = lax.dynamic_update_slice_in_dim(
                pair_grads, pair_blocks[step], ((here + step) % LINES) * plane, axis=0
            )
        grad_logits = (
            gates * (pair_grads - jnp.sum(gates * pair_grads, axis=0, keepdims=True))
        ).astype(bf16)
        router_w = jnp.einsum(
            "td,et->de", normed_mid, grad_logits, preferred_element_type=f32
        )
        grad_mid = grad_mid_sum + jnp.einsum(
            "et,de->td", grad_logits, router, preferred_element_type=f32
        )
        grad_residual, grad_gain = norm_backward(grad_mid, residual, recip_second, gain_second)
        gain_second_w = grad_gain
        grad_residual = cotan_in + grad_residual
        grad_attn = (res_scale * grad_residual).astype(bf16)
        out_w = jnp.einsum("tc,td->cd", mixed, grad_attn, preferred_element_type=f32)
        grad_mixture = jnp.einsum(
            "td,cd->tc", grad_attn, out_proj, preferred_element_type=f32
        ).astype(bf16)
        grad_queries, grad_keys, grad_values = run_attention_back(
            queries, keys, values, grad_mixture, tables, block_ids, micro
        )
        grad_qkv = jnp.concatenate([grad_queries, grad_keys, grad_values], axis=1)
        qkv_w = jnp.einsum("td,tc->dc", first_normed, grad_qkv, preferred_element_type=f32)
        grad_normed = jnp.einsum("tc,dc->td", grad_qkv, qkv_proj, preferred_element_type=f32)
        grad_source, grad_gain = norm_backward(grad_normed, tokens_in, first_recip, gain_first)
        return (
            grad_residual + grad_source,
            out_w,
            qkv_w,
            grad_gain,
            gain_second_w,
            router_w,
        )

    blend_rows = [(res_scale * cotan_seq[m]).astype(bf16) for m in range(2)]
    blend_blocks = [
        spread(hold(blend_rows[0], slot_blocks)),
        spread(hold(blend_rows[1], first)),
    ]
    blend0 = build(0, blend_blocks[0])
    moved_blend0 = exchange(blend0)
    recip_first, normed_in, queries, keys, values, mixture = attend(hold(hidden, blend0))

    def rows_of(value, micro):
        return value[micro * seq_len : (micro + 1) * seq_len]

    blend1 = build(1, hold(blend_blocks[1], mixture))
    moved_blend1 = exchange(hold(blend1, moved_blend0))
    after = [after_attention(rows_of(mixture, m), hidden_seq[m]) for m in range(2)]
    blocks0 = spread(after[0][2])
    blocks1 = spread(after[1][2])
    moved_mid0 = exchange(hold(build(0, blocks0), moved_blend1))
    gates0, slot_gates0 = gates_of(0, blocks0)
    gates1, slot_gates1 = gates_of(1, blocks1)
    mid1 = build(1, blocks1)
    gate_rows = exchange(
        hold(jnp.stack([slot_gates0, slot_gates1], axis=1), moved_mid0, mid1)
    )
    moved_mid1 = exchange(hold(mid1, gate_rows))
    grads0, scaled0, pairs0, weights0 = run_expert(
        hold(moved_mid0, mid1), moved_blend0, gate_rows[:, 0]
    )
    moved_grads0 = exchange(hold(grads0, moved_mid1))
    grads1, scaled1, pairs1, weights1 = run_expert(moved_mid1, moved_blend1, gate_rows[:, 1])
    pair_back = exchange(hold(jnp.stack([pairs0, pairs1], axis=1), moved_grads0))
    moved_grads1 = exchange(hold(grads1, pair_back))
    pair_blocks = pairs_home(pair_back)
    back0 = sums_of(0, moved_grads0)
    moved_scaled0 = exchange(hold(scaled0, moved_grads1, back0))
    back1 = sums_of(1, moved_grads1)
    result0 = attend_back(
        0, hold(total_of(back0), back1[0]), [block[0] for block in pair_blocks], gates0
    )
    moved_scaled1 = exchange(hold(scaled1, moved_scaled0, back1[1], result0))
    blend_back0 = sums_of(0, hold(moved_scaled0, result0))
    result1 = attend_back(
        1,
        hold(total_of(back1), result0, blend_back0[0]),
        [block[1] for block in pair_blocks],
        gates1,
    )
    blend_back1 = sums_of(1, hold(moved_scaled1, result1))
    outputs = [
        after[0][0] + res_scale * total_of(blend_back0),
        after[1][0] + res_scale * total_of(blend_back1),
    ]
    token_grads_out = [result0[0], result1[0]]
    out_w, qkv_w, gain_first_w, gain_second_w, router_w = (
        a + b for a, b in zip(result0[1:], result1[1:], strict=True)
    )
    grad_gate_w, grad_up_w, grad_down_w = (
        a + b for a, b in zip(weights0, weights1, strict=True)
    )

    small_w = jnp.concatenate([gain_second_w[:, None], router_w], axis=1)
    small_w = jnp.pad(small_w, ((0, 0), (0, -small_w.shape[1] % 128)))
    out_sum = lax.psum_scatter(
        jnp.concatenate([out_w, small_w], axis=1).astype(bf16),
        "dp",
        scatter_dimension=0,
        tiled=True,
    ).astype(f32)
    qkv_sum = lax.psum_scatter(
        jnp.concatenate([qkv_w, jnp.pad(gain_first_w[:, None], ((0, 0), (0, 127)))], axis=1).astype(
            bf16
        ),
        "dp",
        scatter_dimension=0,
        tiled=True,
    ).astype(f32)
    return (
        jnp.concatenate(outputs, axis=0),
        jnp.concatenate(token_grads_out, axis=0),
        qkv_sum[:, qkv_width],
        out_sum[:, model_width],
        qkv_sum[:, :query_width],
        qkv_sum[:, query_width : query_width + kv_width],
        qkv_sum[:, query_width + kv_width : qkv_width],
        out_sum[:, :model_width],
        out_sum[:, model_width + 1 : model_width + 1 + experts],
        grad_gate_w[None],
        grad_up_w[None],
        grad_down_w[None],
    )


def solution(mesh):
    return jax.shard_map(
        on_device,
        mesh=mesh,
        in_specs=(
            P("dp", None),
            P("dp", None),
            P("dp", None),
            P("dp", None),
            P("dp", None),
            P("dp"),
            P("dp"),
            P("dp", None),
            P("dp", None),
            P("dp", None),
            P("dp", None),
            P("dp", None),
            P("dp", None, None),
            P("dp", None, None),
            P("dp", None, None),
        ),
        out_specs=(
            P("dp", None),
            P("dp", None),
            P("dp"),
            P("dp"),
            P("dp", None),
            P("dp", None),
            P("dp", None),
            P("dp", None),
            P("dp", None),
            P("dp", None, None),
            P("dp", None, None),
            P("dp", None, None),
        ),
        check_vma=False,
    )
```

```python
import jax
import jax.numpy as jnp
from jax import lax
from jax.experimental import pallas as pl
from jax.experimental.pallas import tpu as pltpu
from jax.sharding import PartitionSpec as P

H = 24
KVH = 8
HD = 64


res_scale = 0.22
attn_scale = 0.015625
norm_eps = 1e-06
rope_base = 10000.0


def rotary_tables(length, head_size):
    half_size = head_size // 2
    frequency = rope_base ** (-(jnp.arange(half_size, dtype=jnp.float32) * 2.0) / head_size)
    angles = jnp.arange(length, dtype=jnp.float32)[:, None] * frequency[None, :]
    return (jnp.cos(angles)[:, None, :], jnp.sin(angles)[:, None, :])


LINES = 4


def norm_backward(grad_normed, source, recip, gain):
    scaled_grad = grad_normed * gain
    grad_source = recip * scaled_grad - source * (recip * recip * recip) * jnp.mean(
        scaled_grad * source, axis=1, keepdims=True
    )
    return (grad_source, jnp.sum(grad_normed * source * recip, axis=0))


def masked_gates(logits, routed):
    peak = jnp.max(jnp.where(routed, logits, -jnp.inf), axis=-2, keepdims=True)
    shifted = jnp.where(routed, jnp.exp(jnp.minimum(logits - peak, 0.0)), 0.0)
    return shifted / jnp.sum(shifted, axis=-2, keepdims=True)


def expert_kernel(
    rows_ref,
    blend_ref,
    gates_ref,
    gate_ref,
    up_ref,
    down_ref,
    grads_ref,
    scaled_ref,
    pairs_ref,
    gate_sum_ref,
    up_sum_ref,
    down_sum_ref,
):
    f32 = jnp.float32
    bf16 = jnp.bfloat16

    def product(left, right, left_axis, right_axis):
        return lax.dot_general(
            left, right, (((left_axis,), (right_axis,)), ((), ())), preferred_element_type=f32
        )

    @pl.when(pl.program_id(0) == 0)
    def _():
        gate_sum_ref[...] = jnp.zeros_like(gate_sum_ref)
        up_sum_ref[...] = jnp.zeros_like(up_sum_ref)
        down_sum_ref[...] = jnp.zeros_like(down_sum_ref)

    rows = rows_ref[...]
    gates = gates_ref[...]
    blend = blend_ref[...].astype(f32)
    gate_pre = product(rows, gate_ref[...], 1, 0)
    up_pre = product(rows, up_ref[...], 1, 0)
    logistic = 1.0 / (1.0 + jnp.exp(-gate_pre))
    silu = gate_pre * logistic
    hidden_act = (silu * up_pre).astype(bf16)
    produced = product(hidden_act, down_ref[...], 1, 0)
    pairs_ref[...] = jnp.sum(produced * blend, axis=1, keepdims=True)
    scaled_ref[...] = (gates * produced).astype(bf16)
    grad_produced = (gates * blend).astype(bf16)
    grad_inner = product(grad_produced, down_ref[...], 1, 1)
    grad_gate_pre = (
        grad_inner * up_pre * (logistic * (1.0 + gate_pre * (1.0 - logistic)))
    ).astype(bf16)
    grad_up_pre = (grad_inner * silu).astype(bf16)
    grads_ref[...] = (
        product(grad_gate_pre, gate_ref[...], 1, 1) + product(grad_up_pre, up_ref[...], 1, 1)
    ).astype(bf16)
    down_sum_ref[...] += product(hidden_act, grad_produced, 0, 0)
    gate_sum_ref[...] += product(rows, grad_gate_pre, 0, 0)
    up_sum_ref[...] += product(rows, grad_up_pre, 0, 0)


def run_experts(rows, blend, gates, gate_local, up_local, down_local):
    count, width = rows.shape
    ff_width = gate_local.shape[1]
    block = next(b for b in (384, 256, 128, count) if count % b == 0)
    f32 = jnp.float32
    wide = pl.BlockSpec((block, width), lambda i: (i, 0))
    thin = pl.BlockSpec((block, 1), lambda i: (i, 0))
    inner = pl.BlockSpec((width, ff_width), lambda i: (0, 0))
    outer = pl.BlockSpec((ff_width, width), lambda i: (0, 0))
    return pl.pallas_call(
        expert_kernel,
        grid=(count // block,),
        in_specs=[wide, wide, thin, inner, inner, outer],
        out_specs=[wide, wide, thin, inner, inner, outer],
        out_shape=[
            jax.ShapeDtypeStruct((count, width), rows.dtype),
            jax.ShapeDtypeStruct((count, width), rows.dtype),
            jax.ShapeDtypeStruct((count, 1), f32),
            jax.ShapeDtypeStruct((width, ff_width), f32),
            jax.ShapeDtypeStruct((width, ff_width), f32),
            jax.ShapeDtypeStruct((ff_width, width), f32),
        ],
        cost_estimate=pl.CostEstimate(flops=1000, bytes_accessed=1000, transcendentals=0),
        name="experts",
    )(rows, blend, gates, gate_local, up_local, down_local)


def build_kernel(slots_ref, *refs):
    out_ref = refs[-1]
    plane, lines, capacity, width = out_ref.shape
    for line in range(lines):
        slots = slots_ref[line]
        places = lax.broadcasted_iota(jnp.int32, (plane, capacity, slots.shape[1]), 1)
        picks = jnp.where(slots[:, None, :] == places, 1.0, 0.0)
        rows = jnp.dot(
            picks.reshape(plane * capacity, slots.shape[1]).astype(jnp.bfloat16),
            refs[line][...],
            preferred_element_type=jnp.float32,
        )
        out_ref[:, line] = rows.reshape(plane, capacity, width).astype(jnp.bfloat16)


def build_rows(slots, blocks, capacity):
    lines, plane, unused = slots.shape
    width = blocks[0].shape[1]
    return pl.pallas_call(
        build_kernel,
        out_shape=jax.ShapeDtypeStruct((plane, lines, capacity, width), blocks[0].dtype),
        cost_estimate=pl.CostEstimate(flops=1000, bytes_accessed=1000, transcendentals=0),
        name="build_rows",
    )(slots, *blocks)


def swap_halves(value):
    width = value.shape[1]
    half = HD // 2
    lanes = lax.broadcasted_iota(jnp.int32, value.shape, 1)
    return jnp.where(
        lanes % HD < half, pltpu.roll(value, width - half, 1), pltpu.roll(value, half, 1)
    )


def head_of(value, head):
    return value[:, head * HD : (head + 1) * HD]


def head_product(left, right, left_axis, right_axis):
    return lax.dot_general(
        left,
        right,
        (((left_axis,), (right_axis,)), ((), ())),
        preferred_element_type=jnp.float32,
    )


def probabilities(query, key, visible):
    scores = jnp.where(visible, attn_scale * head_product(query, key, 1, 1), -1e30)
    shifted = jnp.exp(scores - jnp.max(scores, axis=1, keepdims=True))
    return shifted / jnp.sum(shifted, axis=1, keepdims=True)


def attend_kernel(
    query_ref,
    key_ref,
    value_ref,
    cos_ref,
    sin_ref,
    own_ref,
    other_ref,
    query_out,
    key_out,
    value_out,
    mixture_out,
):
    bf16 = jnp.bfloat16
    key_width = key_ref.shape[1]
    queries = query_ref[...]
    keys = key_ref[...]
    cos_table = cos_ref[...]
    sin_table = sin_ref[...]
    queries = (queries * cos_table + swap_halves(queries) * sin_table).astype(bf16)
    keys = (
        keys * cos_table[:, :key_width] + swap_halves(keys) * sin_table[:, :key_width]
    ).astype(bf16)
    values = value_ref[...].astype(bf16)
    query_out[...] = queries
    key_out[...] = keys
    value_out[...] = values
    visible = other_ref[0] <= own_ref[...]
    mixed = []
    for head in range(queries.shape[1] // HD):
        shared = head // (H // KVH)
        probs = probabilities(head_of(queries, head), head_of(keys, shared), visible)
        mixed.append(head_product(probs.astype(bf16), head_of(values, shared), 1, 0))
    mixture_out[...] = jnp.concatenate(mixed, axis=1).astype(bf16)


def attend_back_kernel(
    query_ref,
    key_ref,
    value_ref,
    mixture_ref,
    cos_ref,
    sin_ref,
    own_ref,
    other_ref,
    query_out,
    key_out,
    value_out,
):
    bf16 = jnp.bfloat16
    key_width = key_ref.shape[1]
    queries = query_ref[...]
    keys = key_ref[...]
    values = value_ref[...]
    grad_mixture = mixture_ref[...]
    cos_table = cos_ref[...]
    sin_table = sin_ref[...]
    visible = other_ref[0] <= own_ref[...]
    grad_queries = []
    grad_keys = [0.0] * (key_width // HD)
    grad_values = [0.0] * (key_width // HD)
    for head in range(queries.shape[1] // HD):
        shared = head // (H // KVH)
        query, key = head_of(queries, head), head_of(keys, shared)
        grad_mix = head_of(grad_mixture, head)
        probs = probabilities(query, key, visible)
        grad_probs = head_product(grad_mix, head_of(values, shared), 1, 1)
        inner = jnp.sum(probs * grad_probs, axis=1, keepdims=True)
        grad_scores = (probs * (grad_probs - inner)).astype(bf16)
        grad_values[shared] += head_product(probs.astype(bf16), grad_mix, 0, 0)
        grad_keys[shared] += head_product(grad_scores, query, 0, 0)
        grad_queries.append(head_product(grad_scores, key, 1, 0))
    grad_query = attn_scale * jnp.concatenate(grad_queries, axis=1)
    grad_key = attn_scale * jnp.concatenate(grad_keys, axis=1)
    query_out[...] = (grad_query * cos_table - swap_halves(grad_query) * sin_table).astype(bf16)
    key_out[...] = (
        grad_key * cos_table[:, :key_width] - swap_halves(grad_key) * sin_table[:, :key_width]
    ).astype(bf16)
    value_out[...] = jnp.concatenate(grad_values, axis=1).astype(bf16)


def attention_specs(seq_len):
    query_block = 2 * (H // KVH) * HD
    key_block = 2 * HD
    wide = pl.BlockSpec((seq_len, query_block), lambda m, i: (m, i))
    thin = pl.BlockSpec((seq_len, key_block), lambda m, i: (m, i))
    table = pl.BlockSpec((seq_len, query_block), lambda m, i: (0, 0))
    own = pl.BlockSpec((seq_len, 1), lambda m, i: (m, 0))
    other = pl.BlockSpec((1, 1, seq_len), lambda m, i: (m, 0, 0))
    return wide, thin, table, own, other


def wide_tables(seq_len):
    cos_table, sin_table = rotary_tables(seq_len, HD)
    cos_table, sin_table = cos_table[:, 0], sin_table[:, 0]
    count = 2 * (H // KVH)
    return (
        jnp.tile(jnp.concatenate([cos_table, cos_table], axis=1), (1, count)),
        jnp.tile(jnp.concatenate([-sin_table, sin_table], axis=1), (1, count)),
    )


def run_attention(projected, tables, block_ids):
    micro_count, seq_len = block_ids.shape
    wide, thin, table, own, other = attention_specs(seq_len)
    rows = projected.shape[0]
    bf16 = jnp.bfloat16
    first_key = H * HD // (2 * HD)
    first_value = first_key + KVH // 2
    return pl.pallas_call(
        attend_kernel,
        grid=(micro_count, KVH // 2),
        in_specs=[
            wide,
            pl.BlockSpec((seq_len, 2 * HD), lambda m, i: (m, first_key + i)),
            pl.BlockSpec((seq_len, 2 * HD), lambda m, i: (m, first_value + i)),
            table,
            table,
            own,
            other,
        ],
        out_specs=[wide, thin, thin, wide],
        out_shape=[
            jax.ShapeDtypeStruct((rows, H * HD), bf16),
            jax.ShapeDtypeStruct((rows, KVH * HD), bf16),
            jax.ShapeDtypeStruct((rows, KVH * HD), bf16),
            jax.ShapeDtypeStruct((rows, H * HD), bf16),
        ],
        cost_estimate=pl.CostEstimate(flops=1000, bytes_accessed=1000, transcendentals=0),
        name="attention",
    )(
        projected,
        projected,
        projected,
        *tables,
        block_ids.reshape(-1, 1),
        block_ids.reshape(micro_count, 1, seq_len),
    )


def run_attention_back(queries, keys, values, grad_mixture, tables, block_ids, micro):
    micro_count, seq_len = block_ids.shape
    wide, thin, table, own, other = attention_specs(seq_len)
    bf16 = jnp.bfloat16

    def at(spec, index):
        return pl.BlockSpec(spec.block_shape, index)

    return pl.pallas_call(
        attend_back_kernel,
        grid=(1, KVH // 2),
        in_specs=[
            at(wide, lambda m, i: (micro, i)),
            at(thin, lambda m, i: (micro, i)),
            at(thin, lambda m, i: (micro, i)),
            wide,
            table,
            table,
            at(own, lambda m, i: (micro, 0)),
            at(other, lambda m, i: (micro, 0, 0)),
        ],
        out_specs=[wide, thin, thin],
        out_shape=[
            jax.ShapeDtypeStruct((seq_len, H * HD), bf16),
            jax.ShapeDtypeStruct((seq_len, KVH * HD), bf16),
            jax.ShapeDtypeStruct((seq_len, KVH * HD), bf16),
        ],
        cost_estimate=pl.CostEstimate(flops=1000, bytes_accessed=1000, transcendentals=0),
        name="attention_back",
    )(
        queries,
        keys,
        values,
        grad_mixture,
        *tables,
        block_ids.reshape(-1, 1),
        block_ids.reshape(micro_count, 1, seq_len),
    )


def weights_kernel(left_ref, right_ref, *refs):
    out_ref = refs[-1]
    width = right_ref.shape[1]
    product = head_product(left_ref[...], right_ref[...], 0, 0)
    if len(refs) == 1:
        out_ref[...] = product.astype(out_ref.dtype)
    else:
        out_ref[:, :width] = product.astype(out_ref.dtype)
        out_ref[:, width:] = refs[0][...].astype(out_ref.dtype)


def run_weights(left, right, extra, dtype):
    tokens, height = left.shape
    width = right.shape[1]
    block = 256 if height % 256 == 0 else height
    in_specs = [
        pl.BlockSpec((tokens, block), lambda i: (0, i)),
        pl.BlockSpec((tokens, width), lambda i: (0, 0)),
    ]
    operands = [left, right]
    if extra is not None:
        in_specs.append(pl.BlockSpec((block, extra.shape[1]), lambda i: (i, 0)))
        operands.append(extra)
        width += extra.shape[1]
    return pl.pallas_call(
        weights_kernel,
        grid=(height // block,),
        in_specs=in_specs,
        out_specs=pl.BlockSpec((block, width), lambda i: (i, 0)),
        out_shape=jax.ShapeDtypeStruct((height, width), dtype),
        cost_estimate=pl.CostEstimate(flops=1000, bytes_accessed=1000, transcendentals=0),
        name="weights",
    )(*operands)


def on_device(
    hidden,
    cotangent,
    block_ids,
    routes,
    pair_rank,
    norm1_gain,
    norm2_gain,
    w_query,
    w_key,
    w_value,
    w_out,
    w_router,
    w_gate,
    w_up,
    w_down,
):
    micro_count, seq_len = block_ids.shape
    model_width = hidden.shape[1]
    top_count = routes.shape[1]
    devices = lax.axis_size("dp")
    experts = w_router.shape[1]
    plane = devices // LINES
    capacity = (9 * seq_len * top_count + 8 * experts - 1) // (8 * experts)
    query_width = w_query.shape[1]
    kv_width = w_key.shape[1]
    qkv_width = query_width + 2 * kv_width
    tables = wide_tables(seq_len)
    gate_local = w_gate[0]
    up_local = w_up[0]
    down_local = w_down[0]
    bf16 = jnp.bfloat16
    f32 = jnp.float32
    here = lax.axis_index("dp") // plane
    plane_groups = [[line * plane + i for i in range(plane)] for line in range(LINES)]

    def line_shift(step):
        return [
            (i, ((i // plane + step) % LINES) * plane + i % plane) for i in range(devices)
        ]

    def spread(block):
        return [block] + [
            lax.ppermute(block, "dp", line_shift(step)) for step in range(1, LINES)
        ]

    def give_back(blocks):
        return [blocks[0]] + [
            lax.ppermute(blocks[step], "dp", line_shift(-step)) for step in range(1, LINES)
        ]

    def hold(value, *after):
        return lax.optimization_barrier((value, after))[0]

    def reduce_rows(value, early, late):
        if plane != 8:
            return lax.psum_scatter(
                value.astype(bf16), "dp", scatter_dimension=0, tiled=True
            ).astype(f32)
        index = lax.axis_index("dp")
        rows = value.shape[0] // devices
        half = value.shape[1] // 256 * 128

        def fold(block, axis, bit):
            side = (index // bit) % 2
            kept = lax.dynamic_index_in_dim(block, side, axis, keepdims=False)
            sent = lax.dynamic_index_in_dim(block, 1 - side, axis, keepdims=False)
            other = lax.ppermute(
                sent.astype(bf16), "dp", [(i, i ^ bit) for i in range(devices)]
            )
            return kept + other.astype(f32)

        block = fold(value.reshape(LINES, 2, 2, 2, rows, value.shape[1]), 3, 1)
        left, right = block[..., :half], block[..., half:]
        left, right = fold(left, 1, 4), fold(right, 2, 2)
        left, right = hold((left, right), early)
        left, right = fold(left, 1, 2), fold(right, 1, 4)
        block = hold(jnp.concatenate([left, right], axis=2), late)
        total = lax.dynamic_index_in_dim(block, here, 0, keepdims=False)
        for step in range(1, LINES):
            sent = lax.dynamic_index_in_dim(block, (here + step) % LINES, 0, keepdims=False)
            total = total + lax.ppermute(sent.astype(bf16), "dp", line_shift(step)).astype(f32)
        return total


    def exchange(block):
        return lax.all_to_all(
            block, "dp", split_axis=0, concat_axis=0, tiled=True, axis_index_groups=plane_groups
        )

    small = jnp.concatenate([norm1_gain[:, None], norm2_gain[:, None], w_router], axis=1)
    pad = -small.shape[1] % 128
    shared = lax.all_gather(
        jnp.concatenate(
            [w_query, w_key, w_value, w_out, jnp.pad(small, ((0, 0), (0, pad)))], axis=1
        ),
        "dp",
        axis=0,
        tiled=True,
    )
    qkv_proj = shared[:, :qkv_width]
    first_small = qkv_width + model_width
    out_proj = shared[:, qkv_width:first_small]
    gain_first = shared[:, first_small].astype(f32)
    gain_second = shared[:, first_small + 1].astype(f32)
    router = shared[:, first_small + 2 : first_small + 2 + experts]

    labels = jnp.arange(experts, dtype=jnp.int32)
    route_seq = routes.reshape(micro_count, seq_len, top_count)
    rank_seq = pair_rank.reshape(micro_count, seq_len, top_count)
    named = route_seq[:, None, :, :] == labels[None, :, None, None]
    routed = jnp.any(named, axis=3)
    rank_of = jnp.where(
        routed, jnp.sum(jnp.where(named, rank_seq[:, None], 0), axis=3), seq_len * top_count
    )
    ahead = jnp.sum((rank_of[:, :, :, None] < rank_of[:, :, None, :]).astype(jnp.int32), axis=2)
    slot_of = jnp.where(routed, ahead, -1)
    slot_blocks = jnp.stack(spread(slot_of))
    slots_here = lax.dynamic_slice_in_dim(slot_blocks, here * plane, plane, axis=2)
    places = jnp.arange(capacity, dtype=jnp.int32)
    picks = [
        (slots_here[:, micro, :, None, :] == places[None, None, :, None]).astype(bf16)
        for micro in range(micro_count)
    ]

    cotan_seq = cotangent.reshape(micro_count, seq_len, model_width)
    hidden_seq = hidden.reshape(micro_count, seq_len, model_width)

    def build(micro, blocks):
        if capacity % 8 == 0:
            rows = build_rows(slots_here[:, micro], blocks, capacity)
        else:
            rows = jnp.einsum(
                "ject,jtd->ejcd", picks[micro], jnp.stack(blocks), preferred_element_type=f32
            ).astype(bf16)
        return rows.reshape(plane, LINES * capacity, model_width)

    def sums_of(micro, arrived):
        sums = jnp.einsum(
            "ject,ejcd->jtd",
            picks[micro],
            arrived.reshape(plane, LINES, capacity, model_width),
            preferred_element_type=f32,
        ).astype(bf16)
        return give_back([sums[step] for step in range(LINES)])

    def total_of(parts):
        total = parts[0].astype(f32)
        for part in parts[1:]:
            total = total + part.astype(f32)
        return total

    def attend(tokens_in):
        recip_first = lax.rsqrt(jnp.mean(tokens_in * tokens_in, axis=1, keepdims=True) + norm_eps)
        normed_in = (tokens_in * recip_first * gain_first).astype(bf16)
        projected = jnp.dot(normed_in, qkv_proj, preferred_element_type=f32)
        queries, keys, values, mixture = run_attention(projected, tables, block_ids)
        return recip_first, normed_in, queries, keys, values, mixture

    def after_attention(mixture, tokens_in):
        attn_out = jnp.dot(mixture, out_proj, preferred_element_type=f32)
        residual = tokens_in + res_scale * attn_out
        recip_second = lax.rsqrt(jnp.mean(residual * residual, axis=1, keepdims=True) + norm_eps)
        normed_mid = (residual * recip_second * gain_second).astype(bf16)
        return residual, recip_second, normed_mid

    def gates_of(micro, blocks):
        logits = jnp.einsum("de,jtd->jet", router, jnp.stack(blocks), preferred_element_type=f32)
        gates = masked_gates(logits, slot_blocks[:, micro] >= 0)
        gates_here = lax.dynamic_slice_in_dim(gates, here * plane, plane, axis=1)
        slot_gates = jnp.sum(
            jnp.where(picks[micro] > 0, gates_here[:, :, None, :], 0.0), axis=3
        ).transpose(1, 0, 2)
        return gates[0], slot_gates.reshape(plane, LINES * capacity)

    def run_expert(mid, blend, gate_rows):
        grads, scaled, pair_grads, *weights = run_experts(
            mid.reshape(-1, model_width),
            blend.reshape(-1, model_width),
            gate_rows.reshape(-1, 1),
            gate_local,
            up_local,
            down_local,
        )
        return (
            grads.reshape(mid.shape),
            scaled.reshape(mid.shape),
            pair_grads.reshape(mid.shape[:2]),
            weights,
        )

    def pairs_home(pair_back):
        token_grads = [
            jnp.sum(
                jnp.where(
                    picks[m] > 0,
                    pair_back[:, m]
                    .reshape(plane, LINES, capacity)
                    .transpose(1, 0, 2)[:, :, :, None],
                    0.0,
                ),
                axis=2,
            )
            for m in range(micro_count)
        ]
        both = jnp.stack(token_grads, axis=1)
        return give_back([both[step] for step in range(LINES)])

    def attend_back(micro, grad_mid_sum, pair_blocks, gates, before):
        tokens_in = hidden_seq[micro]
        cotan_in = cotan_seq[micro]
        residual, recip_second, normed_mid = after[micro]
        first_recip = rows_of(recip_first, micro)
        pair_grads = jnp.zeros((experts, seq_len), f32)
        for step in range(LINES):
            pair_grads = lax.dynamic_update_slice_in_dim(
                pair_grads, pair_blocks[step], ((here + step) % LINES) * plane, axis=0
            )
        grad_logits = (
            gates * (pair_grads - jnp.sum(gates * pair_grads, axis=0, keepdims=True))
        ).astype(bf16)
        grad_mid = grad_mid_sum + jnp.einsum(
            "et,de->td", grad_logits, router, preferred_element_type=f32
        )
        grad_residual, grad_gain = norm_backward(grad_mid, residual, recip_second, gain_second)
        gain_second_w = grad_gain
        grad_residual = cotan_in + grad_residual
        grad_attn = (res_scale * grad_residual).astype(bf16)
        grad_mixture = jnp.einsum(
            "td,cd->tc", grad_attn, out_proj, preferred_element_type=f32
        ).astype(bf16)
        grad_queries, grad_keys, grad_values = run_attention_back(
            queries, keys, values, hold(grad_mixture, before(grad_attn)), tables, block_ids, micro
        )
        grad_qkv = jnp.concatenate([grad_queries, grad_keys, grad_values], axis=1)
        grad_normed = jnp.einsum("tc,dc->td", grad_qkv, qkv_proj, preferred_element_type=f32)
        grad_source, grad_gain = norm_backward(grad_normed, tokens_in, first_recip, gain_first)
        return (
            grad_residual + grad_source,
            grad_attn,
            grad_qkv,
            grad_logits,
            gain_second_w,
            grad_gain,
        )

    blend_rows = [(res_scale * cotan_seq[m]).astype(bf16) for m in range(2)]
    blend_blocks = [
        spread(hold(blend_rows[0], slot_blocks)),
        spread(hold(blend_rows[1], slot_blocks)),
    ]
    blend0 = build(0, blend_blocks[0])
    moved_blend0 = exchange(blend0)
    recip_first, normed_in, queries, keys, values, mixture = attend(hold(hidden, blend0, blend_blocks[1]))

    def rows_of(value, micro):
        return value[micro * seq_len : (micro + 1) * seq_len]

    blend1 = build(1, hold(blend_blocks[1], mixture))
    moved_blend1 = exchange(hold(blend1, moved_blend0))
    after = [after_attention(rows_of(mixture, m), hidden_seq[m]) for m in range(2)]
    blocks0 = spread(after[0][2])
    blocks1 = spread(after[1][2])
    moved_mid0 = exchange(hold(build(0, blocks0), moved_blend1))
    gates0, slot_gates0 = gates_of(0, blocks0)
    gates1, slot_gates1 = gates_of(1, blocks1)
    mid1 = build(1, blocks1)
    gate_rows = exchange(
        hold(jnp.stack([slot_gates0, slot_gates1], axis=1), moved_mid0, mid1)
    )
    moved_mid1 = exchange(hold(mid1, gate_rows))
    grads0, scaled0, pairs0, weights0 = run_expert(
        hold(moved_mid0, mid1), moved_blend0, gate_rows[:, 0]
    )
    moved_grads0 = exchange(hold(grads0, moved_mid1))
    grads1, scaled1, pairs1, weights1 = run_expert(moved_mid1, moved_blend1, gate_rows[:, 1])
    pair_back = exchange(hold(jnp.stack([pairs0, pairs1], axis=1), moved_grads0))
    moved_grads1 = exchange(hold(grads1, pair_back))
    pair_blocks = pairs_home(pair_back)
    back0 = sums_of(0, moved_grads0)
    moved_scaled0 = exchange(hold(scaled0, moved_grads1, back0))
    back1 = sums_of(1, moved_grads1)
    result0 = attend_back(
        0,
        hold(total_of(back0), back1[0]),
        [block[0] for block in pair_blocks],
        gates0,
        lambda grad_attn: (),
    )
    moved_scaled1 = exchange(hold(scaled1, moved_scaled0, back1[1], result0))
    blend_back0 = sums_of(0, hold(moved_scaled0, result0))

    def out_grads(grad_attn):
        return run_weights(
            mixture, jnp.concatenate([result0[1], grad_attn], axis=0), None, bf16
        )

    result1 = attend_back(
        1,
        hold(total_of(back1), result0),
        [block[1] for block in pair_blocks],
        gates1,
        lambda grad_attn: (moved_scaled0, blend_back0[0], out_grads(grad_attn)),
    )
    blend_back1 = sums_of(1, hold(moved_scaled1, result1))
    outputs = [
        after[0][0] + res_scale * total_of(blend_back0),
        after[1][0] + res_scale * total_of(blend_back1),
    ]
    token_grads_out = [result0[0], result1[0]]
    grad_qkv = jnp.concatenate([result0[2], result1[2]], axis=0)
    out_w = out_grads(result1[1])
    router_w = jnp.einsum(
        "td,et->de",
        jnp.concatenate([after[0][2], after[1][2]], axis=0),
        jnp.concatenate([result0[3], result1[3]], axis=1),
        preferred_element_type=f32,
    )
    gain_second_w = result0[4] + result1[4]
    gain_first_w = result0[5] + result1[5]
    grad_gate_w, grad_up_w, grad_down_w = (
        a + b for a, b in zip(weights0, weights1, strict=True)
    )

    small_w = jnp.concatenate([gain_first_w[:, None], gain_second_w[:, None], router_w], axis=1)
    small_w = jnp.pad(small_w, ((0, 0), (0, -small_w.shape[1] % 128)))
    out_sum = lax.psum_scatter(out_w, "dp", scatter_dimension=0, tiled=True)
    qkv_sum = reduce_rows(
        run_weights(normed_in, grad_qkv, small_w, f32),
        (blend_back0, moved_scaled1),
        blend_back1[0],
    )
    out_sum = hold(out_sum, qkv_sum).astype(f32)
    return (
        jnp.concatenate(outputs, axis=0),
        jnp.concatenate(token_grads_out, axis=0),
        qkv_sum[:, qkv_width],
        qkv_sum[:, qkv_width + 1],
        qkv_sum[:, :query_width],
        qkv_sum[:, query_width : query_width + kv_width],
        qkv_sum[:, query_width + kv_width : qkv_width],
        out_sum,
        qkv_sum[:, qkv_width + 2 : qkv_width + 2 + experts],
        grad_gate_w[None],
        grad_up_w[None],
        grad_down_w[None],
    )


def solution(mesh):
    return jax.shard_map(
        on_device,
        mesh=mesh,
        in_specs=(
            P("dp", None),
            P("dp", None),
            P("dp", None),
            P("dp", None),
            P("dp", None),
            P("dp"),
            P("dp"),
            P("dp", None),
            P("dp", None),
            P("dp", None),
            P("dp", None),
            P("dp", None),
            P("dp", None, None),
            P("dp", None, None),
            P("dp", None, None),
        ),
        out_specs=(
            P("dp", None),
            P("dp", None),
            P("dp"),
            P("dp"),
            P("dp", None),
            P("dp", None),
            P("dp", None),
            P("dp", None),
            P("dp", None),
            P("dp", None, None),
            P("dp", None, None),
            P("dp", None, None),
        ),
        check_vma=False,
    )
```

```python
import jax
import jax.numpy as jnp
from jax import lax
from jax.experimental import pallas as pl
from jax.experimental.pallas import tpu as pltpu
from jax.sharding import PartitionSpec as P

H = 24
KVH = 8
HD = 64


res_scale = 0.22
attn_scale = 0.015625
norm_eps = 1e-06
rope_base = 10000.0


def rotary_tables(length, head_size):
    half_size = head_size // 2
    frequency = rope_base ** (-(jnp.arange(half_size, dtype=jnp.float32) * 2.0) / head_size)
    angles = jnp.arange(length, dtype=jnp.float32)[:, None] * frequency[None, :]
    return (jnp.cos(angles)[:, None, :], jnp.sin(angles)[:, None, :])


LINES = 4


def norm_backward(grad_normed, source, recip, gain):
    scaled_grad = grad_normed * gain
    grad_source = recip * scaled_grad - source * (recip * recip * recip) * jnp.mean(
        scaled_grad * source, axis=1, keepdims=True
    )
    return (grad_source, jnp.sum(grad_normed * source * recip, axis=0))


def masked_gates(logits, routed):
    peak = jnp.max(jnp.where(routed, logits, -jnp.inf), axis=-2, keepdims=True)
    shifted = jnp.where(routed, jnp.exp(jnp.minimum(logits - peak, 0.0)), 0.0)
    return shifted / jnp.sum(shifted, axis=-2, keepdims=True)


def expert_kernel(
    rows_ref,
    blend_ref,
    gates_ref,
    gate_ref,
    up_ref,
    down_ref,
    grads_ref,
    scaled_ref,
    pairs_ref,
    gate_sum_ref,
    up_sum_ref,
    down_sum_ref,
):
    f32 = jnp.float32
    bf16 = jnp.bfloat16

    def product(left, right, left_axis, right_axis):
        return lax.dot_general(
            left, right, (((left_axis,), (right_axis,)), ((), ())), preferred_element_type=f32
        )

    @pl.when(pl.program_id(0) == 0)
    def _():
        gate_sum_ref[...] = jnp.zeros_like(gate_sum_ref)
        up_sum_ref[...] = jnp.zeros_like(up_sum_ref)
        down_sum_ref[...] = jnp.zeros_like(down_sum_ref)

    rows = rows_ref[...]
    gates = gates_ref[...]
    blend = blend_ref[...].astype(f32)
    gate_pre = product(rows, gate_ref[...], 1, 0)
    up_pre = product(rows, up_ref[...], 1, 0)
    logistic = 1.0 / (1.0 + jnp.exp(-gate_pre))
    silu = gate_pre * logistic
    hidden_act = (silu * up_pre).astype(bf16)
    produced = product(hidden_act, down_ref[...], 1, 0)
    pairs_ref[...] = jnp.sum(produced * blend, axis=1, keepdims=True)
    scaled_ref[...] = (gates * produced).astype(bf16)
    grad_produced = (gates * blend).astype(bf16)
    grad_inner = product(grad_produced, down_ref[...], 1, 1)
    grad_gate_pre = (
        grad_inner * up_pre * (logistic * (1.0 + gate_pre * (1.0 - logistic)))
    ).astype(bf16)
    grad_up_pre = (grad_inner * silu).astype(bf16)
    grads_ref[...] = (
        product(grad_gate_pre, gate_ref[...], 1, 1) + product(grad_up_pre, up_ref[...], 1, 1)
    ).astype(bf16)
    down_sum_ref[...] += product(hidden_act, grad_produced, 0, 0)
    gate_sum_ref[...] += product(rows, grad_gate_pre, 0, 0)
    up_sum_ref[...] += product(rows, grad_up_pre, 0, 0)


def run_experts(rows, blend, gates, gate_local, up_local, down_local):
    count, width = rows.shape
    ff_width = gate_local.shape[1]
    block = next(b for b in (384, 256, 128, count) if count % b == 0)
    f32 = jnp.float32
    wide = pl.BlockSpec((block, width), lambda i: (i, 0))
    thin = pl.BlockSpec((block, 1), lambda i: (i, 0))
    inner = pl.BlockSpec((width, ff_width), lambda i: (0, 0))
    outer = pl.BlockSpec((ff_width, width), lambda i: (0, 0))
    return pl.pallas_call(
        expert_kernel,
        grid=(count // block,),
        in_specs=[wide, wide, thin, inner, inner, outer],
        out_specs=[wide, wide, thin, inner, inner, outer],
        out_shape=[
            jax.ShapeDtypeStruct((count, width), rows.dtype),
            jax.ShapeDtypeStruct((count, width), rows.dtype),
            jax.ShapeDtypeStruct((count, 1), f32),
            jax.ShapeDtypeStruct((width, ff_width), f32),
            jax.ShapeDtypeStruct((width, ff_width), f32),
            jax.ShapeDtypeStruct((ff_width, width), f32),
        ],
        cost_estimate=pl.CostEstimate(flops=1000, bytes_accessed=1000, transcendentals=0),
        name="experts",
    )(rows, blend, gates, gate_local, up_local, down_local)


def build_kernel(slots_ref, *refs):
    out_ref = refs[-1]
    plane, lines, capacity, width = out_ref.shape
    for line in range(lines):
        slots = slots_ref[line]
        places = lax.broadcasted_iota(jnp.int32, (plane, capacity, slots.shape[1]), 1)
        picks = jnp.where(slots[:, None, :] == places, 1.0, 0.0)
        rows = jnp.dot(
            picks.reshape(plane * capacity, slots.shape[1]).astype(jnp.bfloat16),
            refs[line][...],
            preferred_element_type=jnp.float32,
        )
        out_ref[:, line] = rows.reshape(plane, capacity, width).astype(jnp.bfloat16)


def build_rows(slots, blocks, capacity):
    lines, plane, unused = slots.shape
    width = blocks[0].shape[1]
    return pl.pallas_call(
        build_kernel,
        out_shape=jax.ShapeDtypeStruct((plane, lines, capacity, width), blocks[0].dtype),
        cost_estimate=pl.CostEstimate(flops=1000, bytes_accessed=1000, transcendentals=0),
        name="build_rows",
    )(slots, *blocks)


def swap_halves(value):
    width = value.shape[1]
    half = HD // 2
    lanes = lax.broadcasted_iota(jnp.int32, value.shape, 1)
    return jnp.where(
        lanes % HD < half, pltpu.roll(value, width - half, 1), pltpu.roll(value, half, 1)
    )


def head_of(value, head):
    return value[:, head * HD : (head + 1) * HD]


def head_product(left, right, left_axis, right_axis):
    return lax.dot_general(
        left,
        right,
        (((left_axis,), (right_axis,)), ((), ())),
        preferred_element_type=jnp.float32,
    )


def probabilities(query, key, visible):
    scores = jnp.where(visible, attn_scale * head_product(query, key, 1, 1), -1e30)
    shifted = jnp.exp(scores - jnp.max(scores, axis=1, keepdims=True))
    return shifted / jnp.sum(shifted, axis=1, keepdims=True)


def attend_kernel(
    query_ref,
    key_ref,
    value_ref,
    cos_ref,
    sin_ref,
    own_ref,
    other_ref,
    query_out,
    key_out,
    value_out,
    mixture_out,
):
    bf16 = jnp.bfloat16
    key_width = key_ref.shape[1]
    queries = query_ref[...]
    keys = key_ref[...]
    cos_table = cos_ref[...]
    sin_table = sin_ref[...]
    queries = (queries * cos_table + swap_halves(queries) * sin_table).astype(bf16)
    keys = (
        keys * cos_table[:, :key_width] + swap_halves(keys) * sin_table[:, :key_width]
    ).astype(bf16)
    values = value_ref[...].astype(bf16)
    query_out[...] = queries
    key_out[...] = keys
    value_out[...] = values
    visible = other_ref[0] <= own_ref[...]
    mixed = []
    for head in range(queries.shape[1] // HD):
        shared = head // (H // KVH)
        probs = probabilities(head_of(queries, head), head_of(keys, shared), visible)
        mixed.append(head_product(probs.astype(bf16), head_of(values, shared), 1, 0))
    mixture_out[...] = jnp.concatenate(mixed, axis=1).astype(bf16)


def attend_back_kernel(
    query_ref,
    key_ref,
    value_ref,
    mixture_ref,
    cos_ref,
    sin_ref,
    own_ref,
    other_ref,
    query_out,
    key_out,
    value_out,
):
    bf16 = jnp.bfloat16
    key_width = key_ref.shape[1]
    queries = query_ref[...]
    keys = key_ref[...]
    values = value_ref[...]
    grad_mixture = mixture_ref[...]
    cos_table = cos_ref[...]
    sin_table = sin_ref[...]
    visible = other_ref[0] <= own_ref[...]
    grad_queries = []
    grad_keys = [0.0] * (key_width // HD)
    grad_values = [0.0] * (key_width // HD)
    for head in range(queries.shape[1] // HD):
        shared = head // (H // KVH)
        query, key = head_of(queries, head), head_of(keys, shared)
        grad_mix = head_of(grad_mixture, head)
        probs = probabilities(query, key, visible)
        grad_probs = head_product(grad_mix, head_of(values, shared), 1, 1)
        inner = jnp.sum(probs * grad_probs, axis=1, keepdims=True)
        grad_scores = (probs * (grad_probs - inner)).astype(bf16)
        grad_values[shared] += head_product(probs.astype(bf16), grad_mix, 0, 0)
        grad_keys[shared] += head_product(grad_scores, query, 0, 0)
        grad_queries.append(head_product(grad_scores, key, 1, 0))
    grad_query = attn_scale * jnp.concatenate(grad_queries, axis=1)
    grad_key = attn_scale * jnp.concatenate(grad_keys, axis=1)
    query_out[...] = (grad_query * cos_table - swap_halves(grad_query) * sin_table).astype(bf16)
    key_out[...] = (
        grad_key * cos_table[:, :key_width] - swap_halves(grad_key) * sin_table[:, :key_width]
    ).astype(bf16)
    value_out[...] = jnp.concatenate(grad_values, axis=1).astype(bf16)


def attention_specs(seq_len):
    query_block = 2 * (H // KVH) * HD
    key_block = 2 * HD
    wide = pl.BlockSpec((seq_len, query_block), lambda m, i: (m, i))
    thin = pl.BlockSpec((seq_len, key_block), lambda m, i: (m, i))
    table = pl.BlockSpec((seq_len, query_block), lambda m, i: (0, 0))
    own = pl.BlockSpec((seq_len, 1), lambda m, i: (m, 0))
    other = pl.BlockSpec((1, 1, seq_len), lambda m, i: (m, 0, 0))
    return wide, thin, table, own, other


def wide_tables(seq_len):
    cos_table, sin_table = rotary_tables(seq_len, HD)
    cos_table, sin_table = cos_table[:, 0], sin_table[:, 0]
    count = 2 * (H // KVH)
    return (
        jnp.tile(jnp.concatenate([cos_table, cos_table], axis=1), (1, count)),
        jnp.tile(jnp.concatenate([-sin_table, sin_table], axis=1), (1, count)),
    )


def run_attention(projected, tables, block_ids):
    micro_count, seq_len = block_ids.shape
    wide, thin, table, own, other = attention_specs(seq_len)
    rows = projected.shape[0]
    bf16 = jnp.bfloat16
    first_key = H * HD // (2 * HD)
    first_value = first_key + KVH // 2
    return pl.pallas_call(
        attend_kernel,
        grid=(micro_count, KVH // 2),
        in_specs=[
            wide,
            pl.BlockSpec((seq_len, 2 * HD), lambda m, i: (m, first_key + i)),
            pl.BlockSpec((seq_len, 2 * HD), lambda m, i: (m, first_value + i)),
            table,
            table,
            own,
            other,
        ],
        out_specs=[wide, thin, thin, wide],
        out_shape=[
            jax.ShapeDtypeStruct((rows, H * HD), bf16),
            jax.ShapeDtypeStruct((rows, KVH * HD), bf16),
            jax.ShapeDtypeStruct((rows, KVH * HD), bf16),
            jax.ShapeDtypeStruct((rows, H * HD), bf16),
        ],
        cost_estimate=pl.CostEstimate(flops=1000, bytes_accessed=1000, transcendentals=0),
        name="attention",
    )(
        projected,
        projected,
        projected,
        *tables,
        block_ids.reshape(-1, 1),
        block_ids.reshape(micro_count, 1, seq_len),
    )


def run_attention_back(queries, keys, values, grad_mixture, tables, block_ids, micro):
    micro_count, seq_len = block_ids.shape
    wide, thin, table, own, other = attention_specs(seq_len)
    bf16 = jnp.bfloat16

    def at(spec, index):
        return pl.BlockSpec(spec.block_shape, index)

    return pl.pallas_call(
        attend_back_kernel,
        grid=(1, KVH // 2),
        in_specs=[
            at(wide, lambda m, i: (micro, i)),
            at(thin, lambda m, i: (micro, i)),
            at(thin, lambda m, i: (micro, i)),
            wide,
            table,
            table,
            at(own, lambda m, i: (micro, 0)),
            at(other, lambda m, i: (micro, 0, 0)),
        ],
        out_specs=[wide, thin, thin],
        out_shape=[
            jax.ShapeDtypeStruct((seq_len, H * HD), bf16),
            jax.ShapeDtypeStruct((seq_len, KVH * HD), bf16),
            jax.ShapeDtypeStruct((seq_len, KVH * HD), bf16),
        ],
        cost_estimate=pl.CostEstimate(flops=1000, bytes_accessed=1000, transcendentals=0),
        name="attention_back",
    )(
        queries,
        keys,
        values,
        grad_mixture,
        *tables,
        block_ids.reshape(-1, 1),
        block_ids.reshape(micro_count, 1, seq_len),
    )


def weights_kernel(left_ref, right_ref, *refs):
    out_ref = refs[-1]
    width = right_ref.shape[1]
    product = head_product(left_ref[...], right_ref[...], 0, 0)
    if len(refs) == 1:
        out_ref[...] = product.astype(out_ref.dtype)
    else:
        out_ref[:, :width] = product.astype(out_ref.dtype)
        out_ref[:, width:] = refs[0][...].astype(out_ref.dtype)


def run_weights(left, right, extra, dtype):
    tokens, height = left.shape
    width = right.shape[1]
    block = 256 if height % 256 == 0 else height
    in_specs = [
        pl.BlockSpec((tokens, block), lambda i: (0, i)),
        pl.BlockSpec((tokens, width), lambda i: (0, 0)),
    ]
    operands = [left, right]
    if extra is not None:
        in_specs.append(pl.BlockSpec((block, extra.shape[1]), lambda i: (i, 0)))
        operands.append(extra)
        width += extra.shape[1]
    return pl.pallas_call(
        weights_kernel,
        grid=(height // block,),
        in_specs=in_specs,
        out_specs=pl.BlockSpec((block, width), lambda i: (i, 0)),
        out_shape=jax.ShapeDtypeStruct((height, width), dtype),
        cost_estimate=pl.CostEstimate(flops=1000, bytes_accessed=1000, transcendentals=0),
        name="weights",
    )(*operands)


def on_device(
    hidden,
    cotangent,
    block_ids,
    routes,
    pair_rank,
    norm1_gain,
    norm2_gain,
    w_query,
    w_key,
    w_value,
    w_out,
    w_router,
    w_gate,
    w_up,
    w_down,
):
    micro_count, seq_len = block_ids.shape
    model_width = hidden.shape[1]
    top_count = routes.shape[1]
    devices = lax.axis_size("dp")
    experts = w_router.shape[1]
    plane = devices // LINES
    capacity = (9 * seq_len * top_count + 8 * experts - 1) // (8 * experts)
    query_width = w_query.shape[1]
    kv_width = w_key.shape[1]
    qkv_width = query_width + 2 * kv_width
    tables = wide_tables(seq_len)
    gate_local = w_gate[0]
    up_local = w_up[0]
    down_local = w_down[0]
    bf16 = jnp.bfloat16
    f32 = jnp.float32
    here = lax.axis_index("dp") // plane
    plane_groups = [[line * plane + i for i in range(plane)] for line in range(LINES)]

    def line_shift(step):
        return [
            (i, ((i // plane + step) % LINES) * plane + i % plane) for i in range(devices)
        ]

    def spread(block):
        return [block] + [
            lax.ppermute(block, "dp", line_shift(step)) for step in range(1, LINES)
        ]

    def give_back(blocks):
        return [blocks[0]] + [
            lax.ppermute(blocks[step], "dp", line_shift(-step)) for step in range(1, LINES)
        ]

    def hold(value, *after):
        return lax.optimization_barrier((value, after))[0]

    def reduce_rows(value, early, late):
        if plane != 8:
            return lax.psum_scatter(
                value.astype(bf16), "dp", scatter_dimension=0, tiled=True
            ).astype(f32)
        index = lax.axis_index("dp")
        rows = value.shape[0] // devices
        half = value.shape[1] // 256 * 128

        def fold(block, axis, bit):
            side = (index // bit) % 2
            kept = lax.dynamic_index_in_dim(block, side, axis, keepdims=False)
            sent = lax.dynamic_index_in_dim(block, 1 - side, axis, keepdims=False)
            other = lax.ppermute(
                sent.astype(bf16), "dp", [(i, i ^ bit) for i in range(devices)]
            )
            return kept + other.astype(f32)

        block = fold(value.reshape(LINES, 2, 2, 2, rows, value.shape[1]), 3, 1)
        left, right = block[..., :half], block[..., half:]
        left, right = fold(left, 1, 4), fold(right, 2, 2)
        left, right = hold((left, right), early)
        left, right = fold(left, 1, 2), fold(right, 1, 4)
        block = hold(jnp.concatenate([left, right], axis=2), late)
        total = lax.dynamic_index_in_dim(block, here, 0, keepdims=False)
        for step in range(1, LINES):
            sent = lax.dynamic_index_in_dim(block, (here + step) % LINES, 0, keepdims=False)
            total = total + lax.ppermute(sent.astype(bf16), "dp", line_shift(step)).astype(f32)
        return total


    def exchange(block):
        return lax.all_to_all(
            block, "dp", split_axis=0, concat_axis=0, tiled=True, axis_index_groups=plane_groups
        )

    small = jnp.concatenate([norm1_gain[:, None], norm2_gain[:, None], w_router], axis=1)
    pad = -small.shape[1] % 128
    shared = lax.all_gather(
        jnp.concatenate(
            [w_query, w_key, w_value, w_out, jnp.pad(small, ((0, 0), (0, pad)))], axis=1
        ),
        "dp",
        axis=0,
        tiled=True,
    )
    qkv_proj = shared[:, :qkv_width]
    first_small = qkv_width + model_width
    out_proj = shared[:, qkv_width:first_small]
    gain_first = shared[:, first_small].astype(f32)
    gain_second = shared[:, first_small + 1].astype(f32)
    router = shared[:, first_small + 2 : first_small + 2 + experts]

    labels = jnp.arange(experts, dtype=jnp.int32)
    route_seq = routes.reshape(micro_count, seq_len, top_count)
    rank_seq = pair_rank.reshape(micro_count, seq_len, top_count)
    named = route_seq[:, None, :, :] == labels[None, :, None, None]
    routed = jnp.any(named, axis=3)
    rank_of = jnp.where(
        routed, jnp.sum(jnp.where(named, rank_seq[:, None], 0), axis=3), seq_len * top_count
    )
    ahead = jnp.sum((rank_of[:, :, :, None] < rank_of[:, :, None, :]).astype(jnp.int32), axis=2)
    slot_of = jnp.where(routed, ahead, -1)
    slot_blocks = jnp.stack(spread(slot_of))
    slots_here = lax.dynamic_slice_in_dim(slot_blocks, here * plane, plane, axis=2)
    places = jnp.arange(capacity, dtype=jnp.int32)
    picks = [
        (slots_here[:, micro, :, None, :] == places[None, None, :, None]).astype(bf16)
        for micro in range(micro_count)
    ]

    cotan_seq = cotangent.reshape(micro_count, seq_len, model_width)
    hidden_seq = hidden.reshape(micro_count, seq_len, model_width)

    def build(micro, blocks):
        if capacity % 8 == 0:
            rows = build_rows(slots_here[:, micro], blocks, capacity)
        else:
            rows = jnp.einsum(
                "ject,jtd->ejcd", picks[micro], jnp.stack(blocks), preferred_element_type=f32
            ).astype(bf16)
        return rows.reshape(plane, LINES * capacity, model_width)

    def sums_of(micro, arrived):
        sums = jnp.einsum(
            "ject,ejcd->jtd",
            picks[micro],
            arrived.reshape(plane, LINES, capacity, model_width),
            preferred_element_type=f32,
        ).astype(bf16)
        return give_back([sums[step] for step in range(LINES)])

    def total_of(parts):
        total = parts[0].astype(f32)
        for part in parts[1:]:
            total = total + part.astype(f32)
        return total

    def attend(tokens_in):
        recip_first = lax.rsqrt(jnp.mean(tokens_in * tokens_in, axis=1, keepdims=True) + norm_eps)
        normed_in = (tokens_in * recip_first * gain_first).astype(bf16)
        projected = jnp.dot(normed_in, qkv_proj, preferred_element_type=f32)
        queries, keys, values, mixture = run_attention(projected, tables, block_ids)
        return recip_first, normed_in, queries, keys, values, mixture

    def after_attention(mixture, tokens_in):
        attn_out = jnp.dot(mixture, out_proj, preferred_element_type=f32)
        residual = tokens_in + res_scale * attn_out
        recip_second = lax.rsqrt(jnp.mean(residual * residual, axis=1, keepdims=True) + norm_eps)
        normed_mid = (residual * recip_second * gain_second).astype(bf16)
        return residual, recip_second, normed_mid

    def gates_of(micro, blocks):
        logits = jnp.einsum("de,jtd->jet", router, jnp.stack(blocks), preferred_element_type=f32)
        gates = masked_gates(logits, slot_blocks[:, micro] >= 0)
        gates_here = lax.dynamic_slice_in_dim(gates, here * plane, plane, axis=1)
        slot_gates = jnp.sum(
            jnp.where(picks[micro] > 0, gates_here[:, :, None, :], 0.0), axis=3
        ).transpose(1, 0, 2)
        return gates[0], slot_gates.reshape(plane, LINES * capacity)

    def run_expert(mid, blend, gate_rows):
        grads, scaled, pair_grads, *weights = run_experts(
            mid.reshape(-1, model_width),
            blend.reshape(-1, model_width),
            gate_rows.reshape(-1, 1),
            gate_local,
            up_local,
            down_local,
        )
        return (
            grads.reshape(mid.shape),
            scaled.reshape(mid.shape),
            pair_grads.reshape(mid.shape[:2]),
            weights,
        )

    def pairs_home(pair_back):
        token_grads = [
            jnp.sum(
                jnp.where(
                    picks[m] > 0,
                    pair_back[:, m]
                    .reshape(plane, LINES, capacity)
                    .transpose(1, 0, 2)[:, :, :, None],
                    0.0,
                ),
                axis=2,
            )
            for m in range(micro_count)
        ]
        both = jnp.stack(token_grads, axis=1)
        return give_back([both[step] for step in range(LINES)])

    def attend_back(micro, grad_mid_sum, pair_blocks, gates, before, then):
        tokens_in = hidden_seq[micro]
        cotan_in = cotan_seq[micro]
        residual, recip_second, normed_mid = after[micro]
        first_recip = rows_of(recip_first, micro)
        pair_grads = jnp.zeros((experts, seq_len), f32)
        for step in range(LINES):
            pair_grads = lax.dynamic_update_slice_in_dim(
                pair_grads, pair_blocks[step], ((here + step) % LINES) * plane, axis=0
            )
        grad_logits = (
            gates * (pair_grads - jnp.sum(gates * pair_grads, axis=0, keepdims=True))
        ).astype(bf16)
        grad_mid = grad_mid_sum + jnp.einsum(
            "et,de->td", grad_logits, router, preferred_element_type=f32
        )
        grad_residual, grad_gain = norm_backward(grad_mid, residual, recip_second, gain_second)
        gain_second_w = grad_gain
        grad_residual = cotan_in + grad_residual
        grad_attn = (res_scale * grad_residual).astype(bf16)
        grad_mixture = jnp.einsum(
            "td,cd->tc", grad_attn, out_proj, preferred_element_type=f32
        ).astype(bf16)
        grad_queries, grad_keys, grad_values = run_attention_back(
            queries, keys, values, hold(grad_mixture, before(grad_attn)), tables, block_ids, micro
        )
        grad_qkv = hold(jnp.concatenate([grad_queries, grad_keys, grad_values], axis=1), then)
        grad_normed = jnp.einsum("tc,dc->td", grad_qkv, qkv_proj, preferred_element_type=f32)
        grad_source, grad_gain = norm_backward(grad_normed, tokens_in, first_recip, gain_first)
        return (
            grad_residual + grad_source,
            grad_attn,
            grad_qkv,
            grad_logits,
            gain_second_w,
            grad_gain,
        )

    blend_rows = [(res_scale * cotan_seq[m]).astype(bf16) for m in range(2)]
    blend_blocks = [
        spread(hold(blend_rows[0], slot_blocks)),
        spread(hold(blend_rows[1], slot_blocks)),
    ]
    blend0 = build(0, blend_blocks[0])
    moved_blend0 = exchange(blend0)
    recip_first, normed_in, queries, keys, values, mixture = attend(hold(hidden, blend0, blend_blocks[1]))

    def rows_of(value, micro):
        return value[micro * seq_len : (micro + 1) * seq_len]

    blend1 = build(1, hold(blend_blocks[1], mixture))
    moved_blend1 = exchange(hold(blend1, moved_blend0))
    after = [after_attention(rows_of(mixture, m), hidden_seq[m]) for m in range(2)]
    blocks0 = spread(after[0][2])
    blocks1 = spread(after[1][2])
    moved_mid0 = exchange(hold(build(0, blocks0), moved_blend1))
    gates0, slot_gates0 = gates_of(0, blocks0)
    gates1, slot_gates1 = gates_of(1, blocks1)
    mid1 = build(1, blocks1)
    gate_rows = exchange(
        hold(jnp.stack([slot_gates0, slot_gates1], axis=1), moved_mid0, mid1)
    )
    moved_mid1 = exchange(hold(mid1, gate_rows))
    grads0, scaled0, pairs0, weights0 = run_expert(
        hold(moved_mid0, mid1), moved_blend0, gate_rows[:, 0]
    )
    moved_grads0 = exchange(hold(grads0, moved_mid1))
    grads1, scaled1, pairs1, weights1 = run_expert(moved_mid1, moved_blend1, gate_rows[:, 1])
    pair_back = exchange(hold(jnp.stack([pairs0, pairs1], axis=1), moved_grads0))
    moved_grads1 = exchange(hold(grads1, pair_back))
    pair_blocks = pairs_home(pair_back)
    back0 = sums_of(0, moved_grads0)
    moved_scaled0 = exchange(hold(scaled0, moved_grads1))
    back1 = sums_of(1, moved_grads1)
    result0 = attend_back(
        0,
        hold(total_of(back0), back1[0]),
        [block[0] for block in pair_blocks],
        gates0,
        lambda grad_attn: (moved_grads1, back1[0]),
        (),
    )
    moved_scaled1 = exchange(hold(scaled1, moved_scaled0, back1[1], result0))
    blend_back0 = sums_of(0, hold(moved_scaled0, result0))

    def out_grads(grad_attn):
        return run_weights(
            mixture, jnp.concatenate([result0[1], grad_attn], axis=0), None, bf16
        )

    result1 = attend_back(
        1,
        hold(total_of(back1), result0),
        [block[1] for block in pair_blocks],
        gates1,
        lambda grad_attn: (moved_scaled0, blend_back0[0], out_grads(grad_attn)),
        blend_back0,
    )
    blend_back1 = sums_of(1, hold(moved_scaled1, result1))
    outputs = [
        after[0][0] + res_scale * total_of(blend_back0),
        after[1][0] + res_scale * total_of(blend_back1),
    ]
    token_grads_out = [result0[0], result1[0]]
    grad_qkv = jnp.concatenate([result0[2], result1[2]], axis=0)
    out_w = out_grads(result1[1])
    router_w = jnp.einsum(
        "td,et->de",
        jnp.concatenate([after[0][2], after[1][2]], axis=0),
        jnp.concatenate([result0[3], result1[3]], axis=1),
        preferred_element_type=f32,
    )
    gain_second_w = result0[4] + result1[4]
    gain_first_w = result0[5] + result1[5]
    grad_gate_w, grad_up_w, grad_down_w = (
        a + b for a, b in zip(weights0, weights1, strict=True)
    )

    small_w = jnp.concatenate([gain_first_w[:, None], gain_second_w[:, None], router_w], axis=1)
    small_w = jnp.pad(small_w, ((0, 0), (0, -small_w.shape[1] % 128)))
    out_sum = lax.psum_scatter(out_w, "dp", scatter_dimension=0, tiled=True)
    qkv_sum = reduce_rows(
        run_weights(normed_in, hold(grad_qkv, moved_scaled1), small_w, f32),
        blend_back0,
        blend_back1[0],
    )
    out_sum = hold(out_sum, qkv_sum).astype(f32)
    return (
        jnp.concatenate(outputs, axis=0),
        jnp.concatenate(token_grads_out, axis=0),
        qkv_sum[:, qkv_width],
        qkv_sum[:, qkv_width + 1],
        qkv_sum[:, :query_width],
        qkv_sum[:, query_width : query_width + kv_width],
        qkv_sum[:, query_width + kv_width : qkv_width],
        out_sum,
        qkv_sum[:, qkv_width + 2 : qkv_width + 2 + experts],
        grad_gate_w[None],
        grad_up_w[None],
        grad_down_w[None],
    )


def solution(mesh):
    return jax.shard_map(
        on_device,
        mesh=mesh,
        in_specs=(
            P("dp", None),
            P("dp", None),
            P("dp", None),
            P("dp", None),
            P("dp", None),
            P("dp"),
            P("dp"),
            P("dp", None),
            P("dp", None),
            P("dp", None),
            P("dp", None),
            P("dp", None),
            P("dp", None, None),
            P("dp", None, None),
            P("dp", None, None),
        ),
        out_specs=(
            P("dp", None),
            P("dp", None),
            P("dp"),
            P("dp"),
            P("dp", None),
            P("dp", None),
            P("dp", None),
            P("dp", None),
            P("dp", None),
            P("dp", None, None),
            P("dp", None, None),
            P("dp", None, None),
        ),
        check_vma=False,
    )
```

```python
import jax
import jax.numpy as jnp
from jax import lax
from jax.experimental import pallas as pl
from jax.experimental.pallas import tpu as pltpu
from jax.sharding import PartitionSpec as P

H = 24
KVH = 8
HD = 64


res_scale = 0.22
attn_scale = 0.015625
norm_eps = 1e-06
rope_base = 10000.0


def rotary_tables(length, head_size):
    half_size = head_size // 2
    frequency = rope_base ** (-(jnp.arange(half_size, dtype=jnp.float32) * 2.0) / head_size)
    angles = jnp.arange(length, dtype=jnp.float32)[:, None] * frequency[None, :]
    return (jnp.cos(angles)[:, None, :], jnp.sin(angles)[:, None, :])


LINES = 4


def masked_gates(logits, routed):
    peak = jnp.max(jnp.where(routed, logits, -jnp.inf), axis=-2, keepdims=True)
    shifted = jnp.where(routed, jnp.exp(jnp.minimum(logits - peak, 0.0)), 0.0)
    return shifted / jnp.sum(shifted, axis=-2, keepdims=True)


def expert_kernel(
    rows_ref,
    blend_ref,
    gates_ref,
    gate_ref,
    up_ref,
    down_ref,
    grads_ref,
    scaled_ref,
    pairs_ref,
    gate_sum_ref,
    up_sum_ref,
    down_sum_ref,
):
    f32 = jnp.float32
    bf16 = jnp.bfloat16

    def product(left, right, left_axis, right_axis):
        return lax.dot_general(
            left, right, (((left_axis,), (right_axis,)), ((), ())), preferred_element_type=f32
        )

    @pl.when(pl.program_id(0) == 0)
    def _():
        gate_sum_ref[...] = jnp.zeros_like(gate_sum_ref)
        up_sum_ref[...] = jnp.zeros_like(up_sum_ref)
        down_sum_ref[...] = jnp.zeros_like(down_sum_ref)

    rows = rows_ref[...]
    gates = gates_ref[...]
    blend = blend_ref[...].astype(f32)
    gate_pre = product(rows, gate_ref[...], 1, 0)
    up_pre = product(rows, up_ref[...], 1, 0)
    logistic = 1.0 / (1.0 + jnp.exp(-gate_pre))
    silu = gate_pre * logistic
    hidden_act = (silu * up_pre).astype(bf16)
    produced = product(hidden_act, down_ref[...], 1, 0)
    pairs_ref[...] = jnp.sum(produced * blend, axis=1, keepdims=True)
    scaled_ref[...] = (gates * produced).astype(bf16)
    grad_produced = (gates * blend).astype(bf16)
    grad_inner = product(grad_produced, down_ref[...], 1, 1)
    grad_gate_pre = (
        grad_inner * up_pre * (logistic * (1.0 + gate_pre * (1.0 - logistic)))
    ).astype(bf16)
    grad_up_pre = (grad_inner * silu).astype(bf16)
    grads_ref[...] = (
        product(grad_gate_pre, gate_ref[...], 1, 1) + product(grad_up_pre, up_ref[...], 1, 1)
    ).astype(bf16)
    down_sum_ref[...] += product(hidden_act, grad_produced, 0, 0)
    gate_sum_ref[...] += product(rows, grad_gate_pre, 0, 0)
    up_sum_ref[...] += product(rows, grad_up_pre, 0, 0)


def run_experts(rows, blend, gates, gate_local, up_local, down_local):
    count, width = rows.shape
    ff_width = gate_local.shape[1]
    block = next(b for b in (384, 256, 128, count) if count % b == 0)
    f32 = jnp.float32
    wide = pl.BlockSpec((block, width), lambda i: (i, 0))
    thin = pl.BlockSpec((block, 1), lambda i: (i, 0))
    inner = pl.BlockSpec((width, ff_width), lambda i: (0, 0))
    outer = pl.BlockSpec((ff_width, width), lambda i: (0, 0))
    return pl.pallas_call(
        expert_kernel,
        grid=(count // block,),
        in_specs=[wide, wide, thin, inner, inner, outer],
        out_specs=[wide, wide, thin, inner, inner, outer],
        out_shape=[
            jax.ShapeDtypeStruct((count, width), rows.dtype),
            jax.ShapeDtypeStruct((count, width), rows.dtype),
            jax.ShapeDtypeStruct((count, 1), f32),
            jax.ShapeDtypeStruct((width, ff_width), f32),
            jax.ShapeDtypeStruct((width, ff_width), f32),
            jax.ShapeDtypeStruct((ff_width, width), f32),
        ],
        cost_estimate=pl.CostEstimate(flops=1000, bytes_accessed=1000, transcendentals=0),
        name="experts",
    )(rows, blend, gates, gate_local, up_local, down_local)


def build_kernel(slots_ref, *refs):
    out_ref = refs[-1]
    plane, lines, capacity, width = out_ref.shape
    for line in range(lines):
        slots = slots_ref[line]
        places = lax.broadcasted_iota(jnp.int32, (plane, capacity, slots.shape[1]), 1)
        picks = jnp.where(slots[:, None, :] == places, 1.0, 0.0)
        rows = jnp.dot(
            picks.reshape(plane * capacity, slots.shape[1]).astype(jnp.bfloat16),
            refs[line][...],
            preferred_element_type=jnp.float32,
        )
        out_ref[:, line] = rows.reshape(plane, capacity, width).astype(jnp.bfloat16)


def build_rows(slots, blocks, capacity):
    lines, plane, unused = slots.shape
    width = blocks[0].shape[1]
    return pl.pallas_call(
        build_kernel,
        out_shape=jax.ShapeDtypeStruct((plane, lines, capacity, width), blocks[0].dtype),
        cost_estimate=pl.CostEstimate(flops=1000, bytes_accessed=1000, transcendentals=0),
        name="build_rows",
    )(slots, *blocks)


def swap_halves(value):
    width = value.shape[1]
    half = HD // 2
    lanes = lax.broadcasted_iota(jnp.int32, value.shape, 1)
    return jnp.where(
        lanes % HD < half, pltpu.roll(value, width - half, 1), pltpu.roll(value, half, 1)
    )


def head_of(value, head):
    return value[:, head * HD : (head + 1) * HD]


def head_product(left, right, left_axis, right_axis):
    return lax.dot_general(
        left,
        right,
        (((left_axis,), (right_axis,)), ((), ())),
        preferred_element_type=jnp.float32,
    )


def probabilities(query, key, visible):
    scores = jnp.where(visible, attn_scale * head_product(query, key, 1, 1), -1e30)
    shifted = jnp.exp(scores - jnp.max(scores, axis=1, keepdims=True))
    return shifted / jnp.sum(shifted, axis=1, keepdims=True)


def attend_kernel(
    query_ref,
    key_ref,
    value_ref,
    cos_ref,
    sin_ref,
    own_ref,
    other_ref,
    query_out,
    key_out,
    value_out,
    mixture_out,
):
    bf16 = jnp.bfloat16
    key_width = key_ref.shape[1]
    queries = query_ref[...]
    keys = key_ref[...]
    cos_table = cos_ref[...]
    sin_table = sin_ref[...]
    queries = (queries * cos_table + swap_halves(queries) * sin_table).astype(bf16)
    keys = (
        keys * cos_table[:, :key_width] + swap_halves(keys) * sin_table[:, :key_width]
    ).astype(bf16)
    values = value_ref[...].astype(bf16)
    query_out[...] = queries
    key_out[...] = keys
    value_out[...] = values
    visible = other_ref[0] <= own_ref[...]
    mixed = []
    for head in range(queries.shape[1] // HD):
        shared = head // (H // KVH)
        probs = probabilities(head_of(queries, head), head_of(keys, shared), visible)
        mixed.append(head_product(probs.astype(bf16), head_of(values, shared), 1, 0))
    mixture_out[...] = jnp.concatenate(mixed, axis=1).astype(bf16)


def attend_back_kernel(
    query_ref,
    key_ref,
    value_ref,
    mixture_ref,
    cos_ref,
    sin_ref,
    own_ref,
    other_ref,
    query_out,
    key_out,
    value_out,
):
    bf16 = jnp.bfloat16
    key_width = key_ref.shape[1]
    queries = query_ref[...]
    keys = key_ref[...]
    values = value_ref[...]
    grad_mixture = mixture_ref[...]
    cos_table = cos_ref[...]
    sin_table = sin_ref[...]
    visible = other_ref[0] <= own_ref[...]
    grad_queries = []
    grad_keys = [0.0] * (key_width // HD)
    grad_values = [0.0] * (key_width // HD)
    for head in range(queries.shape[1] // HD):
        shared = head // (H // KVH)
        query, key = head_of(queries, head), head_of(keys, shared)
        grad_mix = head_of(grad_mixture, head)
        probs = probabilities(query, key, visible)
        grad_probs = head_product(grad_mix, head_of(values, shared), 1, 1)
        inner = jnp.sum(probs * grad_probs, axis=1, keepdims=True)
        grad_scores = (probs * (grad_probs - inner)).astype(bf16)
        grad_values[shared] += head_product(probs.astype(bf16), grad_mix, 0, 0)
        grad_keys[shared] += head_product(grad_scores, query, 0, 0)
        grad_queries.append(head_product(grad_scores, key, 1, 0))
    grad_query = attn_scale * jnp.concatenate(grad_queries, axis=1)
    grad_key = attn_scale * jnp.concatenate(grad_keys, axis=1)
    query_out[...] = (grad_query * cos_table - swap_halves(grad_query) * sin_table).astype(bf16)
    key_out[...] = (
        grad_key * cos_table[:, :key_width] - swap_halves(grad_key) * sin_table[:, :key_width]
    ).astype(bf16)
    value_out[...] = jnp.concatenate(grad_values, axis=1).astype(bf16)


def attention_specs(seq_len):
    query_block = 2 * (H // KVH) * HD
    key_block = 2 * HD
    wide = pl.BlockSpec((seq_len, query_block), lambda m, i: (m, i))
    thin = pl.BlockSpec((seq_len, key_block), lambda m, i: (m, i))
    table = pl.BlockSpec((seq_len, query_block), lambda m, i: (0, 0))
    own = pl.BlockSpec((seq_len, 1), lambda m, i: (m, 0))
    other = pl.BlockSpec((1, 1, seq_len), lambda m, i: (m, 0, 0))
    return wide, thin, table, own, other


def wide_tables(seq_len):
    cos_table, sin_table = rotary_tables(seq_len, HD)
    cos_table, sin_table = cos_table[:, 0], sin_table[:, 0]
    count = 2 * (H // KVH)
    return (
        jnp.tile(jnp.concatenate([cos_table, cos_table], axis=1), (1, count)),
        jnp.tile(jnp.concatenate([-sin_table, sin_table], axis=1), (1, count)),
    )


def run_attention(projected, tables, block_ids):
    micro_count, seq_len = block_ids.shape
    wide, thin, table, own, other = attention_specs(seq_len)
    rows = projected.shape[0]
    bf16 = jnp.bfloat16
    first_key = H * HD // (2 * HD)
    first_value = first_key + KVH // 2
    return pl.pallas_call(
        attend_kernel,
        grid=(micro_count, KVH // 2),
        in_specs=[
            wide,
            pl.BlockSpec((seq_len, 2 * HD), lambda m, i: (m, first_key + i)),
            pl.BlockSpec((seq_len, 2 * HD), lambda m, i: (m, first_value + i)),
            table,
            table,
            own,
            other,
        ],
        out_specs=[wide, thin, thin, wide],
        out_shape=[
            jax.ShapeDtypeStruct((rows, H * HD), bf16),
            jax.ShapeDtypeStruct((rows, KVH * HD), bf16),
            jax.ShapeDtypeStruct((rows, KVH * HD), bf16),
            jax.ShapeDtypeStruct((rows, H * HD), bf16),
        ],
        cost_estimate=pl.CostEstimate(flops=1000, bytes_accessed=1000, transcendentals=0),
        name="attention",
    )(
        projected,
        projected,
        projected,
        *tables,
        block_ids.reshape(-1, 1),
        block_ids.reshape(micro_count, 1, seq_len),
    )


def run_attention_back(queries, keys, values, grad_mixture, tables, block_ids, micro):
    micro_count, seq_len = block_ids.shape
    wide, thin, table, own, other = attention_specs(seq_len)
    bf16 = jnp.bfloat16

    def at(spec, index):
        return pl.BlockSpec(spec.block_shape, index)

    return pl.pallas_call(
        attend_back_kernel,
        grid=(1, KVH // 2),
        in_specs=[
            at(wide, lambda m, i: (micro, i)),
            at(thin, lambda m, i: (micro, i)),
            at(thin, lambda m, i: (micro, i)),
            wide,
            table,
            table,
            at(own, lambda m, i: (micro, 0)),
            at(other, lambda m, i: (micro, 0, 0)),
        ],
        out_specs=[wide, thin, thin],
        out_shape=[
            jax.ShapeDtypeStruct((seq_len, H * HD), bf16),
            jax.ShapeDtypeStruct((seq_len, KVH * HD), bf16),
            jax.ShapeDtypeStruct((seq_len, KVH * HD), bf16),
        ],
        cost_estimate=pl.CostEstimate(flops=1000, bytes_accessed=1000, transcendentals=0),
        name="attention_back",
    )(
        queries,
        keys,
        values,
        grad_mixture,
        *tables,
        block_ids.reshape(-1, 1),
        block_ids.reshape(micro_count, 1, seq_len),
    )


def weights_kernel(left_ref, right_ref, *refs):
    out_ref = refs[-1]
    width = right_ref.shape[1]
    product = head_product(left_ref[...], right_ref[...], 0, 0)
    if len(refs) == 1:
        out_ref[...] = product.astype(out_ref.dtype)
    else:
        out_ref[:, :width] = product.astype(out_ref.dtype)
        out_ref[:, width:] = refs[0][...].astype(out_ref.dtype)


def run_weights(left, right, extra, dtype):
    tokens, height = left.shape
    width = right.shape[1]
    block = 256 if height % 256 == 0 else height
    in_specs = [
        pl.BlockSpec((tokens, block), lambda i: (0, i)),
        pl.BlockSpec((tokens, width), lambda i: (0, 0)),
    ]
    operands = [left, right]
    if extra is not None:
        in_specs.append(pl.BlockSpec((block, extra.shape[1]), lambda i: (i, 0)))
        operands.append(extra)
        width += extra.shape[1]
    return pl.pallas_call(
        weights_kernel,
        grid=(height // block,),
        in_specs=in_specs,
        out_specs=pl.BlockSpec((block, width), lambda i: (i, 0)),
        out_shape=jax.ShapeDtypeStruct((height, width), dtype),
        cost_estimate=pl.CostEstimate(flops=1000, bytes_accessed=1000, transcendentals=0),
        name="weights",
    )(*operands)


def sums_kernel(slots_ref, rows_ref, *out_refs):
    plane, lines, capacity, width = rows_ref.shape
    for line in range(lines):
        slots = slots_ref[line]
        places = lax.broadcasted_iota(jnp.int32, (plane, capacity, slots.shape[1]), 1)
        picks = jnp.where(slots[:, None, :] == places, 1.0, 0.0)
        rows = rows_ref[:, line].astype(jnp.float32).reshape(plane * capacity, width)
        out_refs[line][...] = head_product(
            picks.reshape(plane * capacity, slots.shape[1]).astype(jnp.bfloat16),
            rows.astype(jnp.bfloat16),
            0,
            0,
        ).astype(jnp.bfloat16)


def sum_rows(slots, rows):
    lines, unused, tokens = slots.shape
    return pl.pallas_call(
        sums_kernel,
        out_shape=[jax.ShapeDtypeStruct((tokens, rows.shape[3]), rows.dtype)] * lines,
        cost_estimate=pl.CostEstimate(flops=1000, bytes_accessed=1000, transcendentals=0),
        name="sum_rows",
    )(slots, rows)


def norm_grads(grad_normed, source, recip, gain):
    scaled = grad_normed * gain
    centre = jnp.mean(scaled * source, axis=1, keepdims=True)
    grad_source = recip * scaled - source * (recip * recip * recip) * centre
    return grad_source, jnp.sum(grad_normed * source * recip, axis=0, keepdims=True)


def middle_kernel(*refs):
    parts = refs[:LINES]
    logits_ref, router_ref, residual_ref, recip_ref, gain_ref, cotan_ref, proj_ref = refs[LINES:-4]
    residual_out, attn_out, mixture_out, gain_out = refs[-4:]
    bf16 = jnp.bfloat16
    grad_mid = head_product(logits_ref[...], router_ref[...], 0, 1)
    for part in parts:
        grad_mid = grad_mid + part[...].astype(jnp.float32)
    grad_source, grad_gain = norm_grads(
        grad_mid, residual_ref[...], recip_ref[...], gain_ref[...]
    )
    grad_residual = cotan_ref[...] + grad_source
    grad_attn = (res_scale * grad_residual).astype(bf16)
    residual_out[...] = grad_residual
    attn_out[...] = grad_attn
    mixture_out[...] = head_product(grad_attn, proj_ref[...], 1, 1).astype(bf16)
    gain_out[...] = grad_gain


def run_middle(parts, grad_logits, router, residual, recip, gain, cotangent, out_proj):
    tokens, width = residual.shape
    shape = jax.ShapeDtypeStruct
    return pl.pallas_call(
        middle_kernel,
        out_shape=[
            shape((tokens, width), jnp.float32),
            shape((tokens, width), jnp.bfloat16),
            shape((tokens, out_proj.shape[0]), jnp.bfloat16),
            shape((1, width), jnp.float32),
        ],
        cost_estimate=pl.CostEstimate(flops=1000, bytes_accessed=1000, transcendentals=0),
        name="middle_back",
    )(*parts, grad_logits, router, residual, recip, gain[None], cotangent, out_proj)


def first_kernel(
    query_ref, key_ref, value_ref, proj_ref, tokens_ref, recip_ref, gain_ref, residual_ref,
    out_ref, gain_out,
):
    start = 0
    grad_normed = 0.0
    for ref in (query_ref, key_ref, value_ref):
        stop = start + ref.shape[1]
        grad_normed = grad_normed + head_product(ref[...], proj_ref[:, start:stop], 1, 1)
        start = stop
    grad_source, grad_gain = norm_grads(
        grad_normed, tokens_ref[...], recip_ref[...], gain_ref[...]
    )
    out_ref[...] = residual_ref[...] + grad_source
    gain_out[...] = grad_gain


def run_first(queries, keys, values, qkv_proj, tokens, recip, gain, grad_residual):
    shape = jax.ShapeDtypeStruct
    return pl.pallas_call(
        first_kernel,
        out_shape=[shape(tokens.shape, jnp.float32), shape((1, tokens.shape[1]), jnp.float32)],
        cost_estimate=pl.CostEstimate(flops=1000, bytes_accessed=1000, transcendentals=0),
        name="first_back",
    )(queries, keys, values, qkv_proj, tokens, recip, gain[None], grad_residual)


def on_device(
    hidden,
    cotangent,
    block_ids,
    routes,
    pair_rank,
    norm1_gain,
    norm2_gain,
    w_query,
    w_key,
    w_value,
    w_out,
    w_router,
    w_gate,
    w_up,
    w_down,
):
    micro_count, seq_len = block_ids.shape
    model_width = hidden.shape[1]
    top_count = routes.shape[1]
    devices = lax.axis_size("dp")
    experts = w_router.shape[1]
    plane = devices // LINES
    capacity = (9 * seq_len * top_count + 8 * experts - 1) // (8 * experts)
    query_width = w_query.shape[1]
    kv_width = w_key.shape[1]
    qkv_width = query_width + 2 * kv_width
    tables = wide_tables(seq_len)
    gate_local = w_gate[0]
    up_local = w_up[0]
    down_local = w_down[0]
    bf16 = jnp.bfloat16
    f32 = jnp.float32
    here = lax.axis_index("dp") // plane
    plane_groups = [[line * plane + i for i in range(plane)] for line in range(LINES)]

    def line_shift(step):
        return [
            (i, ((i // plane + step) % LINES) * plane + i % plane) for i in range(devices)
        ]

    def spread(block):
        return [block] + [
            lax.ppermute(block, "dp", line_shift(step)) for step in range(1, LINES)
        ]

    def give_back(blocks):
        return [blocks[0]] + [
            lax.ppermute(blocks[step], "dp", line_shift(-step)) for step in range(1, LINES)
        ]

    def hold(value, *after):
        return lax.optimization_barrier((value, after))[0]

    def reduce_rows(value, first, early, late):
        if plane != 8:
            return lax.psum_scatter(
                value.astype(bf16), "dp", scatter_dimension=0, tiled=True
            ).astype(f32)
        index = lax.axis_index("dp")
        rows = value.shape[0] // devices
        half = value.shape[1] // 256 * 128

        def fold(block, axis, bit):
            side = (index // bit) % 2
            kept = lax.dynamic_index_in_dim(block, side, axis, keepdims=False)
            sent = lax.dynamic_index_in_dim(block, 1 - side, axis, keepdims=False)
            other = lax.ppermute(
                sent.astype(bf16), "dp", [(i, i ^ bit) for i in range(devices)]
            )
            return kept + other.astype(f32)

        value = hold(value, first)
        block = hold(fold(value.reshape(LINES, 2, 2, 2, rows, value.shape[1]), 3, 1), early)
        left, right = block[..., :half], block[..., half:]
        left, right = fold(left, 1, 4), fold(right, 2, 2)
        left, right = hold((left, right), late)
        left, right = fold(left, 1, 2), fold(right, 1, 4)
        block = jnp.concatenate([left, right], axis=2)
        total = lax.dynamic_index_in_dim(block, here, 0, keepdims=False)
        for step in range(1, LINES):
            sent = lax.dynamic_index_in_dim(block, (here + step) % LINES, 0, keepdims=False)
            total = total + lax.ppermute(sent.astype(bf16), "dp", line_shift(step)).astype(f32)
        return total


    def exchange(block):
        return lax.all_to_all(
            block, "dp", split_axis=0, concat_axis=0, tiled=True, axis_index_groups=plane_groups
        )

    small = jnp.concatenate([norm1_gain[:, None], norm2_gain[:, None], w_router], axis=1)
    pad = -small.shape[1] % 128
    shared = lax.all_gather(
        jnp.concatenate(
            [w_query, w_key, w_value, w_out, jnp.pad(small, ((0, 0), (0, pad)))], axis=1
        ),
        "dp",
        axis=0,
        tiled=True,
    )
    qkv_proj = shared[:, :qkv_width]
    first_small = qkv_width + model_width
    out_proj = shared[:, qkv_width:first_small]
    gain_first = shared[:, first_small].astype(f32)
    gain_second = shared[:, first_small + 1].astype(f32)
    router = shared[:, first_small + 2 : first_small + 2 + experts]

    labels = jnp.arange(experts, dtype=jnp.int32)
    route_seq = routes.reshape(micro_count, seq_len, top_count)
    rank_seq = pair_rank.reshape(micro_count, seq_len, top_count)
    named = route_seq[:, None, :, :] == labels[None, :, None, None]
    routed = jnp.any(named, axis=3)
    rank_of = jnp.where(
        routed, jnp.sum(jnp.where(named, rank_seq[:, None], 0), axis=3), seq_len * top_count
    )
    ahead = jnp.sum((rank_of[:, :, :, None] < rank_of[:, :, None, :]).astype(jnp.int32), axis=2)
    slot_of = jnp.where(routed, ahead, -1)
    slot_blocks = jnp.stack(spread(slot_of))
    slots_here = lax.dynamic_slice_in_dim(slot_blocks, here * plane, plane, axis=2)
    places = jnp.arange(capacity, dtype=jnp.int32)
    picks = [
        (slots_here[:, micro, :, None, :] == places[None, None, :, None]).astype(bf16)
        for micro in range(micro_count)
    ]

    cotan_seq = cotangent.reshape(micro_count, seq_len, model_width)
    hidden_seq = hidden.reshape(micro_count, seq_len, model_width)

    def build(micro, blocks):
        if capacity % 8 == 0:
            rows = build_rows(slots_here[:, micro], blocks, capacity)
        else:
            rows = jnp.einsum(
                "ject,jtd->ejcd", picks[micro], jnp.stack(blocks), preferred_element_type=f32
            ).astype(bf16)
        return rows.reshape(plane, LINES * capacity, model_width)

    def sums_of(micro, arrived):
        arrived = arrived.reshape(plane, LINES, capacity, model_width)
        if capacity % 8 == 0:
            return give_back(sum_rows(slots_here[:, micro], arrived))
        sums = jnp.einsum(
            "ject,ejcd->jtd", picks[micro], arrived, preferred_element_type=f32
        ).astype(bf16)
        return give_back([sums[step] for step in range(LINES)])

    def total_of(parts):
        total = parts[0].astype(f32)
        for part in parts[1:]:
            total = total + part.astype(f32)
        return total

    def attend(tokens_in):
        recip_first = lax.rsqrt(jnp.mean(tokens_in * tokens_in, axis=1, keepdims=True) + norm_eps)
        normed_in = (tokens_in * recip_first * gain_first).astype(bf16)
        projected = jnp.dot(normed_in, qkv_proj, preferred_element_type=f32)
        queries, keys, values, mixture = run_attention(projected, tables, block_ids)
        return recip_first, normed_in, queries, keys, values, mixture

    def after_attention(mixture, tokens_in):
        attn_out = jnp.dot(mixture, out_proj, preferred_element_type=f32)
        residual = tokens_in + res_scale * attn_out
        recip_second = lax.rsqrt(jnp.mean(residual * residual, axis=1, keepdims=True) + norm_eps)
        normed_mid = (residual * recip_second * gain_second).astype(bf16)
        return residual, recip_second, normed_mid

    def gates_of(micro, blocks):
        logits = jnp.einsum("de,jtd->jet", router, jnp.stack(blocks), preferred_element_type=f32)
        gates = masked_gates(logits, slot_blocks[:, micro] >= 0)
        gates_here = lax.dynamic_slice_in_dim(gates, here * plane, plane, axis=1)
        slot_gates = jnp.sum(
            jnp.where(picks[micro] > 0, gates_here[:, :, None, :], 0.0), axis=3
        ).transpose(1, 0, 2)
        return gates[0], slot_gates.reshape(plane, LINES * capacity)

    def run_expert(mid, blend, gate_rows):
        grads, scaled, pair_grads, *weights = run_experts(
            mid.reshape(-1, model_width),
            blend.reshape(-1, model_width),
            gate_rows.reshape(-1, 1),
            gate_local,
            up_local,
            down_local,
        )
        return (
            grads.reshape(mid.shape),
            scaled.reshape(mid.shape),
            pair_grads.reshape(mid.shape[:2]),
            weights,
        )

    def pairs_home(pair_back):
        token_grads = [
            jnp.sum(
                jnp.where(
                    picks[m] > 0,
                    pair_back[:, m]
                    .reshape(plane, LINES, capacity)
                    .transpose(1, 0, 2)[:, :, :, None],
                    0.0,
                ),
                axis=2,
            )
            for m in range(micro_count)
        ]
        both = jnp.stack(token_grads, axis=1)
        return give_back([both[step] for step in range(LINES)])

    def attend_back(micro, parts, pair_blocks, gates, before, then):
        residual, recip_second, unused = after[micro]
        pair_grads = jnp.zeros((experts, seq_len), f32)
        for step in range(LINES):
            pair_grads = lax.dynamic_update_slice_in_dim(
                pair_grads, pair_blocks[step], ((here + step) % LINES) * plane, axis=0
            )
        grad_logits = (
            gates * (pair_grads - jnp.sum(gates * pair_grads, axis=0, keepdims=True))
        ).astype(bf16)
        grad_residual, grad_attn, grad_mixture, gain_second_w = run_middle(
            parts,
            grad_logits,
            router,
            residual,
            recip_second,
            gain_second,
            cotan_seq[micro],
            out_proj,
        )
        grads = run_attention_back(
            queries, keys, values, hold(grad_mixture, before(grad_attn)), tables, block_ids, micro
        )
        grad_tokens, gain_first_w = run_first(
            *hold(grads, then),
            qkv_proj,
            hidden_seq[micro],
            rows_of(recip_first, micro),
            gain_first,
            grad_residual,
        )
        return (
            grad_tokens,
            grad_attn,
            jnp.concatenate(grads, axis=1),
            grad_logits,
            gain_second_w,
            gain_first_w,
        )

    blend_rows = [(res_scale * cotan_seq[m]).astype(bf16) for m in range(2)]
    blend_blocks = [
        spread(hold(blend_rows[0], slot_blocks)),
        spread(hold(blend_rows[1], slot_blocks)),
    ]
    blend0 = build(0, blend_blocks[0])
    moved_blend0 = exchange(blend0)
    recip_first, normed_in, queries, keys, values, mixture = attend(hold(hidden, blend0, blend_blocks[1]))

    def rows_of(value, micro):
        return value[micro * seq_len : (micro + 1) * seq_len]

    blend1 = build(1, hold(blend_blocks[1], mixture))
    moved_blend1 = exchange(hold(blend1, moved_blend0))
    after = [after_attention(rows_of(mixture, m), hidden_seq[m]) for m in range(2)]
    blocks0 = spread(after[0][2])
    blocks1 = spread(after[1][2])
    moved_mid0 = exchange(hold(build(0, blocks0), moved_blend1))
    gates0, slot_gates0 = gates_of(0, blocks0)
    gates1, slot_gates1 = gates_of(1, blocks1)
    mid1 = build(1, blocks1)
    gate_rows = exchange(
        hold(jnp.stack([slot_gates0, slot_gates1], axis=1), moved_mid0, mid1)
    )
    moved_mid1 = exchange(hold(mid1, gate_rows))
    grads0, scaled0, pairs0, weights0 = run_expert(
        hold(moved_mid0, mid1), moved_blend0, gate_rows[:, 0]
    )
    moved_grads0 = exchange(hold(grads0, moved_mid1))
    grads1, scaled1, pairs1, weights1 = run_expert(moved_mid1, moved_blend1, gate_rows[:, 1])
    pair_back = exchange(hold(jnp.stack([pairs0, pairs1], axis=1), moved_grads0))
    moved_grads1 = exchange(hold(grads1, pair_back))
    pair_blocks = pairs_home(pair_back)
    back0 = sums_of(0, moved_grads0)
    moved_scaled0 = exchange(hold(scaled0, moved_grads1, back0))
    back1 = sums_of(1, moved_grads1)
    result0 = attend_back(
        0,
        hold(back0, back1[0]),
        [block[0] for block in pair_blocks],
        gates0,
        lambda grad_attn: (moved_grads1, back1[0]),
        (),
    )
    moved_scaled1 = exchange(hold(scaled1, moved_scaled0, back1, result0))
    blend_back0 = sums_of(0, hold(moved_scaled0, result0))

    def out_grads(grad_attn):
        return run_weights(
            mixture, jnp.concatenate([result0[1], grad_attn], axis=0), None, bf16
        )

    result1 = attend_back(
        1,
        hold(back1, result0),
        [block[1] for block in pair_blocks],
        gates1,
        lambda grad_attn: (moved_scaled0, blend_back0[0], out_grads(grad_attn)),
        (),
    )
    blend_back1 = sums_of(1, hold(moved_scaled1, result1))
    outputs = [
        after[0][0] + res_scale * total_of(blend_back0),
        after[1][0] + res_scale * total_of(blend_back1),
    ]
    token_grads_out = [result0[0], result1[0]]
    grad_qkv = jnp.concatenate([result0[2], result1[2]], axis=0)
    out_w = out_grads(result1[1])
    router_w = jnp.einsum(
        "td,et->de",
        jnp.concatenate([after[0][2], after[1][2]], axis=0),
        jnp.concatenate([result0[3], result1[3]], axis=1),
        preferred_element_type=f32,
    )
    gain_second_w = (result0[4] + result1[4])[0]
    gain_first_w = (result0[5] + result1[5])[0]
    grad_gate_w, grad_up_w, grad_down_w = (
        a + b for a, b in zip(weights0, weights1, strict=True)
    )

    small_w = jnp.concatenate([gain_first_w[:, None], gain_second_w[:, None], router_w], axis=1)
    small_w = jnp.pad(small_w, ((0, 0), (0, -small_w.shape[1] % 128)))
    out_sum = lax.psum_scatter(out_w, "dp", scatter_dimension=0, tiled=True)
    qkv_sum = reduce_rows(
        run_weights(normed_in, grad_qkv, small_w, f32),
        (blend_back0, moved_scaled1),
        blend_back1[0],
        blend_back1,
    )
    out_sum = hold(out_sum, qkv_sum).astype(f32)
    return (
        jnp.concatenate(outputs, axis=0),
        jnp.concatenate(token_grads_out, axis=0),
        qkv_sum[:, qkv_width],
        qkv_sum[:, qkv_width + 1],
        qkv_sum[:, :query_width],
        qkv_sum[:, query_width : query_width + kv_width],
        qkv_sum[:, query_width + kv_width : qkv_width],
        out_sum,
        qkv_sum[:, qkv_width + 2 : qkv_width + 2 + experts],
        grad_gate_w[None],
        grad_up_w[None],
        grad_down_w[None],
    )


def solution(mesh):
    return jax.shard_map(
        on_device,
        mesh=mesh,
        in_specs=(
            P("dp", None),
            P("dp", None),
            P("dp", None),
            P("dp", None),
            P("dp", None),
            P("dp"),
            P("dp"),
            P("dp", None),
            P("dp", None),
            P("dp", None),
            P("dp", None),
            P("dp", None),
            P("dp", None, None),
            P("dp", None, None),
            P("dp", None, None),
        ),
        out_specs=(
            P("dp", None),
            P("dp", None),
            P("dp"),
            P("dp"),
            P("dp", None),
            P("dp", None),
            P("dp", None),
            P("dp", None),
            P("dp", None),
            P("dp", None, None),
            P("dp", None, None),
            P("dp", None, None),
        ),
        check_vma=False,
    )
```

```python
import functools

import jax
import jax.numpy as jnp
from jax import lax
from jax.experimental import pallas as pl
from jax.experimental.pallas import tpu as pltpu
from jax.sharding import PartitionSpec as P

H = 24
KVH = 8
HD = 64


res_scale = 0.22
attn_scale = 0.015625
norm_eps = 1e-06
rope_base = 10000.0


def rotary_tables(length, head_size):
    half_size = head_size // 2
    frequency = rope_base ** (-(jnp.arange(half_size, dtype=jnp.float32) * 2.0) / head_size)
    angles = jnp.arange(length, dtype=jnp.float32)[:, None] * frequency[None, :]
    return (jnp.cos(angles)[:, None, :], jnp.sin(angles)[:, None, :])


LINES = 4


def masked_gates(logits, routed):
    peak = jnp.max(jnp.where(routed, logits, -jnp.inf), axis=-2, keepdims=True)
    shifted = jnp.where(routed, jnp.exp(jnp.minimum(logits - peak, 0.0)), 0.0)
    return shifted / jnp.sum(shifted, axis=-2, keepdims=True)


def expert_kernel(
    rows_ref,
    blend_ref,
    gates_ref,
    gate_ref,
    up_ref,
    down_ref,
    grads_ref,
    scaled_ref,
    pairs_ref,
    gate_sum_ref,
    up_sum_ref,
    down_sum_ref,
):
    f32 = jnp.float32
    bf16 = jnp.bfloat16

    def product(left, right, left_axis, right_axis):
        return lax.dot_general(
            left, right, (((left_axis,), (right_axis,)), ((), ())), preferred_element_type=f32
        )

    @pl.when(pl.program_id(0) == 0)
    def _():
        gate_sum_ref[...] = jnp.zeros_like(gate_sum_ref)
        up_sum_ref[...] = jnp.zeros_like(up_sum_ref)
        down_sum_ref[...] = jnp.zeros_like(down_sum_ref)

    rows = rows_ref[...]
    gates = gates_ref[...]
    blend = blend_ref[...].astype(f32)
    gate_pre = product(rows, gate_ref[...], 1, 0)
    up_pre = product(rows, up_ref[...], 1, 0)
    logistic = 1.0 / (1.0 + jnp.exp(-gate_pre))
    silu = gate_pre * logistic
    hidden_act = (silu * up_pre).astype(bf16)
    produced = product(hidden_act, down_ref[...], 1, 0)
    pairs_ref[...] = jnp.sum(produced * blend, axis=1, keepdims=True)
    scaled_ref[...] = (gates * produced).astype(bf16)
    grad_produced = (gates * blend).astype(bf16)
    grad_inner = product(grad_produced, down_ref[...], 1, 1)
    grad_gate_pre = (
        grad_inner * up_pre * (logistic * (1.0 + gate_pre * (1.0 - logistic)))
    ).astype(bf16)
    grad_up_pre = (grad_inner * silu).astype(bf16)
    grads_ref[...] = (
        product(grad_gate_pre, gate_ref[...], 1, 1) + product(grad_up_pre, up_ref[...], 1, 1)
    ).astype(bf16)
    down_sum_ref[...] += product(hidden_act, grad_produced, 0, 0)
    gate_sum_ref[...] += product(rows, grad_gate_pre, 0, 0)
    up_sum_ref[...] += product(rows, grad_up_pre, 0, 0)


def run_experts(rows, blend, gates, gate_local, up_local, down_local):
    count, width = rows.shape
    ff_width = gate_local.shape[1]
    block = next(b for b in (384, 256, 128, count) if count % b == 0)
    f32 = jnp.float32
    wide = pl.BlockSpec((block, width), lambda i: (i, 0))
    thin = pl.BlockSpec((block, 1), lambda i: (i, 0))
    inner = pl.BlockSpec((width, ff_width), lambda i: (0, 0))
    outer = pl.BlockSpec((ff_width, width), lambda i: (0, 0))
    return pl.pallas_call(
        expert_kernel,
        grid=(count // block,),
        in_specs=[wide, wide, thin, inner, inner, outer],
        out_specs=[wide, wide, thin, inner, inner, outer],
        out_shape=[
            jax.ShapeDtypeStruct((count, width), rows.dtype),
            jax.ShapeDtypeStruct((count, width), rows.dtype),
            jax.ShapeDtypeStruct((count, 1), f32),
            jax.ShapeDtypeStruct((width, ff_width), f32),
            jax.ShapeDtypeStruct((width, ff_width), f32),
            jax.ShapeDtypeStruct((ff_width, width), f32),
        ],
        cost_estimate=pl.CostEstimate(flops=1000, bytes_accessed=1000, transcendentals=0),
        name="experts",
    )(rows, blend, gates, gate_local, up_local, down_local)


def build_kernel(slots_ref, *refs):
    out_ref = refs[-1]
    plane, lines, capacity, width = out_ref.shape
    for line in range(lines):
        slots = slots_ref[line]
        places = lax.broadcasted_iota(jnp.int32, (plane, capacity, slots.shape[1]), 1)
        picks = jnp.where(slots[:, None, :] == places, 1.0, 0.0)
        rows = jnp.dot(
            picks.reshape(plane * capacity, slots.shape[1]).astype(jnp.bfloat16),
            refs[line][...],
            preferred_element_type=jnp.float32,
        )
        out_ref[:, line] = rows.reshape(plane, capacity, width).astype(jnp.bfloat16)


def build_rows(slots, blocks, capacity):
    lines, plane, unused = slots.shape
    width = blocks[0].shape[1]
    return pl.pallas_call(
        build_kernel,
        out_shape=jax.ShapeDtypeStruct((plane, lines, capacity, width), blocks[0].dtype),
        cost_estimate=pl.CostEstimate(flops=1000, bytes_accessed=1000, transcendentals=0),
        name="build_rows",
    )(slots, *blocks)


def swap_halves(value):
    width = value.shape[1]
    half = HD // 2
    lanes = lax.broadcasted_iota(jnp.int32, value.shape, 1)
    return jnp.where(
        lanes % HD < half, pltpu.roll(value, width - half, 1), pltpu.roll(value, half, 1)
    )


def head_of(value, head):
    return value[:, head * HD : (head + 1) * HD]


def head_product(left, right, left_axis, right_axis):
    return lax.dot_general(
        left,
        right,
        (((left_axis,), (right_axis,)), ((), ())),
        preferred_element_type=jnp.float32,
    )


def probabilities(query, key, visible):
    scores = jnp.where(visible, attn_scale * head_product(query, key, 1, 1), -1e30)
    shifted = jnp.exp(scores - jnp.max(scores, axis=1, keepdims=True))
    return shifted / jnp.sum(shifted, axis=1, keepdims=True)


def attend_kernel(
    query_ref,
    key_ref,
    value_ref,
    cos_ref,
    sin_ref,
    own_ref,
    other_ref,
    query_out,
    key_out,
    value_out,
    mixture_out,
):
    bf16 = jnp.bfloat16
    key_width = key_ref.shape[1]
    queries = query_ref[...]
    keys = key_ref[...]
    cos_table = cos_ref[...]
    sin_table = sin_ref[...]
    queries = (queries * cos_table + swap_halves(queries) * sin_table).astype(bf16)
    keys = (
        keys * cos_table[:, :key_width] + swap_halves(keys) * sin_table[:, :key_width]
    ).astype(bf16)
    values = value_ref[...].astype(bf16)
    query_out[...] = queries
    key_out[...] = keys
    value_out[...] = values
    visible = other_ref[0] <= own_ref[...]
    mixed = []
    for head in range(queries.shape[1] // HD):
        shared = head // (H // KVH)
        probs = probabilities(head_of(queries, head), head_of(keys, shared), visible)
        mixed.append(head_product(probs.astype(bf16), head_of(values, shared), 1, 0))
    mixture_out[...] = jnp.concatenate(mixed, axis=1).astype(bf16)


def attend_back_kernel(
    query_ref,
    key_ref,
    value_ref,
    mixture_ref,
    cos_ref,
    sin_ref,
    own_ref,
    other_ref,
    query_out,
    key_out,
    value_out,
):
    bf16 = jnp.bfloat16
    key_width = key_ref.shape[1]
    queries = query_ref[...]
    keys = key_ref[...]
    values = value_ref[...]
    grad_mixture = mixture_ref[...]
    cos_table = cos_ref[...]
    sin_table = sin_ref[...]
    visible = other_ref[0] <= own_ref[...]
    grad_queries = []
    grad_keys = [0.0] * (key_width // HD)
    grad_values = [0.0] * (key_width // HD)
    for head in range(queries.shape[1] // HD):
        shared = head // (H // KVH)
        query, key = head_of(queries, head), head_of(keys, shared)
        grad_mix = head_of(grad_mixture, head)
        probs = probabilities(query, key, visible)
        grad_probs = head_product(grad_mix, head_of(values, shared), 1, 1)
        inner = jnp.sum(probs * grad_probs, axis=1, keepdims=True)
        grad_scores = (probs * (grad_probs - inner)).astype(bf16)
        grad_values[shared] += head_product(probs.astype(bf16), grad_mix, 0, 0)
        grad_keys[shared] += head_product(grad_scores, query, 0, 0)
        grad_queries.append(head_product(grad_scores, key, 1, 0))
    grad_query = attn_scale * jnp.concatenate(grad_queries, axis=1)
    grad_key = attn_scale * jnp.concatenate(grad_keys, axis=1)
    query_out[...] = (grad_query * cos_table - swap_halves(grad_query) * sin_table).astype(bf16)
    key_out[...] = (
        grad_key * cos_table[:, :key_width] - swap_halves(grad_key) * sin_table[:, :key_width]
    ).astype(bf16)
    value_out[...] = jnp.concatenate(grad_values, axis=1).astype(bf16)


def attention_specs(seq_len):
    query_block = 2 * (H // KVH) * HD
    key_block = 2 * HD
    wide = pl.BlockSpec((seq_len, query_block), lambda m, i: (m, i))
    thin = pl.BlockSpec((seq_len, key_block), lambda m, i: (m, i))
    table = pl.BlockSpec((seq_len, query_block), lambda m, i: (0, 0))
    own = pl.BlockSpec((seq_len, 1), lambda m, i: (m, 0))
    other = pl.BlockSpec((1, 1, seq_len), lambda m, i: (m, 0, 0))
    return wide, thin, table, own, other


def wide_tables(seq_len):
    cos_table, sin_table = rotary_tables(seq_len, HD)
    cos_table, sin_table = cos_table[:, 0], sin_table[:, 0]
    count = 2 * (H // KVH)
    return (
        jnp.tile(jnp.concatenate([cos_table, cos_table], axis=1), (1, count)),
        jnp.tile(jnp.concatenate([-sin_table, sin_table], axis=1), (1, count)),
    )


def run_attention(projected, tables, block_ids):
    micro_count, seq_len = block_ids.shape
    wide, thin, table, own, other = attention_specs(seq_len)
    rows = projected.shape[0]
    bf16 = jnp.bfloat16
    first_key = H * HD // (2 * HD)
    first_value = first_key + KVH // 2
    return pl.pallas_call(
        attend_kernel,
        grid=(micro_count, KVH // 2),
        in_specs=[
            wide,
            pl.BlockSpec((seq_len, 2 * HD), lambda m, i: (m, first_key + i)),
            pl.BlockSpec((seq_len, 2 * HD), lambda m, i: (m, first_value + i)),
            table,
            table,
            own,
            other,
        ],
        out_specs=[wide, thin, thin, wide],
        out_shape=[
            jax.ShapeDtypeStruct((rows, H * HD), bf16),
            jax.ShapeDtypeStruct((rows, KVH * HD), bf16),
            jax.ShapeDtypeStruct((rows, KVH * HD), bf16),
            jax.ShapeDtypeStruct((rows, H * HD), bf16),
        ],
        cost_estimate=pl.CostEstimate(flops=1000, bytes_accessed=1000, transcendentals=0),
        name="attention",
    )(
        projected,
        projected,
        projected,
        *tables,
        block_ids.reshape(-1, 1),
        block_ids.reshape(micro_count, 1, seq_len),
    )


def run_attention_back(queries, keys, values, grad_mixture, tables, block_ids, micro):
    micro_count, seq_len = block_ids.shape
    wide, thin, table, own, other = attention_specs(seq_len)
    bf16 = jnp.bfloat16

    def at(spec, index):
        return pl.BlockSpec(spec.block_shape, index)

    return pl.pallas_call(
        attend_back_kernel,
        grid=(1, KVH // 2),
        in_specs=[
            at(wide, lambda m, i: (micro, i)),
            at(thin, lambda m, i: (micro, i)),
            at(thin, lambda m, i: (micro, i)),
            wide,
            table,
            table,
            at(own, lambda m, i: (micro, 0)),
            at(other, lambda m, i: (micro, 0, 0)),
        ],
        out_specs=[wide, thin, thin],
        out_shape=[
            jax.ShapeDtypeStruct((seq_len, H * HD), bf16),
            jax.ShapeDtypeStruct((seq_len, KVH * HD), bf16),
            jax.ShapeDtypeStruct((seq_len, KVH * HD), bf16),
        ],
        cost_estimate=pl.CostEstimate(flops=1000, bytes_accessed=1000, transcendentals=0),
        name="attention_back",
    )(
        queries,
        keys,
        values,
        grad_mixture,
        *tables,
        block_ids.reshape(-1, 1),
        block_ids.reshape(micro_count, 1, seq_len),
    )


def weights_kernel(*refs, counts):
    left_ref, out_ref = refs[0], refs[-1]
    rights = refs[1 : 1 + sum(counts)]
    tokens = left_ref.shape[0] // len(counts)
    start = 0
    for i in range(counts[0]):
        width = rights[i].shape[1]
        product = 0.0
        for m in range(len(counts)):
            product = product + head_product(
                left_ref[m * tokens : (m + 1) * tokens], rights[m * counts[0] + i][...], 0, 0
            )
        out_ref[:, start : start + width] = product.astype(out_ref.dtype)
        start += width
    if len(refs) > 2 + sum(counts):
        out_ref[:, start:] = refs[-2][...].astype(out_ref.dtype)


def run_weights(left, groups, extra, dtype):
    tokens, height = left.shape
    block = 256 if height % 256 == 0 else height
    rights = [right for group in groups for right in group]
    width = sum(right.shape[1] for right in groups[0])
    in_specs = [pl.BlockSpec((tokens, block), lambda i: (0, i))] + [
        pl.BlockSpec(right.shape, lambda i: (0, 0)) for right in rights
    ]
    operands = [left, *rights]
    if extra is not None:
        in_specs.append(pl.BlockSpec((block, extra.shape[1]), lambda i: (i, 0)))
        operands.append(extra)
        width += extra.shape[1]
    return pl.pallas_call(
        functools.partial(weights_kernel, counts=tuple(len(group) for group in groups)),
        grid=(height // block,),
        in_specs=in_specs,
        out_specs=pl.BlockSpec((block, width), lambda i: (i, 0)),
        out_shape=jax.ShapeDtypeStruct((height, width), dtype),
        cost_estimate=pl.CostEstimate(flops=1000, bytes_accessed=1000, transcendentals=0),
        name="weights",
    )(*operands)


def sums_kernel(slots_ref, rows_ref, *out_refs):
    plane, lines, capacity, width = rows_ref.shape
    for line in range(lines):
        slots = slots_ref[line]
        places = lax.broadcasted_iota(jnp.int32, (plane, capacity, slots.shape[1]), 1)
        picks = jnp.where(slots[:, None, :] == places, 1.0, 0.0)
        rows = rows_ref[:, line].astype(jnp.float32).reshape(plane * capacity, width)
        out_refs[line][...] = head_product(
            picks.reshape(plane * capacity, slots.shape[1]).astype(jnp.bfloat16),
            rows.astype(jnp.bfloat16),
            0,
            0,
        ).astype(jnp.bfloat16)


def sum_rows(slots, rows):
    lines, unused, tokens = slots.shape
    return pl.pallas_call(
        sums_kernel,
        out_shape=[jax.ShapeDtypeStruct((tokens, rows.shape[3]), rows.dtype)] * lines,
        cost_estimate=pl.CostEstimate(flops=1000, bytes_accessed=1000, transcendentals=0),
        name="sum_rows",
    )(slots, rows)


def norm_grads(grad_normed, source, recip, gain):
    scaled = grad_normed * gain
    centre = jnp.mean(scaled * source, axis=1, keepdims=True)
    grad_source = recip * scaled - source * (recip * recip * recip) * centre
    return grad_source, jnp.sum(grad_normed * source * recip, axis=0, keepdims=True)


def middle_kernel(*refs):
    parts = refs[:LINES]
    logits_ref, router_ref, residual_ref, recip_ref, gain_ref, cotan_ref, proj_ref = refs[LINES:-4]
    residual_out, attn_out, mixture_out, gain_out = refs[-4:]
    bf16 = jnp.bfloat16
    grad_mid = head_product(logits_ref[...], router_ref[...], 0, 1)
    for part in parts:
        grad_mid = grad_mid + part[...].astype(jnp.float32)
    grad_source, grad_gain = norm_grads(
        grad_mid, residual_ref[...], recip_ref[...], gain_ref[...]
    )
    grad_residual = cotan_ref[...] + grad_source
    grad_attn = (res_scale * grad_residual).astype(bf16)
    residual_out[...] = grad_residual
    attn_out[...] = grad_attn
    mixture_out[...] = head_product(grad_attn, proj_ref[...], 1, 1).astype(bf16)
    gain_out[...] = grad_gain


def run_middle(parts, grad_logits, router, residual, recip, gain, cotangent, out_proj):
    tokens, width = residual.shape
    shape = jax.ShapeDtypeStruct
    return pl.pallas_call(
        middle_kernel,
        out_shape=[
            shape((tokens, width), jnp.float32),
            shape((tokens, width), jnp.bfloat16),
            shape((tokens, out_proj.shape[0]), jnp.bfloat16),
            shape((1, width), jnp.float32),
        ],
        cost_estimate=pl.CostEstimate(flops=1000, bytes_accessed=1000, transcendentals=0),
        name="middle_back",
    )(*parts, grad_logits, router, residual, recip, gain[None], cotangent, out_proj)


def first_kernel(
    query_ref, key_ref, value_ref, proj_ref, tokens_ref, recip_ref, gain_ref, residual_ref,
    out_ref, gain_out,
):
    start = 0
    grad_normed = 0.0
    for ref in (query_ref, key_ref, value_ref):
        stop = start + ref.shape[1]
        grad_normed = grad_normed + head_product(ref[...], proj_ref[:, start:stop], 1, 1)
        start = stop
    grad_source, grad_gain = norm_grads(
        grad_normed, tokens_ref[...], recip_ref[...], gain_ref[...]
    )
    out_ref[...] = residual_ref[...] + grad_source
    gain_out[...] = grad_gain


def run_first(queries, keys, values, qkv_proj, tokens, recip, gain, grad_residual):
    shape = jax.ShapeDtypeStruct
    return pl.pallas_call(
        first_kernel,
        out_shape=[shape(tokens.shape, jnp.float32), shape((1, tokens.shape[1]), jnp.float32)],
        cost_estimate=pl.CostEstimate(flops=1000, bytes_accessed=1000, transcendentals=0),
        name="first_back",
    )(queries, keys, values, qkv_proj, tokens, recip, gain[None], grad_residual)


def on_device(
    hidden,
    cotangent,
    block_ids,
    routes,
    pair_rank,
    norm1_gain,
    norm2_gain,
    w_query,
    w_key,
    w_value,
    w_out,
    w_router,
    w_gate,
    w_up,
    w_down,
):
    micro_count, seq_len = block_ids.shape
    model_width = hidden.shape[1]
    top_count = routes.shape[1]
    devices = lax.axis_size("dp")
    experts = w_router.shape[1]
    plane = devices // LINES
    capacity = (9 * seq_len * top_count + 8 * experts - 1) // (8 * experts)
    query_width = w_query.shape[1]
    kv_width = w_key.shape[1]
    qkv_width = query_width + 2 * kv_width
    tables = wide_tables(seq_len)
    gate_local = w_gate[0]
    up_local = w_up[0]
    down_local = w_down[0]
    bf16 = jnp.bfloat16
    f32 = jnp.float32
    here = lax.axis_index("dp") // plane
    plane_groups = [[line * plane + i for i in range(plane)] for line in range(LINES)]

    def line_shift(step):
        return [
            (i, ((i // plane + step) % LINES) * plane + i % plane) for i in range(devices)
        ]

    def spread(block):
        return [block] + [
            lax.ppermute(block, "dp", line_shift(step)) for step in range(1, LINES)
        ]

    def give_back(blocks):
        return [blocks[0]] + [
            lax.ppermute(blocks[step], "dp", line_shift(-step)) for step in range(1, LINES)
        ]

    def hold(value, *after):
        return lax.optimization_barrier((value, after))[0]

    def reduce_rows(value, first, early, late):
        if plane != 8:
            return lax.psum_scatter(
                value.astype(bf16), "dp", scatter_dimension=0, tiled=True
            ).astype(f32)
        index = lax.axis_index("dp")
        rows = value.shape[0] // devices
        half = value.shape[1] // 256 * 128

        def fold(block, axis, bit):
            side = (index // bit) % 2
            kept = lax.dynamic_index_in_dim(block, side, axis, keepdims=False)
            sent = lax.dynamic_index_in_dim(block, 1 - side, axis, keepdims=False)
            other = lax.ppermute(
                sent.astype(bf16), "dp", [(i, i ^ bit) for i in range(devices)]
            )
            return kept + other.astype(f32)

        value = hold(value, first)
        block = hold(fold(value.reshape(LINES, 2, 2, 2, rows, value.shape[1]), 3, 1), early)
        left, right = block[..., :half], block[..., half:]
        left, right = fold(left, 1, 4), fold(right, 2, 2)
        left, right = hold((left, right), late)
        left, right = fold(left, 1, 2), fold(right, 1, 4)
        block = jnp.concatenate([left, right], axis=2)
        total = lax.dynamic_index_in_dim(block, here, 0, keepdims=False)
        for step in range(1, LINES):
            sent = lax.dynamic_index_in_dim(block, (here + step) % LINES, 0, keepdims=False)
            total = total + lax.ppermute(sent.astype(bf16), "dp", line_shift(step)).astype(f32)
        return total


    def exchange(block):
        return lax.all_to_all(
            block, "dp", split_axis=0, concat_axis=0, tiled=True, axis_index_groups=plane_groups
        )

    small = jnp.concatenate([norm1_gain[:, None], norm2_gain[:, None], w_router], axis=1)
    pad = -small.shape[1] % 128
    shared = lax.all_gather(
        jnp.concatenate(
            [w_query, w_key, w_value, w_out, jnp.pad(small, ((0, 0), (0, pad)))], axis=1
        ),
        "dp",
        axis=0,
        tiled=True,
    )
    qkv_proj = shared[:, :qkv_width]
    first_small = qkv_width + model_width
    out_proj = shared[:, qkv_width:first_small]
    gain_first = shared[:, first_small].astype(f32)
    gain_second = shared[:, first_small + 1].astype(f32)
    router = shared[:, first_small + 2 : first_small + 2 + experts]

    labels = jnp.arange(experts, dtype=jnp.int32)
    route_seq = routes.reshape(micro_count, seq_len, top_count)
    rank_seq = pair_rank.reshape(micro_count, seq_len, top_count)
    named = route_seq[:, None, :, :] == labels[None, :, None, None]
    routed = jnp.any(named, axis=3)
    rank_of = jnp.where(
        routed, jnp.sum(jnp.where(named, rank_seq[:, None], 0), axis=3), seq_len * top_count
    )
    ahead = jnp.sum((rank_of[:, :, :, None] < rank_of[:, :, None, :]).astype(jnp.int32), axis=2)
    slot_of = jnp.where(routed, ahead, -1)
    slot_blocks = jnp.stack(spread(slot_of))
    slots_here = lax.dynamic_slice_in_dim(slot_blocks, here * plane, plane, axis=2)
    places = jnp.arange(capacity, dtype=jnp.int32)
    picks = [
        (slots_here[:, micro, :, None, :] == places[None, None, :, None]).astype(bf16)
        for micro in range(micro_count)
    ]

    cotan_seq = cotangent.reshape(micro_count, seq_len, model_width)
    hidden_seq = hidden.reshape(micro_count, seq_len, model_width)

    def build(micro, blocks):
        if capacity % 8 == 0:
            rows = build_rows(slots_here[:, micro], blocks, capacity)
        else:
            rows = jnp.einsum(
                "ject,jtd->ejcd", picks[micro], jnp.stack(blocks), preferred_element_type=f32
            ).astype(bf16)
        return rows.reshape(plane, LINES * capacity, model_width)

    def sums_of(micro, arrived):
        arrived = arrived.reshape(plane, LINES, capacity, model_width)
        if capacity % 8 == 0:
            return give_back(sum_rows(slots_here[:, micro], arrived))
        sums = jnp.einsum(
            "ject,ejcd->jtd", picks[micro], arrived, preferred_element_type=f32
        ).astype(bf16)
        return give_back([sums[step] for step in range(LINES)])

    def total_of(parts):
        total = parts[0].astype(f32)
        for part in parts[1:]:
            total = total + part.astype(f32)
        return total

    def attend(tokens_in):
        recip_first = lax.rsqrt(jnp.mean(tokens_in * tokens_in, axis=1, keepdims=True) + norm_eps)
        normed_in = (tokens_in * recip_first * gain_first).astype(bf16)
        projected = jnp.dot(normed_in, qkv_proj, preferred_element_type=f32)
        queries, keys, values, mixture = run_attention(projected, tables, block_ids)
        return recip_first, normed_in, queries, keys, values, mixture

    def after_attention(mixture, tokens_in):
        attn_out = jnp.dot(mixture, out_proj, preferred_element_type=f32)
        residual = tokens_in + res_scale * attn_out
        recip_second = lax.rsqrt(jnp.mean(residual * residual, axis=1, keepdims=True) + norm_eps)
        normed_mid = (residual * recip_second * gain_second).astype(bf16)
        return residual, recip_second, normed_mid

    def gates_of(micro, blocks):
        logits = jnp.einsum("de,jtd->jet", router, jnp.stack(blocks), preferred_element_type=f32)
        gates = masked_gates(logits, slot_blocks[:, micro] >= 0)
        gates_here = lax.dynamic_slice_in_dim(gates, here * plane, plane, axis=1)
        slot_gates = jnp.sum(
            jnp.where(picks[micro] > 0, gates_here[:, :, None, :], 0.0), axis=3
        ).transpose(1, 0, 2)
        return gates[0], slot_gates.reshape(plane, LINES * capacity)

    def run_expert(mid, blend, gate_rows):
        grads, scaled, pair_grads, *weights = run_experts(
            mid.reshape(-1, model_width),
            blend.reshape(-1, model_width),
            gate_rows.reshape(-1, 1),
            gate_local,
            up_local,
            down_local,
        )
        return (
            grads.reshape(mid.shape),
            scaled.reshape(mid.shape),
            pair_grads.reshape(mid.shape[:2]),
            weights,
        )

    def pairs_home(pair_back):
        token_grads = [
            jnp.sum(
                jnp.where(
                    picks[m] > 0,
                    pair_back[:, m]
                    .reshape(plane, LINES, capacity)
                    .transpose(1, 0, 2)[:, :, :, None],
                    0.0,
                ),
                axis=2,
            )
            for m in range(micro_count)
        ]
        both = jnp.stack(token_grads, axis=1)
        return give_back([both[step] for step in range(LINES)])

    def attend_back(micro, parts, pair_blocks, gates, before, then):
        residual, recip_second, unused = after[micro]
        pair_grads = jnp.zeros((experts, seq_len), f32)
        for step in range(LINES):
            pair_grads = lax.dynamic_update_slice_in_dim(
                pair_grads, pair_blocks[step], ((here + step) % LINES) * plane, axis=0
            )
        grad_logits = (
            gates * (pair_grads - jnp.sum(gates * pair_grads, axis=0, keepdims=True))
        ).astype(bf16)
        grad_residual, grad_attn, grad_mixture, gain_second_w = run_middle(
            parts,
            grad_logits,
            router,
            residual,
            recip_second,
            gain_second,
            cotan_seq[micro],
            proj_copy[1],
        )
        grads = run_attention_back(
            queries, keys, values, hold(grad_mixture, before(grad_attn)), tables, block_ids, micro
        )
        grad_tokens, gain_first_w = run_first(
            *grads,
            proj_copy[0],
            hidden_seq[micro],
            rows_of(recip_first, micro),
            gain_first,
            grad_residual,
        )
        grads, gain_first_w = hold((grads, gain_first_w), then)
        return (
            grad_tokens,
            grad_attn,
            grads,
            grad_logits,
            gain_second_w,
            gain_first_w,
        )

    blend_rows = [(res_scale * cotan_seq[m]).astype(bf16) for m in range(2)]
    blend_blocks = [
        spread(hold(blend_rows[0], slot_blocks)),
        spread(hold(blend_rows[1], slot_blocks)),
    ]
    blend0 = build(0, blend_blocks[0])
    moved_blend0 = exchange(blend0)
    recip_first, normed_in, queries, keys, values, mixture = attend(hold(hidden, blend0, blend_blocks[1]))

    def rows_of(value, micro):
        return value[micro * seq_len : (micro + 1) * seq_len]

    blend1 = build(1, hold(blend_blocks[1], mixture))
    moved_blend1 = exchange(hold(blend1, moved_blend0))
    after = [after_attention(rows_of(mixture, m), hidden_seq[m]) for m in range(2)]
    blocks0 = spread(after[0][2])
    blocks1 = spread(after[1][2])
    moved_mid0 = exchange(hold(build(0, blocks0), moved_blend1))
    gates0, slot_gates0 = gates_of(0, blocks0)
    gates1, slot_gates1 = gates_of(1, blocks1)
    mid1 = build(1, blocks1)
    gate_rows = exchange(
        hold(jnp.stack([slot_gates0, slot_gates1], axis=1), moved_mid0, mid1)
    )
    moved_mid1 = exchange(hold(mid1, gate_rows))
    grads0, scaled0, pairs0, weights0 = run_expert(
        hold(moved_mid0, mid1), moved_blend0, gate_rows[:, 0]
    )
    moved_grads0 = exchange(hold(grads0, moved_mid1))
    proj_copy = hold((qkv_proj, out_proj), moved_mid0)
    grads1, scaled1, pairs1, weights1 = run_expert(
        hold(moved_mid1, proj_copy), moved_blend1, gate_rows[:, 1]
    )
    pair_back = exchange(hold(jnp.stack([pairs0, pairs1], axis=1), moved_grads0))
    moved_grads1 = exchange(hold(grads1, pair_back))
    pair_blocks = pairs_home(pair_back)
    back0 = sums_of(0, moved_grads0)
    moved_scaled0 = exchange(hold(scaled0, moved_grads1, back0, pair_blocks))
    back1 = sums_of(1, moved_grads1)
    result0 = attend_back(
        0,
        hold(back0, back1[0]),
        [block[0] for block in pair_blocks],
        gates0,
        lambda grad_attn: (moved_grads1, back1[0]),
        (),
    )
    moved_scaled1 = exchange(hold(scaled1, moved_scaled0, back1, result0))
    blend_back0 = sums_of(0, hold(moved_scaled0, result0))

    def out_grads(grad_attn):
        return run_weights(
            mixture, [[result0[1]], [grad_attn]], None, bf16
        )

    result1 = attend_back(
        1,
        hold(back1, result0, blend_back0[0]),
        [block[1] for block in pair_blocks],
        gates1,
        lambda grad_attn: (moved_scaled0, blend_back0[0], out_grads(grad_attn)),
        blend_back0,
    )
    blend_back1 = sums_of(1, hold(moved_scaled1, result1))
    outputs = [
        after[0][0] + res_scale * total_of(blend_back0),
        after[1][0] + res_scale * total_of(blend_back1),
    ]
    token_grads_out = [result0[0], result1[0]]
    out_w = out_grads(result1[1])
    router_w = jnp.einsum(
        "td,et->de",
        jnp.concatenate([after[0][2], after[1][2]], axis=0),
        jnp.concatenate([result0[3], result1[3]], axis=1),
        preferred_element_type=f32,
    )
    gain_second_w = (result0[4] + result1[4])[0]
    gain_first_w = (result0[5] + result1[5])[0]
    grad_gate_w, grad_up_w, grad_down_w = (
        a + b for a, b in zip(weights0, weights1, strict=True)
    )

    small_w = jnp.concatenate([gain_first_w[:, None], gain_second_w[:, None], router_w], axis=1)
    small_w = jnp.pad(small_w, ((0, 0), (0, -small_w.shape[1] % 128)))
    out_sum = lax.psum_scatter(out_w, "dp", scatter_dimension=0, tiled=True)
    qkv_sum = reduce_rows(
        run_weights(normed_in, [result0[2], result1[2]], small_w, f32),
        moved_scaled1,
        blend_back1[0],
        blend_back1,
    )
    out_sum = hold(out_sum, qkv_sum).astype(f32)
    return (
        jnp.concatenate(outputs, axis=0),
        jnp.concatenate(token_grads_out, axis=0),
        qkv_sum[:, qkv_width],
        qkv_sum[:, qkv_width + 1],
        qkv_sum[:, :query_width],
        qkv_sum[:, query_width : query_width + kv_width],
        qkv_sum[:, query_width + kv_width : qkv_width],
        out_sum,
        qkv_sum[:, qkv_width + 2 : qkv_width + 2 + experts],
        grad_gate_w[None],
        grad_up_w[None],
        grad_down_w[None],
    )


def solution(mesh):
    return jax.shard_map(
        on_device,
        mesh=mesh,
        in_specs=(
            P("dp", None),
            P("dp", None),
            P("dp", None),
            P("dp", None),
            P("dp", None),
            P("dp"),
            P("dp"),
            P("dp", None),
            P("dp", None),
            P("dp", None),
            P("dp", None),
            P("dp", None),
            P("dp", None, None),
            P("dp", None, None),
            P("dp", None, None),
        ),
        out_specs=(
            P("dp", None),
            P("dp", None),
            P("dp"),
            P("dp"),
            P("dp", None),
            P("dp", None),
            P("dp", None),
            P("dp", None),
            P("dp", None),
            P("dp", None, None),
            P("dp", None, None),
            P("dp", None, None),
        ),
        check_vma=False,
    )
```

```python
import functools

import jax
import jax.numpy as jnp
from jax import lax
from jax.experimental import pallas as pl
from jax.experimental.pallas import tpu as pltpu
from jax.sharding import PartitionSpec as P

H = 24
KVH = 8
HD = 64


res_scale = 0.22
attn_scale = 0.015625
norm_eps = 1e-06
rope_base = 10000.0


def rotary_tables(length, head_size):
    half_size = head_size // 2
    frequency = rope_base ** (-(jnp.arange(half_size, dtype=jnp.float32) * 2.0) / head_size)
    angles = jnp.arange(length, dtype=jnp.float32)[:, None] * frequency[None, :]
    return (jnp.cos(angles)[:, None, :], jnp.sin(angles)[:, None, :])


LINES = 4


def masked_gates(logits, routed):
    peak = jnp.max(jnp.where(routed, logits, -jnp.inf), axis=-2, keepdims=True)
    shifted = jnp.where(routed, jnp.exp(jnp.minimum(logits - peak, 0.0)), 0.0)
    return shifted / jnp.sum(shifted, axis=-2, keepdims=True)


def expert_kernel(
    rows_ref,
    blend_ref,
    gates_ref,
    gate_ref,
    up_ref,
    down_ref,
    grads_ref,
    scaled_ref,
    pairs_ref,
    gate_sum_ref,
    up_sum_ref,
    down_sum_ref,
):
    f32 = jnp.float32
    bf16 = jnp.bfloat16

    def product(left, right, left_axis, right_axis):
        return lax.dot_general(
            left, right, (((left_axis,), (right_axis,)), ((), ())), preferred_element_type=f32
        )

    @pl.when(pl.program_id(0) == 0)
    def _():
        gate_sum_ref[...] = jnp.zeros_like(gate_sum_ref)
        up_sum_ref[...] = jnp.zeros_like(up_sum_ref)
        down_sum_ref[...] = jnp.zeros_like(down_sum_ref)

    rows = rows_ref[...]
    gates = gates_ref[...]
    blend = blend_ref[...].astype(f32)
    gate_pre = product(rows, gate_ref[...], 1, 0)
    up_pre = product(rows, up_ref[...], 1, 0)
    logistic = 1.0 / (1.0 + jnp.exp(-gate_pre))
    silu = gate_pre * logistic
    hidden_act = (silu * up_pre).astype(bf16)
    produced = product(hidden_act, down_ref[...], 1, 0)
    pairs_ref[...] = jnp.sum(produced * blend, axis=1, keepdims=True)
    scaled_ref[...] = (gates * produced).astype(bf16)
    grad_produced = (gates * blend).astype(bf16)
    grad_inner = product(grad_produced, down_ref[...], 1, 1)
    grad_gate_pre = (
        grad_inner * up_pre * (logistic * (1.0 + gate_pre * (1.0 - logistic)))
    ).astype(bf16)
    grad_up_pre = (grad_inner * silu).astype(bf16)
    grads_ref[...] = (
        product(grad_gate_pre, gate_ref[...], 1, 1) + product(grad_up_pre, up_ref[...], 1, 1)
    ).astype(bf16)
    down_sum_ref[...] += product(hidden_act, grad_produced, 0, 0)
    gate_sum_ref[...] += product(rows, grad_gate_pre, 0, 0)
    up_sum_ref[...] += product(rows, grad_up_pre, 0, 0)


def run_experts(rows, blend, gates, gate_local, up_local, down_local):
    count, width = rows.shape
    ff_width = gate_local.shape[1]
    block = next(b for b in (384, 256, 128, count) if count % b == 0)
    f32 = jnp.float32
    wide = pl.BlockSpec((block, width), lambda i: (i, 0))
    thin = pl.BlockSpec((block, 1), lambda i: (i, 0))
    inner = pl.BlockSpec((width, ff_width), lambda i: (0, 0))
    outer = pl.BlockSpec((ff_width, width), lambda i: (0, 0))
    return pl.pallas_call(
        expert_kernel,
        grid=(count // block,),
        in_specs=[wide, wide, thin, inner, inner, outer],
        out_specs=[wide, wide, thin, inner, inner, outer],
        out_shape=[
            jax.ShapeDtypeStruct((count, width), rows.dtype),
            jax.ShapeDtypeStruct((count, width), rows.dtype),
            jax.ShapeDtypeStruct((count, 1), f32),
            jax.ShapeDtypeStruct((width, ff_width), f32),
            jax.ShapeDtypeStruct((width, ff_width), f32),
            jax.ShapeDtypeStruct((ff_width, width), f32),
        ],
        cost_estimate=pl.CostEstimate(flops=1000, bytes_accessed=1000, transcendentals=0),
        name="experts",
    )(rows, blend, gates, gate_local, up_local, down_local)


def build_kernel(slots_ref, *refs):
    out_ref = refs[-1]
    plane, lines, capacity, width = out_ref.shape
    for line in range(lines):
        slots = slots_ref[line]
        places = lax.broadcasted_iota(jnp.int32, (plane, capacity, slots.shape[1]), 1)
        picks = jnp.where(slots[:, None, :] == places, 1.0, 0.0)
        rows = jnp.dot(
            picks.reshape(plane * capacity, slots.shape[1]).astype(jnp.bfloat16),
            refs[line][...],
            preferred_element_type=jnp.float32,
        )
        out_ref[:, line] = rows.reshape(plane, capacity, width).astype(jnp.bfloat16)


def build_rows(slots, blocks, capacity):
    lines, plane, unused = slots.shape
    width = blocks[0].shape[1]
    return pl.pallas_call(
        build_kernel,
        out_shape=jax.ShapeDtypeStruct((plane, lines, capacity, width), blocks[0].dtype),
        cost_estimate=pl.CostEstimate(flops=1000, bytes_accessed=1000, transcendentals=0),
        name="build_rows",
    )(slots, *blocks)


def swap_halves(value):
    width = value.shape[1]
    half = HD // 2
    lanes = lax.broadcasted_iota(jnp.int32, value.shape, 1)
    return jnp.where(
        lanes % HD < half, pltpu.roll(value, width - half, 1), pltpu.roll(value, half, 1)
    )


def head_of(value, head):
    return value[:, head * HD : (head + 1) * HD]


def head_product(left, right, left_axis, right_axis):
    return lax.dot_general(
        left,
        right,
        (((left_axis,), (right_axis,)), ((), ())),
        preferred_element_type=jnp.float32,
    )


def probabilities(query, key, visible):
    scores = jnp.where(visible, attn_scale * head_product(query, key, 1, 1), -1e30)
    shifted = jnp.exp(scores - jnp.max(scores, axis=1, keepdims=True))
    return shifted / jnp.sum(shifted, axis=1, keepdims=True)


def attend_kernel(
    query_ref,
    key_ref,
    value_ref,
    cos_ref,
    sin_ref,
    own_ref,
    other_ref,
    query_out,
    key_out,
    value_out,
    mixture_out,
):
    bf16 = jnp.bfloat16
    key_width = key_ref.shape[1]
    queries = query_ref[...]
    keys = key_ref[...]
    cos_table = cos_ref[...]
    sin_table = sin_ref[...]
    queries = (queries * cos_table + swap_halves(queries) * sin_table).astype(bf16)
    keys = (
        keys * cos_table[:, :key_width] + swap_halves(keys) * sin_table[:, :key_width]
    ).astype(bf16)
    values = value_ref[...].astype(bf16)
    query_out[...] = queries
    key_out[...] = keys
    value_out[...] = values
    visible = other_ref[0] <= own_ref[...]
    mixed = []
    for head in range(queries.shape[1] // HD):
        shared = head // (H // KVH)
        probs = probabilities(head_of(queries, head), head_of(keys, shared), visible)
        mixed.append(head_product(probs.astype(bf16), head_of(values, shared), 1, 0))
    mixture_out[...] = jnp.concatenate(mixed, axis=1).astype(bf16)


def attend_back_kernel(
    query_ref,
    key_ref,
    value_ref,
    mixture_ref,
    cos_ref,
    sin_ref,
    own_ref,
    other_ref,
    query_out,
    key_out,
    value_out,
):
    bf16 = jnp.bfloat16
    key_width = key_ref.shape[1]
    queries = query_ref[...]
    keys = key_ref[...]
    values = value_ref[...]
    grad_mixture = mixture_ref[...]
    cos_table = cos_ref[...]
    sin_table = sin_ref[...]
    visible = other_ref[0] <= own_ref[...]
    grad_queries = []
    grad_keys = [0.0] * (key_width // HD)
    grad_values = [0.0] * (key_width // HD)
    for head in range(queries.shape[1] // HD):
        shared = head // (H // KVH)
        query, key = head_of(queries, head), head_of(keys, shared)
        grad_mix = head_of(grad_mixture, head)
        probs = probabilities(query, key, visible)
        grad_probs = head_product(grad_mix, head_of(values, shared), 1, 1)
        inner = jnp.sum(probs * grad_probs, axis=1, keepdims=True)
        grad_scores = (probs * (grad_probs - inner)).astype(bf16)
        grad_values[shared] += head_product(probs.astype(bf16), grad_mix, 0, 0)
        grad_keys[shared] += head_product(grad_scores, query, 0, 0)
        grad_queries.append(head_product(grad_scores, key, 1, 0))
    grad_query = attn_scale * jnp.concatenate(grad_queries, axis=1)
    grad_key = attn_scale * jnp.concatenate(grad_keys, axis=1)
    query_out[...] = (grad_query * cos_table - swap_halves(grad_query) * sin_table).astype(bf16)
    key_out[...] = (
        grad_key * cos_table[:, :key_width] - swap_halves(grad_key) * sin_table[:, :key_width]
    ).astype(bf16)
    value_out[...] = jnp.concatenate(grad_values, axis=1).astype(bf16)


def attention_specs(seq_len):
    query_block = 2 * (H // KVH) * HD
    key_block = 2 * HD
    wide = pl.BlockSpec((seq_len, query_block), lambda m, i: (m, i))
    thin = pl.BlockSpec((seq_len, key_block), lambda m, i: (m, i))
    table = pl.BlockSpec((seq_len, query_block), lambda m, i: (0, 0))
    own = pl.BlockSpec((seq_len, 1), lambda m, i: (m, 0))
    other = pl.BlockSpec((1, 1, seq_len), lambda m, i: (m, 0, 0))
    return wide, thin, table, own, other


def wide_tables(seq_len):
    cos_table, sin_table = rotary_tables(seq_len, HD)
    cos_table, sin_table = cos_table[:, 0], sin_table[:, 0]
    count = 2 * (H // KVH)
    return (
        jnp.tile(jnp.concatenate([cos_table, cos_table], axis=1), (1, count)),
        jnp.tile(jnp.concatenate([-sin_table, sin_table], axis=1), (1, count)),
    )


def run_attention(projected, tables, block_ids):
    micro_count, seq_len = block_ids.shape
    wide, thin, table, own, other = attention_specs(seq_len)
    rows = projected.shape[0]
    bf16 = jnp.bfloat16
    first_key = H * HD // (2 * HD)
    first_value = first_key + KVH // 2
    return pl.pallas_call(
        attend_kernel,
        grid=(micro_count, KVH // 2),
        in_specs=[
            wide,
            pl.BlockSpec((seq_len, 2 * HD), lambda m, i: (m, first_key + i)),
            pl.BlockSpec((seq_len, 2 * HD), lambda m, i: (m, first_value + i)),
            table,
            table,
            own,
            other,
        ],
        out_specs=[wide, thin, thin, wide],
        out_shape=[
            jax.ShapeDtypeStruct((rows, H * HD), bf16),
            jax.ShapeDtypeStruct((rows, KVH * HD), bf16),
            jax.ShapeDtypeStruct((rows, KVH * HD), bf16),
            jax.ShapeDtypeStruct((rows, H * HD), bf16),
        ],
        cost_estimate=pl.CostEstimate(flops=1000, bytes_accessed=1000, transcendentals=0),
        name="attention",
    )(
        projected,
        projected,
        projected,
        *tables,
        block_ids.reshape(-1, 1),
        block_ids.reshape(micro_count, 1, seq_len),
    )


def run_attention_back(queries, keys, values, grad_mixture, tables, block_ids, micro):
    micro_count, seq_len = block_ids.shape
    wide, thin, table, own, other = attention_specs(seq_len)
    bf16 = jnp.bfloat16

    def at(spec, index):
        return pl.BlockSpec(spec.block_shape, index)

    return pl.pallas_call(
        attend_back_kernel,
        grid=(1, KVH // 2),
        in_specs=[
            at(wide, lambda m, i: (micro, i)),
            at(thin, lambda m, i: (micro, i)),
            at(thin, lambda m, i: (micro, i)),
            wide,
            table,
            table,
            at(own, lambda m, i: (micro, 0)),
            at(other, lambda m, i: (micro, 0, 0)),
        ],
        out_specs=[wide, thin, thin],
        out_shape=[
            jax.ShapeDtypeStruct((seq_len, H * HD), bf16),
            jax.ShapeDtypeStruct((seq_len, KVH * HD), bf16),
            jax.ShapeDtypeStruct((seq_len, KVH * HD), bf16),
        ],
        cost_estimate=pl.CostEstimate(flops=1000, bytes_accessed=1000, transcendentals=0),
        name="attention_back",
    )(
        queries,
        keys,
        values,
        grad_mixture,
        *tables,
        block_ids.reshape(-1, 1),
        block_ids.reshape(micro_count, 1, seq_len),
    )


def weights_kernel(*refs, counts):
    left_ref, out_ref = refs[0], refs[-1]
    rights = refs[1 : 1 + sum(counts)]
    tokens = left_ref.shape[0] // len(counts)
    start = 0
    for i in range(counts[0]):
        width = rights[i].shape[1]
        product = 0.0
        for m in range(len(counts)):
            product = product + head_product(
                left_ref[m * tokens : (m + 1) * tokens], rights[m * counts[0] + i][...], 0, 0
            )
        out_ref[:, start : start + width] = product.astype(out_ref.dtype)
        start += width
    if len(refs) > 2 + sum(counts):
        out_ref[:, start:] = refs[-2][...].astype(out_ref.dtype)


def run_weights(left, groups, extra, dtype):
    tokens, height = left.shape
    block = 256 if height % 256 == 0 else height
    rights = [right for group in groups for right in group]
    width = sum(right.shape[1] for right in groups[0])
    in_specs = [pl.BlockSpec((tokens, block), lambda i: (0, i))] + [
        pl.BlockSpec(right.shape, lambda i: (0, 0)) for right in rights
    ]
    operands = [left, *rights]
    if extra is not None:
        in_specs.append(pl.BlockSpec((block, extra.shape[1]), lambda i: (i, 0)))
        operands.append(extra)
        width += extra.shape[1]
    return pl.pallas_call(
        functools.partial(weights_kernel, counts=tuple(len(group) for group in groups)),
        grid=(height // block,),
        in_specs=in_specs,
        out_specs=pl.BlockSpec((block, width), lambda i: (i, 0)),
        out_shape=jax.ShapeDtypeStruct((height, width), dtype),
        cost_estimate=pl.CostEstimate(flops=1000, bytes_accessed=1000, transcendentals=0),
        name="weights",
    )(*operands)


def sums_kernel(slots_ref, rows_ref, *out_refs):
    plane, lines, capacity, width = rows_ref.shape
    for line in range(lines):
        slots = slots_ref[line]
        places = lax.broadcasted_iota(jnp.int32, (plane, capacity, slots.shape[1]), 1)
        picks = jnp.where(slots[:, None, :] == places, 1.0, 0.0)
        rows = rows_ref[:, line].astype(jnp.float32).reshape(plane * capacity, width)
        out_refs[line][...] = head_product(
            picks.reshape(plane * capacity, slots.shape[1]).astype(jnp.bfloat16),
            rows.astype(jnp.bfloat16),
            0,
            0,
        ).astype(jnp.bfloat16)


def sum_rows(slots, rows):
    lines, unused, tokens = slots.shape
    return pl.pallas_call(
        sums_kernel,
        out_shape=[jax.ShapeDtypeStruct((tokens, rows.shape[3]), rows.dtype)] * lines,
        cost_estimate=pl.CostEstimate(flops=1000, bytes_accessed=1000, transcendentals=0),
        name="sum_rows",
    )(slots, rows)


def norm_grads(grad_normed, source, recip, gain):
    scaled = grad_normed * gain
    centre = jnp.mean(scaled * source, axis=1, keepdims=True)
    grad_source = recip * scaled - source * (recip * recip * recip) * centre
    return grad_source, jnp.sum(grad_normed * source * recip, axis=0, keepdims=True)


def middle_kernel(*refs):
    parts = refs[:LINES]
    logits_ref, router_ref, residual_ref, recip_ref, gain_ref, cotan_ref, proj_ref = refs[LINES:-4]
    residual_out, attn_out, mixture_out, gain_out = refs[-4:]
    bf16 = jnp.bfloat16
    grad_mid = head_product(logits_ref[...], router_ref[...], 0, 1)
    for part in parts:
        grad_mid = grad_mid + part[...].astype(jnp.float32)
    grad_source, grad_gain = norm_grads(
        grad_mid, residual_ref[...], recip_ref[...], gain_ref[...]
    )
    grad_residual = cotan_ref[...] + grad_source
    grad_attn = (res_scale * grad_residual).astype(bf16)
    residual_out[...] = grad_residual
    attn_out[...] = grad_attn
    mixture_out[...] = head_product(grad_attn, proj_ref[...], 1, 1).astype(bf16)
    gain_out[...] = grad_gain


def run_middle(parts, grad_logits, router, residual, recip, gain, cotangent, out_proj):
    tokens, width = residual.shape
    shape = jax.ShapeDtypeStruct
    return pl.pallas_call(
        middle_kernel,
        out_shape=[
            shape((tokens, width), jnp.float32),
            shape((tokens, width), jnp.bfloat16),
            shape((tokens, out_proj.shape[0]), jnp.bfloat16),
            shape((1, width), jnp.float32),
        ],
        cost_estimate=pl.CostEstimate(flops=1000, bytes_accessed=1000, transcendentals=0),
        name="middle_back",
    )(*parts, grad_logits, router, residual, recip, gain[None], cotangent, out_proj)


def first_kernel(
    query_ref, key_ref, value_ref, proj_ref, tokens_ref, recip_ref, gain_ref, residual_ref,
    out_ref, gain_out,
):
    start = 0
    grad_normed = 0.0
    for ref in (query_ref, key_ref, value_ref):
        stop = start + ref.shape[1]
        grad_normed = grad_normed + head_product(ref[...], proj_ref[:, start:stop], 1, 1)
        start = stop
    grad_source, grad_gain = norm_grads(
        grad_normed, tokens_ref[...], recip_ref[...], gain_ref[...]
    )
    out_ref[...] = residual_ref[...] + grad_source
    gain_out[...] = grad_gain


def run_first(queries, keys, values, qkv_proj, tokens, recip, gain, grad_residual):
    shape = jax.ShapeDtypeStruct
    return pl.pallas_call(
        first_kernel,
        out_shape=[shape(tokens.shape, jnp.float32), shape((1, tokens.shape[1]), jnp.float32)],
        cost_estimate=pl.CostEstimate(flops=1000, bytes_accessed=1000, transcendentals=0),
        name="first_back",
    )(queries, keys, values, qkv_proj, tokens, recip, gain[None], grad_residual)


def on_device(
    hidden,
    cotangent,
    block_ids,
    routes,
    pair_rank,
    norm1_gain,
    norm2_gain,
    w_query,
    w_key,
    w_value,
    w_out,
    w_router,
    w_gate,
    w_up,
    w_down,
):
    micro_count, seq_len = block_ids.shape
    model_width = hidden.shape[1]
    top_count = routes.shape[1]
    devices = lax.axis_size("dp")
    experts = w_router.shape[1]
    plane = devices // LINES
    capacity = (9 * seq_len * top_count + 8 * experts - 1) // (8 * experts)
    query_width = w_query.shape[1]
    kv_width = w_key.shape[1]
    qkv_width = query_width + 2 * kv_width
    tables = wide_tables(seq_len)
    gate_local = w_gate[0]
    up_local = w_up[0]
    down_local = w_down[0]
    bf16 = jnp.bfloat16
    f32 = jnp.float32
    here = lax.axis_index("dp") // plane
    plane_groups = [[line * plane + i for i in range(plane)] for line in range(LINES)]

    def line_shift(step):
        return [
            (i, ((i // plane + step) % LINES) * plane + i % plane) for i in range(devices)
        ]

    def spread(block):
        return [block] + [
            lax.ppermute(block, "dp", line_shift(step)) for step in range(1, LINES)
        ]

    def give_back(blocks):
        return [blocks[0]] + [
            lax.ppermute(blocks[step], "dp", line_shift(-step)) for step in range(1, LINES)
        ]

    def hold(value, *after):
        return lax.optimization_barrier((value, after))[0]

    def reduce_rows(value, first, early, late):
        if plane != 8:
            return lax.psum_scatter(
                value.astype(bf16), "dp", scatter_dimension=0, tiled=True
            ).astype(f32)
        index = lax.axis_index("dp")
        rows = value.shape[0] // devices
        half = value.shape[1] // 256 * 128

        def fold(block, axis, bit):
            side = (index // bit) % 2
            kept = lax.dynamic_index_in_dim(block, side, axis, keepdims=False)
            sent = lax.dynamic_index_in_dim(block, 1 - side, axis, keepdims=False)
            other = lax.ppermute(
                sent.astype(bf16), "dp", [(i, i ^ bit) for i in range(devices)]
            )
            return kept + other.astype(f32)

        value = hold(value, first)
        block = hold(fold(value.reshape(LINES, 2, 2, 2, rows, value.shape[1]), 3, 1), early)
        left, right = block[..., :half], block[..., half:]
        left, right = fold(left, 1, 4), fold(right, 2, 2)
        left, right = hold((left, right), late)
        left, right = fold(left, 1, 2), fold(right, 1, 4)
        block = jnp.concatenate([left, right], axis=2)
        total = lax.dynamic_index_in_dim(block, here, 0, keepdims=False)
        for step in range(1, LINES):
            sent = lax.dynamic_index_in_dim(block, (here + step) % LINES, 0, keepdims=False)
            total = total + lax.ppermute(sent.astype(bf16), "dp", line_shift(step)).astype(f32)
        return total


    def exchange(block):
        return lax.all_to_all(
            block, "dp", split_axis=0, concat_axis=0, tiled=True, axis_index_groups=plane_groups
        )

    small = jnp.concatenate([norm1_gain[:, None], norm2_gain[:, None], w_router], axis=1)
    pad = -small.shape[1] % 128
    shared = lax.all_gather(
        jnp.concatenate(
            [w_query, w_key, w_value, w_out, jnp.pad(small, ((0, 0), (0, pad)))], axis=1
        ),
        "dp",
        axis=0,
        tiled=True,
    )
    qkv_proj = shared[:, :qkv_width]
    first_small = qkv_width + model_width
    out_proj = shared[:, qkv_width:first_small]
    gain_first = shared[:, first_small].astype(f32)
    gain_second = shared[:, first_small + 1].astype(f32)
    router = shared[:, first_small + 2 : first_small + 2 + experts]

    labels = jnp.arange(experts, dtype=jnp.int32)
    route_seq = routes.reshape(micro_count, seq_len, top_count)
    rank_seq = pair_rank.reshape(micro_count, seq_len, top_count)
    named = route_seq[:, None, :, :] == labels[None, :, None, None]
    routed = jnp.any(named, axis=3)
    rank_of = jnp.where(
        routed, jnp.sum(jnp.where(named, rank_seq[:, None], 0), axis=3), seq_len * top_count
    )
    ahead = jnp.sum((rank_of[:, :, :, None] < rank_of[:, :, None, :]).astype(jnp.int32), axis=2)
    slot_of = jnp.where(routed, ahead, -1)
    slot_blocks = jnp.stack(spread(slot_of))
    slots_here = lax.dynamic_slice_in_dim(slot_blocks, here * plane, plane, axis=2)
    places = jnp.arange(capacity, dtype=jnp.int32)
    picks = [
        (slots_here[:, micro, :, None, :] == places[None, None, :, None]).astype(bf16)
        for micro in range(micro_count)
    ]

    cotan_seq = cotangent.reshape(micro_count, seq_len, model_width)
    hidden_seq = hidden.reshape(micro_count, seq_len, model_width)

    def build(micro, blocks):
        if capacity % 8 == 0:
            rows = build_rows(slots_here[:, micro], blocks, capacity)
        else:
            rows = jnp.einsum(
                "ject,jtd->ejcd", picks[micro], jnp.stack(blocks), preferred_element_type=f32
            ).astype(bf16)
        return rows.reshape(plane, LINES * capacity, model_width)

    def sums_of(micro, arrived):
        arrived = arrived.reshape(plane, LINES, capacity, model_width)
        if capacity % 8 == 0:
            return give_back(sum_rows(slots_here[:, micro], arrived))
        sums = jnp.einsum(
            "ject,ejcd->jtd", picks[micro], arrived, preferred_element_type=f32
        ).astype(bf16)
        return give_back([sums[step] for step in range(LINES)])

    def total_of(parts):
        total = parts[0].astype(f32)
        for part in parts[1:]:
            total = total + part.astype(f32)
        return total

    def attend(tokens_in):
        recip_first = lax.rsqrt(jnp.mean(tokens_in * tokens_in, axis=1, keepdims=True) + norm_eps)
        normed_in = (tokens_in * recip_first * gain_first).astype(bf16)
        projected = jnp.dot(normed_in, qkv_proj, preferred_element_type=f32)
        queries, keys, values, mixture = run_attention(projected, tables, block_ids)
        return recip_first, normed_in, queries, keys, values, mixture

    def after_attention(mixture, tokens_in):
        attn_out = jnp.dot(mixture, out_proj, preferred_element_type=f32)
        residual = tokens_in + res_scale * attn_out
        recip_second = lax.rsqrt(jnp.mean(residual * residual, axis=1, keepdims=True) + norm_eps)
        normed_mid = (residual * recip_second * gain_second).astype(bf16)
        return residual, recip_second, normed_mid

    def gates_of(micro, blocks):
        logits = jnp.einsum("de,jtd->jet", router, jnp.stack(blocks), preferred_element_type=f32)
        gates = masked_gates(logits, slot_blocks[:, micro] >= 0)
        gates_here = lax.dynamic_slice_in_dim(gates, here * plane, plane, axis=1)
        slot_gates = jnp.sum(
            jnp.where(picks[micro] > 0, gates_here[:, :, None, :], 0.0), axis=3
        ).transpose(1, 0, 2)
        return gates[0], slot_gates.reshape(plane, LINES * capacity)

    def run_expert(mid, blend, gate_rows):
        grads, scaled, pair_grads, *weights = run_experts(
            mid.reshape(-1, model_width),
            blend.reshape(-1, model_width),
            gate_rows.reshape(-1, 1),
            gate_local,
            up_local,
            down_local,
        )
        return (
            grads.reshape(mid.shape),
            scaled.reshape(mid.shape),
            pair_grads.reshape(mid.shape[:2]),
            weights,
        )

    def pairs_home(pair_back):
        token_grads = [
            jnp.sum(
                jnp.where(
                    picks[m] > 0,
                    pair_back[:, m]
                    .reshape(plane, LINES, capacity)
                    .transpose(1, 0, 2)[:, :, :, None],
                    0.0,
                ),
                axis=2,
            )
            for m in range(micro_count)
        ]
        both = jnp.stack(token_grads, axis=1)
        return give_back([both[step] for step in range(LINES)])

    def attend_back(micro, parts, pair_blocks, gates, before, then):
        residual, recip_second, unused = after[micro]
        pair_grads = jnp.zeros((experts, seq_len), f32)
        for step in range(LINES):
            pair_grads = lax.dynamic_update_slice_in_dim(
                pair_grads, pair_blocks[step], ((here + step) % LINES) * plane, axis=0
            )
        grad_logits = (
            gates * (pair_grads - jnp.sum(gates * pair_grads, axis=0, keepdims=True))
        ).astype(bf16)
        grad_residual, grad_attn, grad_mixture, gain_second_w = run_middle(
            parts,
            grad_logits,
            router,
            residual,
            recip_second,
            gain_second,
            cotan_seq[micro],
            proj_copy[1],
        )
        grads = run_attention_back(
            queries, keys, values, hold(grad_mixture, before(grad_attn)), tables, block_ids, micro
        )
        grad_tokens, gain_first_w = run_first(
            *grads,
            proj_copy[0],
            hidden_seq[micro],
            rows_of(recip_first, micro),
            gain_first,
            grad_residual,
        )
        grads, gain_first_w = hold((grads, gain_first_w), then)
        return (
            grad_tokens,
            grad_attn,
            grads,
            grad_logits,
            gain_second_w,
            gain_first_w,
        )

    blend_rows = [(res_scale * cotan_seq[m]).astype(bf16) for m in range(2)]
    blend_blocks = [
        spread(hold(blend_rows[0], slot_blocks)),
        spread(hold(blend_rows[1], slot_blocks)),
    ]
    blend0 = build(0, blend_blocks[0])
    moved_blend0 = exchange(blend0)
    recip_first, normed_in, queries, keys, values, mixture = attend(hold(hidden, blend0, blend_blocks[1]))

    def rows_of(value, micro):
        return value[micro * seq_len : (micro + 1) * seq_len]

    blend1 = build(1, hold(blend_blocks[1], mixture))
    moved_blend1 = exchange(hold(blend1, moved_blend0))
    after = [after_attention(rows_of(mixture, m), hidden_seq[m]) for m in range(2)]
    blocks0 = spread(after[0][2])
    blocks1 = spread(after[1][2])
    moved_mid0 = exchange(hold(build(0, blocks0), moved_blend1))
    gates0, slot_gates0 = gates_of(0, blocks0)
    gates1, slot_gates1 = gates_of(1, blocks1)
    mid1 = build(1, blocks1)
    gate_rows = exchange(
        hold(jnp.stack([slot_gates0, slot_gates1], axis=1), moved_mid0, mid1)
    )
    moved_mid1 = exchange(hold(mid1, gate_rows))
    grads0, scaled0, pairs0, weights0 = run_expert(
        hold(moved_mid0, mid1), moved_blend0, gate_rows[:, 0]
    )
    moved_grads0 = exchange(hold(grads0, moved_mid1))
    proj_copy = hold((qkv_proj, out_proj), moved_mid0)
    grads1, scaled1, pairs1, weights1 = run_expert(
        hold(moved_mid1, proj_copy), moved_blend1, gate_rows[:, 1]
    )
    pair_back = exchange(hold(jnp.stack([pairs0, pairs1], axis=1), moved_grads0))
    moved_grads1 = exchange(hold(grads1, pair_back))
    pair_blocks = pairs_home(pair_back)
    back0 = sums_of(0, moved_grads0)
    expert_w = [a + b for a, b in zip(weights0, weights1, strict=True)]
    moved_scaled0 = exchange(hold(scaled0, moved_grads1, back0, pair_blocks, expert_w))
    grad_gate_w, grad_up_w, grad_down_w = expert_w
    back1 = sums_of(1, moved_grads1)
    result0 = attend_back(
        0,
        hold(back0, back1[0]),
        [block[0] for block in pair_blocks],
        gates0,
        lambda grad_attn: (moved_grads1, back1[0]),
        (),
    )
    moved_scaled1 = exchange(hold(scaled1, moved_scaled0, back1, result0))
    blend_back0 = sums_of(0, hold(moved_scaled0, result0))

    def out_grads(grad_attn):
        return run_weights(
            mixture, [[result0[1]], [grad_attn]], None, bf16
        )

    result1 = attend_back(
        1,
        hold(back1, result0, blend_back0[0]),
        [block[1] for block in pair_blocks],
        gates1,
        lambda grad_attn: (moved_scaled0, blend_back0[0], out_grads(grad_attn)),
        blend_back0,
    )
    blend_back1 = sums_of(1, hold(moved_scaled1, result1))
    outputs = [
        after[0][0] + res_scale * total_of(blend_back0),
        after[1][0] + res_scale * total_of(blend_back1),
    ]
    token_grads_out = [result0[0], result1[0]]
    out_w = out_grads(result1[1])
    router_w = jnp.einsum(
        "td,et->de",
        jnp.concatenate([after[0][2], after[1][2]], axis=0),
        jnp.concatenate([result0[3], result1[3]], axis=1),
        preferred_element_type=f32,
    )
    gain_second_w = (result0[4] + result1[4])[0]
    gain_first_w = (result0[5] + result1[5])[0]

    small_w = jnp.concatenate([gain_first_w[:, None], gain_second_w[:, None], router_w], axis=1)
    small_w = jnp.pad(small_w, ((0, 0), (0, -small_w.shape[1] % 128)))
    out_sum = lax.psum_scatter(out_w, "dp", scatter_dimension=0, tiled=True)
    qkv_sum = reduce_rows(
        run_weights(normed_in, [result0[2], result1[2]], small_w, f32),
        moved_scaled1,
        blend_back1[0],
        blend_back1,
    )
    out_sum = hold(out_sum, qkv_sum).astype(f32)
    return (
        jnp.concatenate(outputs, axis=0),
        jnp.concatenate(token_grads_out, axis=0),
        qkv_sum[:, qkv_width],
        qkv_sum[:, qkv_width + 1],
        qkv_sum[:, :query_width],
        qkv_sum[:, query_width : query_width + kv_width],
        qkv_sum[:, query_width + kv_width : qkv_width],
        out_sum,
        qkv_sum[:, qkv_width + 2 : qkv_width + 2 + experts],
        grad_gate_w[None],
        grad_up_w[None],
        grad_down_w[None],
    )


def solution(mesh):
    return jax.shard_map(
        on_device,
        mesh=mesh,
        in_specs=(
            P("dp", None),
            P("dp", None),
            P("dp", None),
            P("dp", None),
            P("dp", None),
            P("dp"),
            P("dp"),
            P("dp", None),
            P("dp", None),
            P("dp", None),
            P("dp", None),
            P("dp", None),
            P("dp", None, None),
            P("dp", None, None),
            P("dp", None, None),
        ),
        out_specs=(
            P("dp", None),
            P("dp", None),
            P("dp"),
            P("dp"),
            P("dp", None),
            P("dp", None),
            P("dp", None),
            P("dp", None),
            P("dp", None),
            P("dp", None, None),
            P("dp", None, None),
            P("dp", None, None),
        ),
        check_vma=False,
    )
```
